32 devices in a mesh: dev: 32 (over z, y, x, core).
Axes of the slice: x: 2, y: 2, z: 4, core: 2. Of those that a mesh axis runs over, the one named last changes fastest.
Arguments:
- images: bfloat16 [128, 196, 768], P('dev'), may hold values from -6 to 6
- pair_matrix: int32 [128, 14], P('dev'), may hold values from 0 to 1, as said below
- caption_grads: bfloat16 [448, 196, 768], P('dev'), may hold values from -3 to 3
- qkv_weight: float32 [768, 2304], P('dev'), may hold values from -0.21875 to 0.21875
- out_weight: float32 [768, 768], P('dev'), may hold values from -0.875 to 0.875
- up_weight: float32 [768, 3072], P('dev'), may hold values from -0.21875 to 0.21875
- down_weight: float32 [3072, 768], P('dev'), may hold values from -0.109375 to 0.109375
- vector_rows: float32 [12, 768], P(None, 'dev'), may hold values from -1.5 to 1.75, as said below
- first_qkv: float32 [768, 2304], P('dev'), may hold values from -0.00024414062 to 0.00024414062
- first_out: float32 [768, 768], P('dev'), may hold values from -0.00024414062 to 0.00024414062
- first_up: float32 [768, 3072], P('dev'), may hold values from -0.00024414062 to 0.00024414062
- first_down: float32 [3072, 768], P('dev'), may hold values from -0.00024414062 to 0.00024414062
- first_vectors: float32 [12, 768], P(None, 'dev'), may hold values from -0.0009765625 to 0.0009765625
- second_qkv: float32 [768, 2304], P('dev'), may hold values from 1.4110135e-10 to 5.644054e-10
- second_out: float32 [768, 768], P('dev'), may hold values from 1.4110135e-10 to 5.644054e-10
- second_up: float32 [768, 3072], P('dev'), may hold values from 1.4110135e-10 to 5.644054e-10
- second_down: float32 [3072, 768], P('dev'), may hold values from 1.4110135e-10 to 5.644054e-10
- second_vectors: float32 [12, 768], P(None, 'dev'), may hold values from 2.2576216e-09 to 9.030487e-09
Outputs:
- output: float32 [128, 196, 768], P('dev')
- input_grads: float32 [128, 196, 768], P('dev')
- grad_norm: float32 [], replicated
- grad_qkv: float32 [768, 2304], P('dev')
- new_qkv: float32 [768, 2304], P('dev')
- first_qkv_new: float32 [768, 2304], P('dev')
- second_qkv_new: float32 [768, 2304], P('dev')
- grad_out: float32 [768, 768], P('dev')
- new_out: float32 [768, 768], P('dev')
- first_out_new: float32 [768, 768], P('dev')
- second_out_new: float32 [768, 768], P('dev')
- grad_up: float32 [768, 3072], P('dev')
- new_up: float32 [768, 3072], P('dev')
- first_up_new: float32 [768, 3072], P('dev')
- second_up_new: float32 [768, 3072], P('dev')
- grad_down: float32 [3072, 768], P('dev')
- new_down: float32 [3072, 768], P('dev')
- first_down_new: float32 [3072, 768], P('dev')
- second_down_new: float32 [3072, 768], P('dev')
- grad_vectors: float32 [12, 768], P(None, 'dev')
- new_vectors: float32 [12, 768], P(None, 'dev')
- first_vectors_new: float32 [12, 768], P(None, 'dev')
- second_vectors_new: float32 [12, 768], P(None, 'dev')
The draws below stay inside these ranges and needn't reach their ends.
Inputs may be any that keep to these rules, and one draw needn't show every extreme that they name: `pair_matrix`: each image is paired with 2 to 5 captions of its own device's block; a caption may be paired with several images or none. `vector_rows`: rows 0 and 5 are positive gains; the other rows are biases.
All inputs are finite; a program needn't handle non-finite values.
Results may differ from the reference program's by a relative error of at most 0.012.
The reference program's roundings to bfloat16 on the way count: a program that leaves them out, or rounds other values in their place, can miss the bound.
Values may be sent and summed in bfloat16 or wider, within the bound.
A program may use at most 192 MiB of HBM per device.

```python
import math
import jax
import jax.numpy as jnp
from jax import lax

D = 768
HEADS = 12
FF = 3072
HD = 64
S = 196
STEP = 10
IMG_DEV = 4
IMAGES = 128
CAP_DEV = 14
CAPTIONS = 448
VROWS = 12
NPARAM = 7087104
N_DEV = 32


def draw_pair_matrix(key, part):
    count_key, order_key = jax.random.split(key)
    counts = jax.random.randint(count_key, (IMAGES, 1), 2, 6)
    row_keys = jax.random.split(order_key, IMAGES)

    def row_order(row_key):
        return jax.random.permutation(row_key, CAP_DEV)
    orders = jax.vmap(row_order)(row_keys)
    return (orders < counts).astype(jnp.int32)


def draw_vector_rows(key, part):
    noise_key, gain_key = jax.random.split(key)
    rows_index = jnp.arange(VROWS)[:, None]
    column_index = jnp.arange(D).astype(jnp.float32)[None, :]
    noise_draw = jnp.clip(jax.random.normal(noise_key, (VROWS, D), jnp.float32), -3.0, 3.0)
    jitter = jax.random.uniform(gain_key, (VROWS, D), jnp.float32, -1.0, 1.0)
    gain_rows = (0.5 + column_index / D) * (1.0 + 0.15 * jitter)
    scales = jnp.where(rows_index >= 8, 0.5, jnp.where((rows_index == 1) | (rows_index == 6), 0.2, 0.3))
    is_gain = (rows_index == 0) | (rows_index == 5)
    return jnp.where(is_gain, gain_rows, scales * noise_draw).astype(jnp.float32)


def block_levels(key, shape, shards, smallest, top_value):
    level = 1.0
    for dim, blocks in shards:
        draws = jax.random.uniform(jax.random.fold_in(jax.random.fold_in(key, 6), dim), (blocks,), jnp.float32, smallest / len(shards), top_value / len(shards))
        level = level * jnp.repeat(jnp.exp(draws), shape[dim] // blocks).reshape((-1,) + (1,) * (len(shape) - 1 - dim))
    return level


def centred(own_key, extent, scale, reach, cuts=(), held_as=jnp.bfloat16):
    loudness = block_levels(own_key, extent, cuts, -0.22, 0.18) if cuts else 1.0
    values = jax.random.normal(own_key, extent, jnp.float32) * scale * loudness
    return jnp.minimum(jnp.maximum(values, -reach), reach).astype(held_as)


def setup_inputs(seed: int = 0) -> dict:
    arg_keys = jax.random.split(jax.random.key(seed), 19)
    return {
        "images": centred(arg_keys[0], (IMAGES, S, D), 1.0, 6.0, ((0, 32),)),
        "pair_matrix": draw_pair_matrix(jax.random.fold_in(arg_keys[18], 71), 0),
        "caption_grads": centred(arg_keys[2], (CAPTIONS, S, D), 0.5, 3.0, ((0, 32),)),
        "qkv_weight": centred(arg_keys[3], (D, 3 * D), D ** -0.5, 0.21875, ((0, 32),), jnp.float32),
        "out_weight": centred(arg_keys[4], (D, D), (D // 16) ** -0.5, 0.875, ((0, 32),), jnp.float32),
        "up_weight": centred(arg_keys[5], (D, FF), D ** -0.5, 0.21875, ((0, 32),), jnp.float32),
        "down_weight": centred(arg_keys[6], (FF, D), FF ** -0.5, 0.109375, ((0, 32),), jnp.float32),
        "vector_rows": draw_vector_rows(jax.random.fold_in(arg_keys[18], 71), 0),
        "first_qkv": centred(arg_keys[8], (D, 3 * D), (0.111 * NPARAM ** -0.5), 0.00024414062, ((0, 32),), jnp.float32),
        "first_out": centred(arg_keys[9], (D, D), (0.111 * NPARAM ** -0.5), 0.00024414062, ((0, 32),), jnp.float32),
        "first_up": centred(arg_keys[10], (D, FF), (0.111 * NPARAM ** -0.5), 0.00024414062, ((0, 32),), jnp.float32),
        "first_down": centred(arg_keys[11], (FF, D), (0.111 * NPARAM ** -0.5), 0.00024414062, ((0, 32),), jnp.float32),
        "first_vectors": centred(arg_keys[12], (VROWS, D), (0.444 * NPARAM ** -0.5), 0.0009765625, ((1, 32),), jnp.float32),
        "second_qkv": jnp.clip(jnp.exp(math.log(5.644054112963204e-10) - 1.3862944 * jax.random.uniform(arg_keys[13], (D, 3 * D), jnp.float32) ** block_levels(arg_keys[13], (D, 3 * D), ((0, 32),), -0.2, 0.2)), 1.411013528240801e-10, 5.644054112963204e-10),
        "second_out": jnp.clip(jnp.exp(math.log(5.644054112963204e-10) - 1.3862944 * jax.random.uniform(arg_keys[14], (D, D), jnp.float32) ** block_levels(arg_keys[14], (D, D), ((0, 32),), -0.2, 0.2)), 1.411013528240801e-10, 5.644054112963204e-10),
        "second_up": jnp.clip(jnp.exp(math.log(5.644054112963204e-10) - 1.3862944 * jax.random.uniform(arg_keys[15], (D, FF), jnp.float32) ** block_levels(arg_keys[15], (D, FF), ((0, 32),), -0.2, 0.2)), 1.411013528240801e-10, 5.644054112963204e-10),
        "second_down": jnp.clip(jnp.exp(math.log(5.644054112963204e-10) - 1.3862944 * jax.random.uniform(arg_keys[16], (FF, D), jnp.float32) ** block_levels(arg_keys[16], (FF, D), ((0, 32),), -0.2, 0.2)), 1.411013528240801e-10, 5.644054112963204e-10),
        "second_vectors": jnp.clip(jnp.exp(math.log(9.030486580741126e-09) - 1.3862944 * jax.random.uniform(arg_keys[17], (VROWS, D), jnp.float32) ** block_levels(arg_keys[17], (VROWS, D), ((1, 32),), -0.2, 0.2)), 2.2576216451852815e-09, 9.030486580741126e-09),
    }


@jax.custom_vjp
def low(v):
    return lax.optimization_barrier(v.astype(jnp.bfloat16)).astype(jnp.float32)

@jax.custom_vjp
def low_back(v):
    return v

def low_keep(v):
    return (low(v), None)

def low_pass(kept, grad):
    return (grad,)

def back_keep(v):
    return (v, None)

def back_low(kept, grad):
    return (low(grad),)
low.defvjp(low_keep, low_pass)
low_back.defvjp(back_keep, back_low)
precise = lax.Precision.HIGHEST
norm_eps = 1e-06
clip_limit = 1.0
beta_one = 0.9
beta_two = 0.999
adam_eps = 1e-08
rate_matrix = 0.08
rate_vector = 0.5
decay_matrix = 0.1
score_scale = 0.125

def layer_norm(values, gain_row, shift_row):
    centre = lax.optimization_barrier(jnp.mean(values, axis=-1, keepdims=True))
    offset = values - centre
    spread = lax.optimization_barrier(jnp.mean(offset * offset, axis=-1, keepdims=True))
    return offset * lax.rsqrt(spread + norm_eps) * gain_row + shift_row

def softmax_rows(scores):
    shifted = scores - lax.optimization_barrier(jnp.max(scores, axis=-1, keepdims=True))
    weights = jnp.exp(shifted)
    return weights / lax.optimization_barrier(jnp.sum(weights, axis=-1, keepdims=True))

def layer_forward(weights, inputs):
    qkv_low, out_low, up_low, down_low, vector_low = [low(weight) for weight in weights]
    image_count = inputs.shape[0]
    normed = low(layer_norm(inputs, vector_low[0], vector_low[1]))
    bias_qkv = jnp.concatenate([vector_low[2], jnp.zeros_like(vector_low[2]), vector_low[3]])
    projected = jnp.einsum('bsd,de->bse', normed, qkv_low, precision=precise) + bias_qkv
    projected = low(low_back(projected)).reshape(image_count, S, 3, HEADS, HD)
    queries = projected[:, :, 0]
    keys_all = projected[:, :, 1]
    values_all = projected[:, :, 2]
    scores = low_back(jnp.einsum('bqhd,bkhd->bhqk', queries, keys_all, precision=precise) * score_scale)
    probabilities = low(softmax_rows(scores))
    mixed_heads = jnp.einsum('bhqk,bkhd->bqhd', probabilities, values_all, precision=precise).reshape(image_count, S, D)
    mixed_heads = low(low_back(mixed_heads))
    attended = low_back(jnp.einsum('bsd,de->bse', mixed_heads, out_low, precision=precise) + vector_low[4])
    middle = inputs + attended
    normed_two = low(layer_norm(middle, vector_low[5], vector_low[6]))
    upward = low_back(jnp.einsum('bsd,df->bsf', normed_two, up_low, precision=precise) + vector_low[8:].reshape(FF))
    active = low(jax.nn.gelu(upward, approximate=True))
    downward = low_back(jnp.einsum('bsf,fd->bsd', active, down_low, precision=precise) + vector_low[7])
    return middle + downward

def adam_update(master, raw_grad, moment_one, moment_two, factor, step_rate, decay_rate):
    clipped = raw_grad * factor
    moment_one_new = beta_one * moment_one + (1.0 - beta_one) * clipped
    moment_two_new = beta_two * moment_two + (1.0 - beta_two) * clipped * clipped
    first_hat = moment_one_new / (1.0 - beta_one ** STEP)
    second_hat = moment_two_new / (1.0 - beta_two ** STEP)
    master_new = master - step_rate * (first_hat / (jnp.sqrt(second_hat) + adam_eps) + decay_rate * master)
    return (clipped, master_new, moment_one_new, moment_two_new)

def reference(images, pair_matrix, caption_grads, qkv_weight, out_weight, up_weight, down_weight, vector_rows, first_qkv, first_out, first_up, first_down, first_vectors, second_qkv, second_out, second_up, second_down, second_vectors):
    weights = (qkv_weight, out_weight, up_weight, down_weight, vector_rows)
    pair_blocks = pair_matrix.astype(jnp.float32).reshape(N_DEV, IMG_DEV, CAP_DEV)
    caption_blocks = caption_grads.astype(jnp.float32).reshape(N_DEV, CAP_DEV, S * D)
    upstream = jnp.einsum('nic,ncf->nif', pair_blocks, caption_blocks, precision=precise)
    block_size = math.gcd(IMAGES, 16)
    block_count = IMAGES // block_size
    upstream = upstream.reshape(block_count, block_size, S, D)
    inputs_all = images.astype(jnp.float32).reshape(block_count, block_size, S, D)

    def one_block(totals, block_pair):
        inputs, cotangent = block_pair
        result, pullback = jax.vjp(layer_forward, weights, inputs)
        weight_grads, input_part = pullback(cotangent)
        totals = tuple((running + grad_part for running, grad_part in zip(totals, weight_grads)))
        return (totals, (result, input_part))
    zero_grads = tuple((jnp.zeros(weight.shape, jnp.float32) for weight in weights))
    summed, (outputs, input_grads) = lax.scan(one_block, zero_grads, (inputs_all, upstream))
    squares = jnp.sum(summed[0] * summed[0]) + jnp.sum(summed[1] * summed[1]) + jnp.sum(summed[2] * summed[2]) + jnp.sum(summed[3] * summed[3]) + jnp.sum(summed[4] * summed[4])
    grad_norm = jnp.sqrt(squares)
    factor = clip_limit / jnp.maximum(grad_norm, clip_limit)
    qkv_parts = adam_update(qkv_weight, summed[0], first_qkv, second_qkv, factor, rate_matrix, decay_matrix)
    out_parts = adam_update(out_weight, summed[1], first_out, second_out, factor, rate_matrix, decay_matrix)
    up_parts = adam_update(up_weight, summed[2], first_up, second_up, factor, rate_matrix, decay_matrix)
    down_parts = adam_update(down_weight, summed[3], first_down, second_down, factor, rate_matrix, decay_matrix)
    vector_parts = adam_update(vector_rows, summed[4], first_vectors, second_vectors, factor, rate_vector, 0.0)
    return (outputs.reshape(IMAGES, S, D), input_grads.reshape(IMAGES, S, D), grad_norm, qkv_parts[0], qkv_parts[1], qkv_parts[2], qkv_parts[3], out_parts[0], out_parts[1], out_parts[2], out_parts[3], up_parts[0], up_parts[1], up_parts[2], up_parts[3], down_parts[0], down_parts[1], down_parts[2], down_parts[3], vector_parts[0], vector_parts[1], vector_parts[2], vector_parts[3])
```

```python
import jax
import jax.numpy as jnp
from jax import lax
from jax.experimental import pallas as pl
from jax.experimental.pallas import tpu as pltpu
from jax.sharding import PartitionSpec as P

HD = 64
STEP = 10


norm_eps = 1e-06
clip_limit = 1.0
beta_one = 0.9
beta_two = 0.999
adam_eps = 1e-08
rate_matrix = 0.08
rate_vector = 0.5
decay_matrix = 0.1
score_scale = 0.125


def layer_norm(values, gain_row, shift_row):
    centre = jnp.mean(values, axis=-1, keepdims=True)
    offset = values - centre
    spread = jnp.mean(offset * offset, axis=-1, keepdims=True)
    return offset * lax.rsqrt(spread + norm_eps) * gain_row + shift_row


def softmax_rows(scores):
    shifted = scores - jnp.max(scores, axis=-1, keepdims=True)
    weights = jnp.exp(shifted)
    return weights / jnp.sum(weights, axis=-1, keepdims=True)


def gelu_tanh(values):
    return jax.nn.gelu(values, approximate=True)


def contract_last(left_side, right_side):
    return lax.dot_general(
        left_side, right_side, (((1,), (1,)), ((), ())), preferred_element_type=jnp.float32
    )


def contract_first(left_side, right_side):
    return lax.dot_general(
        left_side, right_side, (((0,), (0,)), ((), ())), preferred_element_type=jnp.float32
    )


def forward_pass(gathered, inputs):
    qkv_full, out_full, up_full, down_full, vector_low = gathered
    vector_full = vector_low.astype(jnp.float32)
    image_count, patches, model_width = inputs.shape
    row_count = image_count * patches
    head_count = model_width // HD
    flat_inputs = inputs.astype(jnp.float32).reshape(row_count, model_width)
    normed_low = layer_norm(flat_inputs, vector_full[0], vector_full[1]).astype(jnp.bfloat16)
    bias_qkv = jnp.concatenate([vector_full[2], jnp.zeros_like(vector_full[2]), vector_full[3]])
    projected = jnp.dot(normed_low, qkv_full, preferred_element_type=jnp.float32) + bias_qkv
    projected_low = projected.astype(jnp.bfloat16).reshape(image_count, patches, 3, head_count, HD)
    queries = projected_low[:, :, 0]
    keys_all = projected_low[:, :, 1]
    values_all = projected_low[:, :, 2]
    scores = (
        jnp.einsum("bqhd,bkhd->bhqk", queries, keys_all, preferred_element_type=jnp.float32)
        * score_scale
    )
    probabilities = softmax_rows(scores)
    prob_low = probabilities.astype(jnp.bfloat16)
    mixed_heads = jnp.einsum(
        "bhqk,bkhd->bqhd", prob_low, values_all, preferred_element_type=jnp.float32
    )
    mixed_low = mixed_heads.reshape(row_count, model_width).astype(jnp.bfloat16)
    attended = jnp.dot(mixed_low, out_full, preferred_element_type=jnp.float32) + vector_full[4]
    middle = flat_inputs + attended
    normed_two_low = layer_norm(middle, vector_full[5], vector_full[6]).astype(jnp.bfloat16)
    upward = jnp.dot(normed_two_low, up_full, preferred_element_type=jnp.float32) + vector_full[
        8:
    ].reshape(-1)
    active_low = gelu_tanh(upward).astype(jnp.bfloat16)
    downward = jnp.dot(active_low, down_full, preferred_element_type=jnp.float32) + vector_full[7]
    result = middle + downward
    kept_values = (
        flat_inputs,
        normed_low,
        queries,
        keys_all,
        values_all,
        probabilities,
        prob_low,
        mixed_low,
        middle,
        normed_two_low,
        upward,
        active_low,
    )
    return (result, kept_values)


def adam_update(master, raw_grad, moment_one, moment_two, factor, step_rate, decay_rate):
    clipped = raw_grad * factor
    moment_one_new = beta_one * moment_one + (1.0 - beta_one) * clipped
    moment_two_new = beta_two * moment_two + (1.0 - beta_two) * clipped * clipped
    first_hat = moment_one_new / (1.0 - beta_one**STEP)
    second_hat = moment_two_new / (1.0 - beta_two**STEP)
    master_new = master - step_rate * (
        first_hat / (jnp.sqrt(second_hat) + adam_eps) + decay_rate * master
    )
    return (clipped, master_new, moment_one_new, moment_two_new)


MESH = pl.DeviceIdType.MESH
bf = jnp.bfloat16
f32 = jnp.float32
VMEM = pltpu.VMEM
WNAMES = ("qkv", "out", "up", "down")


class Place:
    def __init__(self):
        me = lax.axis_index("dev")
        self.me = me
        self.c = me % 2
        self.x = (me // 2) % 2
        self.y = (me // 4) % 2
        self.z = me // 8
        self.q = me // 2
        self.sib = me + 1 - 2 * self.c
        self.xn = me + 2 - 4 * self.x
        self.yn = me + 4 - 8 * self.y
        self.xo = 1 - self.x
        self.yo = 1 - self.y

    def zz(self, k):
        return (self.z + k) % 4

    def zp(self, k):
        return self.zz(k) * 8 + self.me % 8

    def chip(self, k, y, x):
        return self.zz(k) * 4 + y * 2 + x

    def greet(self):
        bar = pltpu.get_barrier_semaphore()
        for dev in (self.sib, self.xn, self.yn, self.zp(1), self.zp(2), self.zp(3)):
            pl.semaphore_signal(bar, inc=1, device_id=(dev,), device_id_type=MESH)

    def meet(self):
        pl.semaphore_wait(pltpu.get_barrier_semaphore(), 6)


class Sends:
    def __init__(self, sems):
        self.sems = sems
        self.used = 0
        self.open = []

    def go(self, src, dst, recv, dev):
        copy = pltpu.make_async_remote_copy(
            src_ref=src, dst_ref=dst, send_sem=self.sems.at[self.used], recv_sem=recv,
            device_id=(dev,), device_id_type=MESH,
        )
        self.used += 1
        copy.start()
        self.open.append(copy)

    def drain(self):
        for copy in self.open:
            copy.wait_send()
        self.open = []


def await_recv(place, ref, recv, spare):
    pltpu.make_async_remote_copy(
        src_ref=ref, dst_ref=ref, send_sem=spare, recv_sem=recv,
        device_id=(place.sib,), device_id_type=MESH,
    ).wait_recv()


SPLIT = {"qkv": 640, "out": 128, "up": 768}


def piece(name, shape, rows_at, rows, c, part):
    half = shape[1] // 2
    col = c * half
    if name == "down" or part is None:
        width = half
    else:
        first = SPLIT[name]
        width = first if part == 0 else half - first
        col = col + (0 if part == 0 else first)
    if name == "down" and part is not None:
        rows = rows // 2
        rows_at = rows_at + part * rows
    return (pl.ds(pl.multiple_of(rows_at, 16), rows), pl.ds(pl.multiple_of(col, 128), width))


class Gather:
    def __init__(self, place, shards, stages, fulls, sends, stage_sem, rail_sem, sib_sem):
        self.p = place
        self.shards, self.stages, self.fulls = shards, stages, fulls
        self.sends, self.stage_sem, self.rail_sem, self.sib_sem = sends, stage_sem, rail_sem, sib_sem

    def at(self, w, q, part, c=None):
        full = self.fulls[w]
        rows = full.shape[0] // 16
        return full.at[piece(WNAMES[w], full.shape, q * rows, rows, self.p.c if c is None else c, part)]

    def stage(self, w):
        p, half = self.p, self.fulls[w].shape[1] // 2
        self.sends.go(
            self.shards[w].at[:, pl.ds(pl.multiple_of((1 - p.c) * half, 128), half)],
            self.stages[w], self.stage_sem.at[w], p.sib,
        )

    def own(self, w):
        p, full = self.p, self.fulls[w]
        half, rows = full.shape[1] // 2, full.shape[0] // 16
        await_recv(p, self.stages[w], self.stage_sem.at[w], self.sends.sems.at[0])
        mine = self.shards[w][:, pl.ds(pl.multiple_of(p.c * half, 128), half)]
        other = self.stages[w][...]
        low = p.c == 0
        block = jnp.concatenate([jnp.where(low, mine, other), jnp.where(low, other, mine)], axis=0)
        full[piece(WNAMES[w], full.shape, p.q * rows, rows, p.c, None)] = block.astype(bf)
        for k in (1, 2, 3):
            ref = self.at(w, p.q, None)
            self.sends.go(ref, ref, self.rail_sem.at[w, p.q, 0], p.zp(k))
        self.plane(w, 0)

    def plane(self, w, k):
        p = self.p
        q = p.chip(k, p.y, p.x)
        for part in (0, 1):
            ref = self.at(w, q, part)
            order = (p.xn, p.yn) if part == 0 else (p.yn, p.xn)
            for dev in order:
                self.sends.go(ref, ref, self.rail_sem.at[w, q, part], dev)

    def wait(self, w, q, part, sem_part):
        await_recv(self.p, self.at(w, q, part), self.rail_sem.at[w, q, sem_part], self.sends.sems.at[0])

    def arrive(self, w, k):
        self.wait(w, self.p.chip(k, self.p.y, self.p.x), None, 0)
        self.plane(w, k)

    def forward(self, w, k):
        p = self.p
        q = p.chip(k, p.y, p.xo)
        self.wait(w, q, 0, 0)
        ref = self.at(w, q, 0)
        self.sends.go(ref, ref, self.rail_sem.at[w, q, 0], p.yn)
        q = p.chip(k, p.yo, p.x)
        self.wait(w, q, 1, 1)
        ref = self.at(w, q, 1)
        self.sends.go(ref, ref, self.rail_sem.at[w, q, 1], p.xn)

    def level(self, w, k, c):
        full = self.fulls[w]
        rows = full.shape[0] // 4
        return full.at[piece(WNAMES[w], full.shape, self.p.zz(k) * rows, rows, c, None)]

    def share(self, w, k):
        p = self.p
        self.wait(w, p.chip(k, p.y, p.xo), 1, 1)
        self.wait(w, p.chip(k, p.yo, p.x), 0, 0)
        self.wait(w, p.chip(k, p.yo, p.xo), 0, 0)
        self.wait(w, p.chip(k, p.yo, p.xo), 1, 1)
        ref = self.level(w, k, p.c)
        self.sends.go(ref, ref, self.sib_sem.at[w, p.zz(k)], p.sib)

    def finish(self, w):
        for k in range(4):
            await_recv(self.p, self.level(w, k, 1 - self.p.c), self.sib_sem.at[w, self.p.zz(k)], self.sends.sems.at[0])


class GatherVectors:
    def __init__(self, place, slots, sends, rail_sem, sib_sem):
        self.p, self.slots, self.sends, self.rail_sem, self.sib_sem = place, slots, sends, rail_sem, sib_sem

    def go(self, q, dev):
        ref = self.slots.at[q * 2 + self.p.c]
        self.sends.go(ref, ref, self.rail_sem.at[q], dev)

    def wait(self, q):
        await_recv(self.p, self.slots.at[q * 2 + self.p.c], self.rail_sem.at[q], self.sends.sems.at[0])

    def own(self):
        p = self.p
        for k in (1, 2, 3):
            self.go(p.q, p.zp(k))
        self.go(p.q, p.xn)
        self.go(p.q, p.yn)

    def rest(self):
        p = self.p
        for k in (1, 2, 3):
            q = p.chip(k, p.y, p.x)
            self.wait(q)
            self.go(q, p.xn)
            self.go(q, p.yn)
        for k in range(4):
            q = p.chip(k, p.y, p.xo)
            self.wait(q)
            self.go(q, p.yn)
        for k in range(4):
            self.wait(p.chip(k, p.yo, p.x))
            self.wait(p.chip(k, p.yo, p.xo))
        for k in range(4):
            for y in (0, 1):
                for x in (0, 1):
                    q = p.chip(k, y, x)
                    ref = self.slots.at[q * 2 + p.c]
                    self.sends.go(ref, ref, self.sib_sem.at[q], p.sib)
        for k in range(4):
            for y in (0, 1):
                for x in (0, 1):
                    q = p.chip(k, y, x)
                    await_recv(p, self.slots.at[q * 2 + 1 - p.c], self.sib_sem.at[q], self.sends.sems.at[0])


def join_vectors(slots):
    lane = lax.broadcasted_iota(jnp.int32, (16, 128), 1)
    tiles = [jnp.zeros((16, 128), f32) for _ in range(7)]
    for d in range(32):
        tile, off = (24 * d) // 128, (24 * d) % 128
        turned = pltpu.roll(slots[d], off, 1) if off else slots[d]
        tiles[tile] = jnp.where((lane >= off) & (lane < off + 24), turned, tiles[tile])
        if off + 24 > 128:
            tiles[tile + 1] = jnp.where(lane < off - 104, turned, tiles[tile + 1])
    return jnp.concatenate(tiles[:6], axis=1).astype(bf).astype(f32)


class Reduce:
    def __init__(self, place, w, grad, bufs, final, swap, sends, sems):
        self.p, self.w, self.grad, self.final, self.swap = place, w, grad, final, swap
        self.cb, self.pa, self.pb, self.qa, self.qb, self.zb = bufs
        self.sends, self.sems = sends, sems
        self.name = WNAMES[w]
        self.rows, self.cols = grad.shape[3], grad.shape[4]
        self.half = self.cols // 2

    def col(self, c):
        return pl.ds(pl.multiple_of(c * self.half, 128), self.half)

    def part(self, part):
        if self.name == "down":
            return (pl.ds(part * (self.rows // 2), self.rows // 2), self.col(self.p.c))
        first = SPLIT[self.name]
        start = self.p.c * self.half + (0 if part == 0 else first)
        return (slice(None), pl.ds(pl.multiple_of(start, 128), first if part == 0 else self.half - first))

    def wait(self, ref, n):
        await_recv(self.p, ref, self.sems.at[self.w, n], self.sends.sems.at[0])

    def core_go(self):
        self.sends.go(self.grad.at[:, :, :, :, self.col(1 - self.p.c)], self.cb, self.sems.at[self.w, 0], self.p.sib)

    def add(self, index, buf, at, parts):
        cur = self.grad[index].astype(f32) + buf[at].astype(f32)
        self.grad[index] = cur.astype(bf)

    def core_add(self):
        self.wait(self.cb, 0)
        col = self.col(self.p.c)

        def body(i, _):
            z, y, x = i // 4, (i // 2) % 2, i % 2
            self.add((z, y, x, slice(None), col), self.cb, (z, y, x), None)
            return 0
        lax.fori_loop(0, 16, body, 0)

    def first_go(self):
        p = self.p
        self.sends.go(self.grad.at[(slice(None), p.yo, slice(None)) + self.part(0)], self.pa, self.sems.at[self.w, 1], p.yn)
        self.sends.go(self.grad.at[(slice(None), slice(None), p.xo) + self.part(1)], self.pb, self.sems.at[self.w, 2], p.xn)

    def first_add(self):
        p = self.p
        self.wait(self.pa, 1)
        self.wait(self.pb, 2)

        def body(i, _):
            z, o = i // 2, i % 2
            self.add((z, p.y, o) + self.part(0), self.pa, (z, o), None)
            self.add((z, o, p.x) + self.part(1), self.pb, (z, o), None)
            return 0
        lax.fori_loop(0, 8, body, 0)

    def second_go(self):
        p = self.p
        self.sends.go(self.grad.at[(slice(None), p.y, p.xo) + self.part(0)], self.qa, self.sems.at[self.w, 3], p.xn)
        self.sends.go(self.grad.at[(slice(None), p.yo, p.x) + self.part(1)], self.qb, self.sems.at[self.w, 4], p.yn)

    def second_add(self):
        p = self.p
        self.wait(self.qa, 3)
        self.wait(self.qb, 4)

        def body(z, _):
            self.add((z, p.y, p.x) + self.part(0), self.qa, (z,), None)
            self.add((z, p.y, p.x) + self.part(1), self.qb, (z,), None)
            return 0
        lax.fori_loop(0, 4, body, 0)

    def line_go(self):
        p = self.p
        for k in (1, 2, 3):
            self.sends.go(
                self.grad.at[p.zz(k), p.y, p.x, :, self.col(p.c)], self.zb.at[k - 1], self.sems.at[self.w, 4 + k], p.zp(k)
            )

    def line_add(self):
        p = self.p
        for k in (1, 2, 3):
            self.wait(self.zb.at[k - 1], 4 + k)
        total = self.grad[p.z, p.y, p.x, :, self.col(p.c)].astype(f32)
        for k in range(3):
            total = total + self.zb[k].astype(f32)
        self.final[...] = total
        shard = self.rows // 2
        self.sends.go(
            self.final.at[pl.ds(pl.multiple_of((1 - p.c) * shard, 8), shard), :], self.swap, self.sems.at[self.w, 8], p.sib
        )
        square = total * total
        tile = jnp.sum(square.reshape(self.rows // 8, 8, self.half), axis=0)
        folded = tile[:, :128]
        for j in range(1, self.half // 128):
            folded = folded + tile[:, j * 128 : (j + 1) * 128]
        return folded

    def emit(self, out):
        p, shard = self.p, self.rows // 2
        out[:, self.col(p.c)] = self.final[pl.ds(pl.multiple_of(p.c * shard, 8), shard), :]
        self.wait(self.swap, 8)
        out[:, self.col(1 - p.c)] = self.swap[...]


class SumAll:
    def __init__(self, place, value, buf, zbuf, sends, sems):
        self.p, self.value, self.buf, self.zbuf, self.sends, self.sems = place, value, buf, zbuf, sends, sems

    def hop(self, n, dev):
        self.sends.go(self.value, self.buf.at[n], self.sems.at[n], dev)
        await_recv(self.p, self.buf.at[n], self.sems.at[n], self.sends.sems.at[0])
        self.sends.open.pop().wait_send()
        self.value[...] = self.value[...] + self.buf[n]

    def run(self):
        p = self.p
        self.hop(0, p.sib)
        self.hop(1, p.xn)
        self.hop(2, p.yn)
        self.zbuf[p.z] = self.value[...]
        for k in (1, 2, 3):
            self.sends.go(self.value, self.zbuf.at[p.z], self.sems.at[3 + p.z], p.zp(k))
        for k in (1, 2, 3):
            await_recv(p, self.zbuf.at[p.zz(k)], self.sems.at[3 + p.zz(k)], self.sends.sems.at[0])
        return (self.zbuf[0] + self.zbuf[1]) + (self.zbuf[2] + self.zbuf[3])


def gather_kernel(
    qkv_in, out_in, up_in, down_in, vec_in, qkv_hbm, out_hbm, up_hbm, down_hbm, vec_out,
    qkv_full, out_full, up_full, down_full, slots, s0, s1, s2, s3,
    send_sem, stage_sem, rail_sem, sib_sem, vrail_sem, vsib_sem, local_sem,
):
    place = Place()
    place.greet()
    sends = Sends(send_sem)
    fulls = (qkv_full, out_full, up_full, down_full)
    tile = jnp.zeros((16, 128), f32)
    slots[place.me] = tile
    slots[place.me, 0:12, 0:24] = vec_in[...]
    ag = Gather(place, (qkv_in, out_in, up_in, down_in), (s0, s1, s2, s3), fulls, sends, stage_sem, rail_sem, sib_sem)
    av = GatherVectors(place, slots, sends, vrail_sem, vsib_sem)
    place.meet()
    for w in range(4):
        ag.stage(w)
    av.own()
    for w in range(4):
        ag.own(w)

    def flow(w):
        ag.forward(w, 0)
        for k in (1, 2, 3):
            ag.arrive(w, k)
            ag.forward(w, k)

    def share(w):
        for k in range(4):
            ag.share(w, k)
    flow(0)
    av.rest()
    vec_out[...] = join_vectors(slots)
    flow(1)
    share(0)
    flow(2)
    share(1)
    flow(3)
    share(2)
    share(3)
    copies = []
    for w, hbm in enumerate((qkv_hbm, out_hbm, up_hbm, down_hbm)):
        ag.finish(w)
        copy = pltpu.make_async_copy(fulls[w], hbm, local_sem.at[w])
        copy.start()
        copies.append(copy)
    sends.drain()
    for copy in copies:
        copy.wait()


def gather_all(weights, vectors):
    shapes = [(w.shape[0] * 32, w.shape[1]) for w in weights]
    dma = pltpu.SemaphoreType.DMA
    vm = pl.BlockSpec(memory_space=VMEM)
    return pl.pallas_call(
        gather_kernel,
        out_shape=[jax.ShapeDtypeStruct(s, bf) for s in shapes] + [jax.ShapeDtypeStruct((16, 768), f32)],
        in_specs=[vm] * 5,
        out_specs=[pl.BlockSpec(memory_space=pl.ANY)] * 4 + [vm],
        scratch_shapes=[VMEM(s, bf) for s in shapes]
        + [VMEM((32, 16, 128), f32)]
        + [VMEM((w.shape[0], w.shape[1] // 2), f32) for w in weights]
        + [dma((160,)), dma((4,)), dma((4, 16, 2)), dma((4, 4)), dma((16,)), dma((16,)), dma((4,))],
        compiler_params=pltpu.CompilerParams(collective_id=0, has_side_effects=True, vmem_limit_bytes=56 << 20),
        name="gather_all",
    )(*weights, vectors)


def reduce_kernel(
    g0, g1, g2, g3, vec_in, r0, r1, r2, r3, vec_out, norm_out, *scratch
):
    grads = scratch[0:4]
    bufs = [scratch[4 + 6 * w : 10 + 6 * w] for w in range(4)]
    finals, swaps = scratch[28:32], scratch[32:36]
    vval, vbuf, vz, nval, nbuf, nz = scratch[36:42]
    send_sem, sems, vsem, nsem, local_sem = scratch[42:]
    place = Place()
    place.greet()
    copies = [pltpu.make_async_copy(g, s, local_sem.at[i]) for i, (g, s) in enumerate(zip((g0, g1, g2, g3), grads))]
    order = (3, 2, 1, 0)
    for w in order:
        copies[w].start()
    sends = Sends(send_sem)
    reds = [Reduce(place, w, grads[w], bufs[w], finals[w], swaps[w], sends, sems) for w in range(4)]
    vval[...] = vec_in[...]
    place.meet()
    for w in order:
        copies[w].wait()
        reds[w].core_go()
    vsum = SumAll(place, vval, vbuf, vz, sends, vsem).run()
    vec_out[...] = vsum
    squares = jnp.zeros((8, 128), f32)
    for t in range(7):
        if t < 4:
            reds[order[t]].core_add()
            reds[order[t]].first_go()
        if 1 <= t < 5:
            reds[order[t - 1]].first_add()
            reds[order[t - 1]].second_go()
        if 2 <= t < 6:
            reds[order[t - 2]].second_add()
            reds[order[t - 2]].line_go()
        if 3 <= t:
            squares = squares + reds[order[t - 3]].line_add()
    nval[...] = squares
    total = SumAll(place, nval, nbuf, nz, sends, nsem).run()
    whole = jnp.sum(total) + jnp.sum(vsum * vsum)
    norm_out[0, 0] = whole
    for w, out in zip(order, (r3, r2, r1, r0)):
        reds[w].emit(out)
    sends.drain()


def reduce_all(grads, vectors):
    dma = pltpu.SemaphoreType.DMA
    vm = pl.BlockSpec(memory_space=VMEM)
    shapes, bufs, finals, swaps, outs = [], [], [], [], []
    for name, g in zip(WNAMES, grads):
        rows, cols = g.shape[0] // 16, g.shape[1]
        half = cols // 2
        shapes.append((4, 2, 2, rows, cols))
        if name == "down":
            a = b = (rows // 2, half)
        else:
            a, b = (rows, SPLIT[name]), (rows, half - SPLIT[name])
        bufs += [
            VMEM((4, 2, 2, rows, half), bf), VMEM((4, 2) + a, bf), VMEM((4, 2) + b, bf),
            VMEM((4,) + a, bf), VMEM((4,) + b, bf), VMEM((3, rows, half), bf),
        ]
        finals.append(VMEM((rows, half), f32))
        swaps.append(VMEM((rows // 2, half), f32))
        outs.append(jax.ShapeDtypeStruct((rows // 2, cols), f32))
    return pl.pallas_call(
        reduce_kernel,
        out_shape=outs + [jax.ShapeDtypeStruct((16, 768), f32), jax.ShapeDtypeStruct((1, 1), f32)],
        in_specs=[pl.BlockSpec(memory_space=pl.ANY)] * 4 + [vm],
        out_specs=[vm] * 5 + [pl.BlockSpec(memory_space=pltpu.SMEM)],
        scratch_shapes=[VMEM(s, bf) for s in shapes] + bufs + finals + swaps
        + [VMEM((16, 768), f32), VMEM((3, 16, 768), f32), VMEM((4, 16, 768), f32)]
        + [VMEM((8, 128), f32), VMEM((3, 8, 128), f32), VMEM((4, 8, 128), f32)]
        + [dma((64,)), dma((4, 9)), dma((7,)), dma((7,)), dma((4,))],
        compiler_params=pltpu.CompilerParams(collective_id=1, has_side_effects=True, vmem_limit_bytes=60 << 20),
        name="reduce_all",
    )(*[g.reshape(s) for g, s in zip(grads, shapes)], vectors)


def local_wide(
    images,
    pair_matrix,
    caption_grads,
    qkv_weight,
    out_weight,
    up_weight,
    down_weight,
    vector_rows,
    first_qkv,
    first_out,
    first_up,
    first_down,
    first_vectors,
    second_qkv,
    second_out,
    second_up,
    second_down,
    second_vectors,
):
    image_count, patches, model_width = images.shape
    row_count = image_count * patches
    head_count = model_width // HD
    qkv_low = qkv_weight.astype(jnp.bfloat16)
    out_low = out_weight.astype(jnp.bfloat16)
    up_low = up_weight.astype(jnp.bfloat16)
    down_low = down_weight.astype(jnp.bfloat16)
    vector_low = vector_rows.astype(jnp.bfloat16)
    gathered = (
        lax.all_gather(qkv_low, "dev", axis=0, tiled=True),
        lax.all_gather(out_low, "dev", axis=0, tiled=True),
        lax.all_gather(up_low, "dev", axis=0, tiled=True),
        lax.all_gather(down_low, "dev", axis=0, tiled=True),
        lax.all_gather(vector_low, "dev", axis=1, tiled=True),
    )
    result, unused_values = forward_pass(gathered, images)
    output = result.reshape(image_count, patches, model_width)
    gathered_again = (
        lax.all_gather(qkv_low, "dev", axis=0, tiled=True),
        lax.all_gather(out_low, "dev", axis=0, tiled=True),
        lax.all_gather(up_low, "dev", axis=0, tiled=True),
        lax.all_gather(down_low, "dev", axis=0, tiled=True),
        lax.all_gather(vector_low, "dev", axis=1, tiled=True),
    )
    qkv_full, out_full, up_full, down_full, vector_again = gathered_again
    vector_full = vector_again.astype(jnp.float32)
    recomputed, kept_values = forward_pass(gathered_again, images)
    (
        flat_inputs,
        normed_low,
        queries,
        keys_all,
        values_all,
        probabilities,
        prob_low,
        mixed_low,
        middle,
        normed_two_low,
        upward,
        active_low,
    ) = kept_values
    caption_flat = caption_grads.reshape(caption_grads.shape[0], patches * model_width)
    upstream = jnp.dot(
        pair_matrix.astype(jnp.bfloat16), caption_flat, preferred_element_type=jnp.float32
    ).reshape(row_count, model_width)
    down_grad_low = upstream.astype(jnp.bfloat16)
    raw_down = contract_first(active_low, down_grad_low)
    bias_down_grad = jnp.sum(down_grad_low.astype(jnp.float32), axis=0)
    active_grad = contract_last(down_grad_low, down_full)
    gelu_value, gelu_pull = jax.vjp(gelu_tanh, upward)
    upward_grad_low = gelu_pull(active_grad)[0].astype(jnp.bfloat16)
    raw_up = contract_first(normed_two_low, upward_grad_low)
    bias_up_grad = jnp.sum(upward_grad_low.astype(jnp.float32), axis=0)
    normed_two_grad = contract_last(upward_grad_low, up_full)
    second_norm_value, second_norm_pull = jax.vjp(
        layer_norm, middle, vector_full[5], vector_full[6]
    )
    middle_norm_grad, gain_two_grad, shift_two_grad = second_norm_pull(normed_two_grad)
    middle_grad = upstream + middle_norm_grad
    attended_low = middle_grad.astype(jnp.bfloat16)
    raw_out = contract_first(mixed_low, attended_low)
    bias_out_grad = jnp.sum(attended_low.astype(jnp.float32), axis=0)
    mixed_grad_low = (
        contract_last(attended_low, out_full)
        .astype(jnp.bfloat16)
        .reshape(image_count, patches, head_count, HD)
    )
    prob_grad = jnp.einsum(
        "bqhd,bkhd->bhqk", mixed_grad_low, values_all, preferred_element_type=jnp.float32
    )
    value_grad = jnp.einsum(
        "bhqk,bqhd->bkhd", prob_low, mixed_grad_low, preferred_element_type=jnp.float32
    )
    score_grad = probabilities * (
        prob_grad - jnp.sum(probabilities * prob_grad, axis=-1, keepdims=True)
    )
    score_grad_low = score_grad.astype(jnp.bfloat16)
    query_grad = (
        jnp.einsum("bhqk,bkhd->bqhd", score_grad_low, keys_all, preferred_element_type=jnp.float32)
        * score_scale
    )
    key_grad = (
        jnp.einsum("bhqk,bqhd->bkhd", score_grad_low, queries, preferred_element_type=jnp.float32)
        * score_scale
    )
    projected_grad_low = (
        jnp.stack([query_grad, key_grad, value_grad], axis=2)
        .astype(jnp.bfloat16)
        .reshape(row_count, 3 * model_width)
    )
    raw_qkv = contract_first(normed_low, projected_grad_low)
    bias_qkv_grad = jnp.sum(projected_grad_low.astype(jnp.float32), axis=0)
    normed_grad = contract_last(projected_grad_low, qkv_full)
    first_norm_value, first_norm_pull = jax.vjp(
        layer_norm, flat_inputs, vector_full[0], vector_full[1]
    )
    inputs_norm_grad, gain_one_grad, shift_one_grad = first_norm_pull(normed_grad)
    input_grads = (middle_grad + inputs_norm_grad).reshape(image_count, patches, model_width)
    small_rows = jnp.stack(
        [
            gain_one_grad,
            shift_one_grad,
            bias_qkv_grad[:model_width],
            bias_qkv_grad[2 * model_width :],
            bias_out_grad,
            gain_two_grad,
            shift_two_grad,
            bias_down_grad,
        ]
    )
    raw_vectors = jnp.concatenate([small_rows, bias_up_grad.reshape(-1, model_width)], axis=0)
    qkv_shard, out_shard, up_shard, down_shard, vector_shard = (
        lax.psum_scatter(raw_qkv, "dev", scatter_dimension=0, tiled=True),
        lax.psum_scatter(raw_out, "dev", scatter_dimension=0, tiled=True),
        lax.psum_scatter(raw_up, "dev", scatter_dimension=0, tiled=True),
        lax.psum_scatter(raw_down, "dev", scatter_dimension=0, tiled=True),
        lax.psum_scatter(raw_vectors, "dev", scatter_dimension=1, tiled=True),
    )
    local_squares = (
        jnp.sum(qkv_shard * qkv_shard)
        + jnp.sum(out_shard * out_shard)
        + jnp.sum(up_shard * up_shard)
        + jnp.sum(down_shard * down_shard)
        + jnp.sum(vector_shard * vector_shard)
    )
    grad_norm = jnp.sqrt(lax.psum(local_squares, "dev"))
    factor = clip_limit / jnp.maximum(grad_norm, clip_limit)
    qkv_parts = adam_update(
        qkv_weight, qkv_shard, first_qkv, second_qkv, factor, rate_matrix, decay_matrix
    )
    out_parts = adam_update(
        out_weight, out_shard, first_out, second_out, factor, rate_matrix, decay_matrix
    )
    up_parts = adam_update(
        up_weight, up_shard, first_up, second_up, factor, rate_matrix, decay_matrix
    )
    down_parts = adam_update(
        down_weight, down_shard, first_down, second_down, factor, rate_matrix, decay_matrix
    )
    vector_parts = adam_update(
        vector_rows, vector_shard, first_vectors, second_vectors, factor, rate_vector, 0.0
    )
    return (
        output,
        input_grads,
        grad_norm,
        qkv_parts[0],
        qkv_parts[1],
        qkv_parts[2],
        qkv_parts[3],
        out_parts[0],
        out_parts[1],
        out_parts[2],
        out_parts[3],
        up_parts[0],
        up_parts[1],
        up_parts[2],
        up_parts[3],
        down_parts[0],
        down_parts[1],
        down_parts[2],
        down_parts[3],
        vector_parts[0],
        vector_parts[1],
        vector_parts[2],
        vector_parts[3],
    )


def local_slice(
    images,
    pair_matrix,
    caption_grads,
    qkv_weight,
    out_weight,
    up_weight,
    down_weight,
    vector_rows,
    first_qkv,
    first_out,
    first_up,
    first_down,
    first_vectors,
    second_qkv,
    second_out,
    second_up,
    second_down,
    second_vectors,
):
    image_count, patches, model_width = images.shape
    row_count = image_count * patches
    head_count = model_width // HD
    *gathered, vector_rows_full = gather_all((qkv_weight, out_weight, up_weight, down_weight), vector_rows)
    vector_full = vector_rows_full[:12]
    qkv_full, out_full, up_full, down_full = gathered
    result, kept_values = forward_pass((*gathered, vector_full), images)
    output = result.reshape(image_count, patches, model_width)
    (
        flat_inputs,
        normed_low,
        queries,
        keys_all,
        values_all,
        probabilities,
        prob_low,
        mixed_low,
        middle,
        normed_two_low,
        upward,
        active_low,
    ) = kept_values
    caption_flat = caption_grads.reshape(caption_grads.shape[0], patches * model_width)
    upstream = jnp.dot(
        pair_matrix.astype(jnp.bfloat16), caption_flat, preferred_element_type=jnp.float32
    ).reshape(row_count, model_width)
    down_grad_low = upstream.astype(jnp.bfloat16)
    raw_down = contract_first(active_low, down_grad_low)
    bias_down_grad = jnp.sum(down_grad_low.astype(jnp.float32), axis=0)
    active_grad = contract_last(down_grad_low, down_full)
    gelu_value, gelu_pull = jax.vjp(gelu_tanh, upward)
    upward_grad_low = gelu_pull(active_grad)[0].astype(jnp.bfloat16)
    raw_up = contract_first(normed_two_low, upward_grad_low)
    bias_up_grad = jnp.sum(upward_grad_low.astype(jnp.float32), axis=0)
    normed_two_grad = contract_last(upward_grad_low, up_full)
    second_norm_value, second_norm_pull = jax.vjp(
        layer_norm, middle, vector_full[5], vector_full[6]
    )
    middle_norm_grad, gain_two_grad, shift_two_grad = second_norm_pull(normed_two_grad)
    middle_grad = upstream + middle_norm_grad
    attended_low = middle_grad.astype(jnp.bfloat16)
    raw_out = contract_first(mixed_low, attended_low)
    bias_out_grad = jnp.sum(attended_low.astype(jnp.float32), axis=0)
    mixed_grad_low = (
        contract_last(attended_low, out_full)
        .astype(jnp.bfloat16)
        .reshape(image_count, patches, head_count, HD)
    )
    prob_grad = jnp.einsum(
        "bqhd,bkhd->bhqk", mixed_grad_low, values_all, preferred_element_type=jnp.float32
    )
    value_grad = jnp.einsum(
        "bhqk,bqhd->bkhd", prob_low, mixed_grad_low, preferred_element_type=jnp.float32
    )
    score_grad = probabilities * (
        prob_grad - jnp.sum(probabilities * prob_grad, axis=-1, keepdims=True)
    )
    score_grad_low = score_grad.astype(jnp.bfloat16)
    query_grad = (
        jnp.einsum("bhqk,bkhd->bqhd", score_grad_low, keys_all, preferred_element_type=jnp.float32)
        * score_scale
    )
    key_grad = (
        jnp.einsum("bhqk,bqhd->bkhd", score_grad_low, queries, preferred_element_type=jnp.float32)
        * score_scale
    )
    projected_grad_low = (
        jnp.stack([query_grad, key_grad, value_grad], axis=2)
        .astype(jnp.bfloat16)
        .reshape(row_count, 3 * model_width)
    )
    raw_qkv = contract_first(normed_low, projected_grad_low)
    bias_qkv_grad = jnp.sum(projected_grad_low.astype(jnp.float32), axis=0)
    normed_grad = contract_last(projected_grad_low, qkv_full)
    first_norm_value, first_norm_pull = jax.vjp(
        layer_norm, flat_inputs, vector_full[0], vector_full[1]
    )
    inputs_norm_grad, gain_one_grad, shift_one_grad = first_norm_pull(normed_grad)
    input_grads = (middle_grad + inputs_norm_grad).reshape(image_count, patches, model_width)
    small_rows = jnp.stack(
        [
            gain_one_grad,
            shift_one_grad,
            bias_qkv_grad[:model_width],
            bias_qkv_grad[2 * model_width :],
            bias_out_grad,
            gain_two_grad,
            shift_two_grad,
            bias_down_grad,
        ]
    )
    raw_vectors = jnp.concatenate([small_rows, bias_up_grad.reshape(-1, model_width)], axis=0)
    low = jnp.bfloat16
    qkv_shard, out_shard, up_shard, down_shard, vector_sum, squares = reduce_all(
        (raw_qkv.astype(low), raw_out.astype(low), raw_up.astype(low), raw_down.astype(low)),
        jnp.pad(raw_vectors, ((0, 4), (0, 0))),
    )
    width = vector_rows.shape[1]
    vector_shard = lax.dynamic_slice(vector_sum, (0, lax.axis_index("dev") * width), (12, width))
    grad_norm = jnp.sqrt(squares[0, 0])
    factor = clip_limit / jnp.maximum(grad_norm, clip_limit)
    qkv_parts = adam_update(
        qkv_weight, qkv_shard, first_qkv, second_qkv, factor, rate_matrix, decay_matrix
    )
    out_parts = adam_update(
        out_weight, out_shard, first_out, second_out, factor, rate_matrix, decay_matrix
    )
    up_parts = adam_update(
        up_weight, up_shard, first_up, second_up, factor, rate_matrix, decay_matrix
    )
    down_parts = adam_update(
        down_weight, down_shard, first_down, second_down, factor, rate_matrix, decay_matrix
    )
    vector_parts = adam_update(
        vector_rows, vector_shard, first_vectors, second_vectors, factor, rate_vector, 0.0
    )
    return (
        output,
        input_grads,
        grad_norm,
        qkv_parts[0],
        qkv_parts[1],
        qkv_parts[2],
        qkv_parts[3],
        out_parts[0],
        out_parts[1],
        out_parts[2],
        out_parts[3],
        up_parts[0],
        up_parts[1],
        up_parts[2],
        up_parts[3],
        down_parts[0],
        down_parts[1],
        down_parts[2],
        down_parts[3],
        vector_parts[0],
        vector_parts[1],
        vector_parts[2],
        vector_parts[3],
    )


def solution(mesh):
    fits = mesh.shape["dev"] == 32
    return jax.shard_map(
        local_slice if fits else local_wide,
        mesh=mesh,
        in_specs=(
            P("dev", None, None),
            P("dev", None),
            P("dev", None, None),
            P("dev", None),
            P("dev", None),
            P("dev", None),
            P("dev", None),
            P(None, "dev"),
            P("dev", None),
            P("dev", None),
            P("dev", None),
            P("dev", None),
            P(None, "dev"),
            P("dev", None),
            P("dev", None),
            P("dev", None),
            P("dev", None),
            P(None, "dev"),
        ),
        out_specs=(
            P("dev", None, None),
            P("dev", None, None),
            P(),
            P("dev", None),
            P("dev", None),
            P("dev", None),
            P("dev", None),
            P("dev", None),
            P("dev", None),
            P("dev", None),
            P("dev", None),
            P("dev", None),
            P("dev", None),
            P("dev", None),
            P("dev", None),
            P("dev", None),
            P("dev", None),
            P("dev", None),
            P("dev", None),
            P(None, "dev"),
            P(None, "dev"),
            P(None, "dev"),
            P(None, "dev"),
        ),
        check_vma=False,
    )
```

```python
import jax
import jax.numpy as jnp
from jax import lax
from jax.experimental import pallas as pl
from jax.experimental.pallas import tpu as pltpu
from jax.sharding import PartitionSpec as P

HD = 64
STEP = 10


norm_eps = 1e-06
clip_limit = 1.0
beta_one = 0.9
beta_two = 0.999
adam_eps = 1e-08
rate_matrix = 0.08
rate_vector = 0.5
decay_matrix = 0.1
score_scale = 0.125


def layer_norm(values, gain_row, shift_row):
    centre = jnp.mean(values, axis=-1, keepdims=True)
    offset = values - centre
    spread = jnp.mean(offset * offset, axis=-1, keepdims=True)
    return offset * lax.rsqrt(spread + norm_eps) * gain_row + shift_row


def softmax_rows(scores):
    shifted = scores - jnp.max(scores, axis=-1, keepdims=True)
    weights = jnp.exp(shifted)
    return weights / jnp.sum(weights, axis=-1, keepdims=True)


def gelu_tanh(values):
    return jax.nn.gelu(values, approximate=True)


def contract_last(left_side, right_side):
    return lax.dot_general(
        left_side, right_side, (((1,), (1,)), ((), ())), preferred_element_type=jnp.float32
    )


def contract_first(left_side, right_side):
    return lax.dot_general(
        left_side, right_side, (((0,), (0,)), ((), ())), preferred_element_type=jnp.float32
    )


def forward_pass(gathered, inputs):
    qkv_full, out_full, up_full, down_full, vector_low = gathered
    vector_full = vector_low.astype(jnp.float32)
    image_count, patches, model_width = inputs.shape
    row_count = image_count * patches
    head_count = model_width // HD
    flat_inputs = inputs.astype(jnp.float32).reshape(row_count, model_width)
    normed_low = layer_norm(flat_inputs, vector_full[0], vector_full[1]).astype(jnp.bfloat16)
    bias_qkv = jnp.concatenate([vector_full[2], jnp.zeros_like(vector_full[2]), vector_full[3]])
    projected = jnp.dot(normed_low, qkv_full, preferred_element_type=jnp.float32) + bias_qkv
    projected_low = projected.astype(jnp.bfloat16).reshape(image_count, patches, 3, head_count, HD)
    queries = projected_low[:, :, 0]
    keys_all = projected_low[:, :, 1]
    values_all = projected_low[:, :, 2]
    scores = (
        jnp.einsum("bqhd,bkhd->bhqk", queries, keys_all, preferred_element_type=jnp.float32)
        * score_scale
    )
    probabilities = softmax_rows(scores)
    prob_low = probabilities.astype(jnp.bfloat16)
    mixed_heads = jnp.einsum(
        "bhqk,bkhd->bqhd", prob_low, values_all, preferred_element_type=jnp.float32
    )
    mixed_low = mixed_heads.reshape(row_count, model_width).astype(jnp.bfloat16)
    attended = jnp.dot(mixed_low, out_full, preferred_element_type=jnp.float32) + vector_full[4]
    middle = flat_inputs + attended
    normed_two_low = layer_norm(middle, vector_full[5], vector_full[6]).astype(jnp.bfloat16)
    upward = jnp.dot(normed_two_low, up_full, preferred_element_type=jnp.float32) + vector_full[
        8:
    ].reshape(-1)
    active_low = gelu_tanh(upward).astype(jnp.bfloat16)
    downward = jnp.dot(active_low, down_full, preferred_element_type=jnp.float32) + vector_full[7]
    result = middle + downward
    kept_values = (
        flat_inputs,
        normed_low,
        queries,
        keys_all,
        values_all,
        probabilities,
        prob_low,
        mixed_low,
        middle,
        normed_two_low,
        upward,
        active_low,
    )
    return (result, kept_values)


def adam_update(master, raw_grad, moment_one, moment_two, factor, step_rate, decay_rate):
    clipped = raw_grad * factor
    moment_one_new = beta_one * moment_one + (1.0 - beta_one) * clipped
    moment_two_new = beta_two * moment_two + (1.0 - beta_two) * clipped * clipped
    first_hat = moment_one_new / (1.0 - beta_one**STEP)
    second_hat = moment_two_new / (1.0 - beta_two**STEP)
    master_new = master - step_rate * (
        first_hat / (jnp.sqrt(second_hat) + adam_eps) + decay_rate * master
    )
    return (clipped, master_new, moment_one_new, moment_two_new)


MESH = pl.DeviceIdType.MESH
bf = jnp.bfloat16
f32 = jnp.float32
VMEM = pltpu.VMEM
ROWS = 208
UNIT = (4, 2, 2, 4, 48, 768)
CHUNKS = ((2, 0, 3), (2, 3, 1), (1, 0, 4), (0, 0, 4))


class Place:
    def __init__(self):
        me = lax.axis_index("dev")
        self.me = me
        self.c = me % 2
        self.x = (me // 2) % 2
        self.y = (me // 4) % 2
        self.z = me // 8
        self.q = me // 2
        self.sib = me + 1 - 2 * self.c
        self.xn = me + 2 - 4 * self.x
        self.yn = me + 4 - 8 * self.y
        self.xo = 1 - self.x
        self.yo = 1 - self.y

    def zz(self, k):
        return (self.z + k) % 4

    def zp(self, k):
        return self.zz(k) * 8 + self.me % 8

    def col(self, c):
        return pl.ds(pl.multiple_of(c * 384, 128), 384)

    def greet(self):
        bar = pltpu.get_barrier_semaphore()
        for dev in (self.sib, self.xn, self.yn, self.zp(1), self.zp(2), self.zp(3)):
            pl.semaphore_signal(bar, inc=1, device_id=(dev,), device_id_type=MESH)

    def meet(self):
        pl.semaphore_wait(pltpu.get_barrier_semaphore(), 6)


class Sends:
    def __init__(self, sems):
        self.sems = sems
        self.used = 0
        self.open = []

    def go(self, src, dst, recv, dev):
        copy = pltpu.make_async_remote_copy(
            src_ref=src, dst_ref=dst, send_sem=self.sems.at[self.used], recv_sem=recv,
            device_id=(dev,), device_id_type=MESH,
        )
        self.used += 1
        copy.start()
        self.open.append(copy)

    def drain(self):
        for copy in self.open:
            copy.wait_send()
        self.open = []


def await_recv(place, ref, recv, spare):
    pltpu.make_async_remote_copy(
        src_ref=ref, dst_ref=ref, send_sem=spare, recv_sem=recv,
        device_id=(place.sib,), device_id_type=MESH,
    ).wait_recv()


class Gather:
    def __init__(self, place, chunk, group, sends, rail_sem, sib_sem):
        self.p, self.group, self.sends = place, group, sends
        self.number = chunk
        _, self.first, self.count = CHUNKS[chunk]
        self.rail_sem, self.sib_sem = rail_sem.at[chunk], sib_sem.at[chunk]

    def at(self, k, y, x):
        return self.group.at[self.p.zz(k), y, x, pl.ds(self.first, self.count), :, self.p.col(self.p.c)]

    def sem(self, k, y, x):
        return self.rail_sem.at[self.p.zz(k) * 4 + y * 2 + x]

    def go(self, k, y, x, dev):
        ref = self.at(k, y, x)
        self.sends.go(ref, ref, self.sem(k, y, x), dev)

    def wait(self, k, y, x):
        await_recv(self.p, self.at(k, y, x), self.sem(k, y, x), self.sends.sems.at[0])

    def own(self):
        p = self.p
        for k in (2, 1, 3):
            self.go(0, p.y, p.x, p.zp(k))
        self.plane(0)

    def turn(self, k):
        return (k + self.number) % 2 == 0

    def plane(self, k):
        p = self.p
        for dev in (p.xn, p.yn) if self.turn(k) else (p.yn, p.xn):
            self.go(k, p.y, p.x, dev)

    def arrive(self, k):
        self.wait(k, self.p.y, self.p.x)
        self.plane(k)

    def forward(self, k):
        p = self.p
        if self.turn(k):
            self.wait(k, p.y, p.xo)
            self.go(k, p.y, p.xo, p.yn)
        else:
            self.wait(k, p.yo, p.x)
            self.go(k, p.yo, p.x, p.xn)

    def flow(self):
        self.forward(0)
        for k in (1, 3, 2):
            self.arrive(k)
            self.forward(k)

    def level(self, k, c):
        return self.group.at[self.p.zz(k), :, :, pl.ds(self.first, self.count), :, self.p.col(c)]

    def share(self):
        p = self.p
        for k in (0, 1, 3, 2):
            if self.turn(k):
                self.wait(k, p.yo, p.x)
            else:
                self.wait(k, p.y, p.xo)
            self.wait(k, p.yo, p.xo)
            ref = self.level(k, p.c)
            self.sends.go(ref, ref, self.sib_sem.at[p.zz(k)], p.sib)

    def finish(self):
        p = self.p
        for k in (0, 1, 3, 2):
            await_recv(p, self.level(k, 1 - p.c), self.sib_sem.at[p.zz(k)], self.sends.sems.at[0])


class GatherVectors:
    def __init__(self, place, slots, sends, rail_sem, sib_sem):
        self.p, self.slots, self.sends, self.rail_sem, self.sib_sem = place, slots, sends, rail_sem, sib_sem

    def at(self, k, y, x, c):
        return self.slots.at[self.p.zz(k), y, x, c]

    def sem(self, k, y, x):
        return self.rail_sem.at[self.p.zz(k) * 4 + y * 2 + x]

    def go(self, k, y, x, dev):
        ref = self.at(k, y, x, self.p.c)
        self.sends.go(ref, ref, self.sem(k, y, x), dev)

    def wait(self, k, y, x):
        await_recv(self.p, self.at(k, y, x, self.p.c), self.sem(k, y, x), self.sends.sems.at[0])

    def own(self):
        p = self.p
        for k in (1, 2, 3):
            self.go(0, p.y, p.x, p.zp(k))
        self.go(0, p.y, p.x, p.xn)
        self.go(0, p.y, p.x, p.yn)

    def rest(self):
        p = self.p
        for k in range(4):
            if k:
                self.wait(k, p.y, p.x)
                self.go(k, p.y, p.x, p.xn)
                self.go(k, p.y, p.x, p.yn)
        for k in range(4):
            self.wait(k, p.y, p.xo)
            self.go(k, p.y, p.xo, p.yn)
        for k in range(4):
            self.wait(k, p.yo, p.x)
            self.wait(k, p.yo, p.xo)
            ref = self.slots.at[p.zz(k), :, :, p.c]
            self.sends.go(ref, ref, self.sib_sem.at[p.zz(k)], p.sib)
        for k in range(4):
            await_recv(p, self.slots.at[p.zz(k), :, :, 1 - p.c], self.sib_sem.at[p.zz(k)], self.sends.sems.at[0])


def join_vectors(slots):
    lane = lax.broadcasted_iota(jnp.int32, (16, 128), 1)
    tiles = [jnp.zeros((16, 128), f32) for _ in range(7)]
    for d in range(32):
        tile, off = (24 * d) // 128, (24 * d) % 128
        held = slots[d // 8, (d // 4) % 2, (d // 2) % 2, d % 2]
        turned = pltpu.roll(held, off, 1) if off else held
        tiles[tile] = jnp.where((lane >= off) & (lane < off + 24), turned, tiles[tile])
        if off + 24 > 128:
            tiles[tile + 1] = jnp.where(lane < off - 104, turned, tiles[tile + 1])
    return jnp.concatenate(tiles[:6], axis=1).astype(bf).astype(f32)


class Reduce:
    def __init__(self, place, turn, grad, first, count, bufs, sends, sems):
        self.p, self.parity, self.grad, self.first, self.count = place, turn, grad, first, count
        self.cb, self.pb, self.qb, self.zb, self.final, self.swap = bufs
        self.sends, self.sems = sends, sems

    def at(self, z, y, x, c):
        return (z, y, x, pl.ds(self.first, self.count), slice(None), self.p.col(c))

    def turn(self, k):
        return (k + self.parity) % 2 == 0

    def wait(self, ref, n):
        await_recv(self.p, ref, self.sems.at[n], self.sends.sems.at[0])

    def go(self, index, dst, n, dev):
        self.sends.go(self.grad.at[index], dst, self.sems.at[n], dev)

    def add(self, index, buf, at):
        self.grad[index] = (self.grad[index].astype(f32) + buf[at].astype(f32)).astype(bf)

    def core_go(self):
        every = slice(None)
        self.go(self.at(every, every, every, 1 - self.p.c), self.cb, 0, self.p.sib)

    def core_add(self):
        self.wait(self.cb, 0)

        def body(i, _):
            z, y, x = i // 4, (i // 2) % 2, i % 2
            self.add(self.at(z, y, x, self.p.c), self.cb, (z, y, x))
            return 0
        lax.fori_loop(0, 16, body, 0)

    def first_go(self):
        p, every = self.p, slice(None)
        for k in range(4):
            if self.turn(k):
                self.go(self.at(p.zz(k), p.yo, every, p.c), self.pb.at[k], 1 + k, p.yn)
            else:
                self.go(self.at(p.zz(k), every, p.xo, p.c), self.pb.at[k], 1 + k, p.xn)

    def first_add(self):
        p = self.p
        for k in range(4):
            self.wait(self.pb.at[k], 1 + k)
            for o in (0, 1):
                y, x = (p.y, o) if self.turn(k) else (o, p.x)
                self.add(self.at(p.zz(k), y, x, p.c), self.pb, (k, o))

    def second_go(self):
        p = self.p
        for k in range(4):
            if self.turn(k):
                self.go(self.at(p.zz(k), p.y, p.xo, p.c), self.qb.at[k], 5 + k, p.xn)
            else:
                self.go(self.at(p.zz(k), p.yo, p.x, p.c), self.qb.at[k], 5 + k, p.yn)

    def second_add(self):
        p = self.p
        for k in (2, 1, 3, 0):
            self.wait(self.qb.at[k], 5 + k)
            self.add(self.at(p.zz(k), p.y, p.x, p.c), self.qb, (k,))
            if k:
                self.go(self.at(p.zz(k), p.y, p.x, p.c), self.zb.at[k - 1], 8 + k, p.zp(k))

    def line_add(self, rows_apart):
        p = self.p
        for k in (1, 2, 3):
            self.wait(self.zb.at[k - 1], 8 + k)
        total = self.grad[self.at(p.z, p.y, p.x, p.c)].astype(f32)
        for k in range(3):
            total = total + self.zb[k].astype(f32)
        self.final[...] = total
        if rows_apart:
            ref = self.final.at[:, pl.ds(pl.multiple_of((1 - p.c) * 24, 8), 24), :]
        else:
            ref = self.final.at[pl.ds((1 - p.c) * (self.count // 2), self.count // 2)]
        self.sends.go(ref, self.swap, self.sems.at[12], p.sib)
        square = total * total
        tile = jnp.sum(square.reshape(self.count * 6, 8, 384), axis=0)
        return tile[:, :128] + tile[:, 128:256] + tile[:, 256:384]


class SumAll:
    def __init__(self, place, value, buf, zbuf, sends, sems):
        self.p, self.value, self.buf, self.zbuf, self.sends, self.sems = place, value, buf, zbuf, sends, sems

    def send(self, n, dev):
        self.sends.go(self.value, self.buf.at[n], self.sems.at[n], dev)

    def hop(self, n):
        await_recv(self.p, self.buf.at[n], self.sems.at[n], self.sends.sems.at[0])
        self.sends.open.pop().wait_send()
        self.value[...] = self.value[...] + self.buf[n]

    def run(self):
        p = self.p
        for n, dev in enumerate((p.sib, p.xn, p.yn)):
            self.send(n, dev)
            self.hop(n)
        self.zbuf[p.z] = self.value[...]
        for k in (1, 2, 3):
            self.sends.go(self.value, self.zbuf.at[p.z], self.sems.at[3 + p.z], p.zp(k))
        for k in (1, 2, 3):
            await_recv(p, self.zbuf.at[p.zz(k)], self.sems.at[3 + p.zz(k)], self.sends.sems.at[0])
        return (self.zbuf[0] + self.zbuf[1]) + (self.zbuf[2] + self.zbuf[3])


def dot(a, b, ca, cb):
    return lax.dot_general(a, b, (((ca,), (cb,)), ((), ())), preferred_element_type=f32)


def unit(group, j):
    return group[:, :, :, j].reshape(768, 768)


def lanes(start, size):
    return pl.ds(pl.multiple_of(start, 128), size)


CHUNK = 32


def row_loop(count, body, init=0):
    def step(i, carry):
        return body(pl.ds(pl.multiple_of(i * CHUNK, CHUNK), CHUNK), carry)
    return lax.fori_loop(0, count // CHUNK, step, init)


def norm_stats(rows):
    centre = jnp.sum(rows, axis=-1, keepdims=True) * (1.0 / 768)
    offset = rows - centre
    spread = jnp.sum(offset * offset, axis=-1, keepdims=True) * (1.0 / 768)
    scale = lax.rsqrt(spread + norm_eps)
    return offset * scale, scale


def pad_images(images, held):
    for i in range(4):
        held[208 * i + 192 : 208 * i + 208, :] = jnp.zeros((16, 768), bf)
        held[208 * i : 208 * i + 196, :] = images[i]


def upstream_sum(pair, captions, dy, dy_low):
    for i in range(4):
        dy[208 * i + 192 : 208 * i + 208, :] = jnp.zeros((16, 768), f32)
        dy_low[208 * i + 192 : 208 * i + 208, :] = jnp.zeros((16, 768), bf)
        weights = [pair[i, c].astype(f32) for c in range(14)]

        def body(j, _, i=i, weights=weights):
            col = lanes(j * 128, 128)
            total = weights[0] * captions[0, :, col].astype(f32)
            for c in range(1, 14):
                total = total + weights[c] * captions[c, :, col].astype(f32)
            dy[208 * i : 208 * i + 196, col] = total
            dy_low[208 * i : 208 * i + 196, col] = total.astype(bf)
            return 0
        lax.fori_loop(0, 6, body, 0)


def attend(base, proj, prob, mixed):
    lane = lax.broadcasted_iota(jnp.int32, (1, 128), 1)
    masks = [jnp.where(lane < 64, score_scale, 0.0).astype(bf), jnp.where(lane < 64, 0.0, score_scale).astype(bf)]
    key = lax.broadcasted_iota(jnp.int32, (208, 256), 1)

    def body(pair, _):
        rows, wide = slice(base, base + 208), slice(base, base + 256)
        q = proj[rows, lanes(pair * 128, 128)]
        k = proj[wide, lanes(768 + pair * 128, 128)]
        v = proj[wide, lanes(1536 + pair * 128, 128)]
        parts = []
        for h in (0, 1):
            scores = dot(q * masks[h], k, 1, 1)
            scores = jnp.where(key < 196, scores, -1e30)
            weights = jnp.exp(scores - jnp.max(scores, axis=-1, keepdims=True))
            low = (weights * (1.0 / jnp.sum(weights, axis=-1, keepdims=True))).astype(bf)
            prob[rows, lanes(pair * 512 + h * 256, 256)] = low
            parts.append(dot(low, v, 1, 0))
        first = lax.broadcasted_iota(jnp.int32, (208, 128), 1) < 64
        mixed[rows, lanes(pair * 128, 128)] = jnp.where(first, parts[0], parts[1]).astype(bf)
        return 0
    lax.fori_loop(0, 6, body, 0)


def own_block(place, shard, stage, group, first, count, step, stacked):
    p = place
    low = p.c == 0
    for j in range(count):
        if stacked:
            rows = shard.shape[0] // 2
            mine = shard[(j % 2) * rows : (j % 2 + 1) * rows, p.col(p.c)]
            other = stage[(j % 2) * rows : (j % 2 + 1) * rows, :]
            block = jnp.where(p.c == j // 2, mine, other)
        else:
            mine = shard[:, lanes(p.c * step + j * 384, 384)]
            other = stage[:, j * 384 : (j + 1) * 384]
            block = jnp.concatenate([jnp.where(low, mine, other), jnp.where(low, other, mine)], axis=0)
        group[p.z, p.y, p.x, first + j, :, p.col(p.c)] = block.astype(bf)


def forward_kernel(
    images, pair, captions_hbm, qkv_in, out_in, up_in, down_in, vec_in,
    w0_hbm, w1_hbm, w2_hbm, dy_hbm, dyl_hbm, normed_hbm, proj_hbm, prob_hbm, mixed_hbm, middle_hbm, two_hbm,
    active_hbm, slope_hbm, held_hbm, out_hbm, vec_out,
    g0, g1, g2, slots, s0, s1, s2, s3, captions, dy, dyl, normed, proj, prob, mixed, middle, two, active, slope, held,
    wide, result, send_sem, stage_sem, rail_sem, sib_sem, vrail_sem, vsib_sem, local_sem,
):
    place = Place()
    place.greet()
    sends = Sends(send_sem)
    groups = (g0, g1, g2)
    shards, stages, steps = (qkv_in, out_in, up_in, down_in), (s0, s1, s2, s3), (1152, 384, 1536, 384)
    local = []

    def keep(ref, hbm):
        copy = pltpu.make_async_copy(ref, hbm, local_sem.at[len(local)])
        copy.start()
        local.append(copy)
    load = pltpu.make_async_copy(captions_hbm, captions, local_sem.at[31])
    load.start()
    slots[place.z, place.y, place.x, place.c] = jnp.zeros((16, 128), f32)
    slots[place.z, place.y, place.x, place.c, 0:12, 0:24] = vec_in[...]
    ags = [Gather(place, n, groups[CHUNKS[n][0]], sends, rail_sem, sib_sem) for n in range(4)]
    av = GatherVectors(place, slots, sends, vrail_sem, vsib_sem)
    place.meet()
    for n in range(4):
        half = stages[n].shape[1]
        sends.go(shards[n].at[:, lanes((1 - place.c) * half, half)], stages[n], stage_sem.at[n], place.sib)
    av.own()
    for n in range(4):
        await_recv(place, stages[n], stage_sem.at[n], send_sem.at[0])
        own_block(place, shards[n], stages[n], groups[CHUNKS[n][0]], CHUNKS[n][1], CHUNKS[n][2], steps[n], n == 3)
        ags[n].own()
    pad_images(images, held)
    keep(held, held_hbm)
    av.rest()
    vec_out[...] = join_vectors(slots)
    ags[0].flow()

    def first_norm(rows, _):
        h, _scale = norm_stats(held[rows, :].astype(f32))
        normed[rows, :] = (h * vec_out[0:1, :] + vec_out[1:2, :]).astype(bf)
        return 0
    row_loop(832, first_norm)
    keep(normed, normed_hbm)
    ags[1].flow()
    ags[0].share()
    ags[2].flow()
    load.wait()
    upstream_sum(pair, captions, dy, dyl)
    keep(dy, dy_hbm)
    keep(dyl, dyl_hbm)
    ags[1].share()
    ags[0].finish()
    proj[832:880, :] = jnp.zeros((48, 2304), bf)
    for j in range(3):
        value = dot(normed[...], unit(g2, j), 1, 0)
        for c in (0, 1):
            at = c * 1152 + j * 384
            part = value[:, c * 384 : (c + 1) * 384]
            if at < 768:
                part = part + vec_out[2:3, at : at + 384]
            elif at >= 1536:
                part = part + vec_out[3:4, at - 1536 : at - 1152]
            proj[0:832, at : at + 384] = part.astype(bf)
    keep(proj, proj_hbm)
    for i in range(4):
        attend(208 * i, proj, prob, mixed)
        if i == 0:
            ags[3].flow()
        if i == 1:
            ags[2].share()
        if i == 2:
            ags[3].share()
    keep(prob, prob_hbm)
    keep(mixed, mixed_hbm)
    ags[1].finish()
    keep(g2, w2_hbm)
    wide[...] = dot(mixed[...], unit(g2, 3), 1, 0)

    def second_norm(rows, _):
        value = wide[rows, :] + held[rows, :].astype(f32) + vec_out[4:5, :]
        middle[rows, :] = value
        h, _scale = norm_stats(value)
        two[rows, :] = (h * vec_out[5:6, :] + vec_out[6:7, :]).astype(bf)
        return 0
    row_loop(832, second_norm)
    keep(middle, middle_hbm)
    keep(two, two_hbm)
    ags[2].finish()
    keep(g1, w1_hbm)
    for j in range(4):
        wide[...] = dot(two[...], unit(g1, j), 1, 0)

        def bend(rows, _, j=j):
            for c in (0, 1):
                at = c * 1536 + j * 384
                u = wide[rows, c * 384 : (c + 1) * 384] + vec_out[8 + at // 768 : 9 + at // 768, at % 768 : at % 768 + 384]
                u2 = u * u
                t = jnp.tanh(u * (0.7978845608028654 + 0.035677408136300125 * u2))
                half = 0.5 * u
                active[rows, at : at + 384] = (half + half * t).astype(bf)
                slope[rows, at : at + 384] = (
                    0.5 + 0.5 * t + half * (1.0 - t * t) * (0.7978845608028654 + 0.10703222440890037 * u2)
                ).astype(bf)
            return 0
        row_loop(832, bend)
    keep(active, active_hbm)
    keep(slope, slope_hbm)
    ags[3].finish()
    keep(g0, w0_hbm)
    for n in range(3):
        wide[:, n * 256 : (n + 1) * 256] = dot(active[...], g0[:, :, :, :, :, n * 256 : (n + 1) * 256].reshape(3072, 256), 1, 0)
    for i in range(4):
        rows = slice(208 * i, 208 * i + 196)
        result[i] = wide[rows, :] + middle[rows, :] + vec_out[7:8, :]
    keep(result, out_hbm)
    sends.drain()
    for copy in local:
        copy.wait()


def forward(images, pair, captions, weights, vectors):
    dma = pltpu.SemaphoreType.DMA
    vm = pl.BlockSpec(memory_space=VMEM)
    anyspace = pl.BlockSpec(memory_space=pl.ANY)
    S = jax.ShapeDtypeStruct
    kept = [
        S((832, 768), f32), S((832, 768), bf), S((832, 768), bf), S((880, 2304), bf), S((832, 3072), bf), S((832, 768), bf),
        S((832, 768), f32), S((832, 768), bf), S((832, 3072), bf), S((832, 3072), bf), S((832, 768), bf),
    ]
    return pl.pallas_call(
        forward_kernel,
        out_shape=[S(UNIT, bf)] * 3 + kept + [S(images.shape, f32), S((16, 768), f32)],
        in_specs=[vm, pl.BlockSpec(memory_space=pltpu.SMEM), anyspace] + [vm] * 5,
        out_specs=[anyspace] * 15 + [vm],
        scratch_shapes=[VMEM(UNIT, bf)] * 3
        + [VMEM((4, 2, 2, 2, 16, 128), f32)]
        + [VMEM((w.shape[0], w.shape[1] // 2), f32) for w in weights]
        + [VMEM(captions.shape, bf)]
        + [VMEM(s.shape, s.dtype) for s in kept]
        + [VMEM((832, 768), f32), VMEM(images.shape, f32)]
        + [dma((112,)), dma((4,)), dma((4, 16)), dma((4, 4)), dma((16,)), dma((4,)), dma((32,))],
        compiler_params=pltpu.CompilerParams(collective_id=0, has_side_effects=True, vmem_limit_bytes=62 << 20),
        name="forward",
    )(images, pair, captions, *weights, vectors)


def backward_kernel(
    vec, w0_hbm, w1_hbm, w2_hbm, dy_hbm, dyl_hbm, normed_hbm, proj_hbm, prob_hbm, mixed_hbm, middle_hbm, two_hbm,
    active_hbm, slope_hbm, held_hbm,
    r_qkv, r_out, r_up, r_down, r_vec, r_norm, ig_hbm,
    x0, x1, x2, gd, b1, b2, dy, dyl, two, middle, mixed, wide, result, *scratch,
):
    bufs, scratch = [scratch[6 * n : 6 * n + 6] for n in range(4)], scratch[24:]
    vval, vbuf, vz, nval, nbuf, nz, send_sem, red_sem, vsem, nsem, local_sem = scratch
    place = Place()
    place.greet()
    sends = Sends(send_sem)
    count = [0]

    def fetch(hbm, ref):
        copy = pltpu.make_async_copy(hbm, ref, local_sem.at[count[0]])
        count[0] += 1
        copy.start()
        return copy
    get_dyl = fetch(dyl_hbm, dyl)
    get_active = fetch(active_hbm, b1)
    get_w0 = fetch(w0_hbm, x0)
    get_slope = fetch(slope_hbm, b2.at[0:832])
    get_two = fetch(two_hbm, two)
    get_w1 = fetch(w1_hbm, x1)
    get_dy = fetch(dy_hbm, dy)
    get_middle = fetch(middle_hbm, middle)
    get_mixed = fetch(mixed_hbm, mixed)
    get_w2 = fetch(w2_hbm, x2)
    reds = [
        Reduce(place, n, group, first, units, bufs[n], sends, red_sem.at[n])
        for n, (group, first, units) in enumerate(((gd, 0, 4), (x0, 0, 4), (x1, 3, 1), (x1, 0, 3)))
    ]
    ones = jnp.ones((16, 832), bf)

    def total(ref, at):
        return dot(ones, ref[0:832, at : at + 768], 1, 0)[0:1, :]
    vval[12:16, :] = jnp.zeros((4, 768), f32)
    get_dyl.wait()
    get_active.wait()
    for z in range(4):
        gd[z] = dot(b1[:, 768 * z : 768 * (z + 1)], dyl[...], 0, 0).astype(bf).reshape(2, 2, 4, 48, 768)
    get_prob = fetch(prob_hbm, b1)
    vval[7:8, :] = total(dyl, 0)
    place.meet()
    reds[0].core_go()
    get_w0.wait()
    get_slope.wait()
    for z in range(4):
        wide[...] = dot(dyl[...], x0[z].reshape(768, 768), 1, 1)

        def scale(rows, _, z=z):
            at = slice(768 * z, 768 * (z + 1))
            b2[rows, at] = (wide[rows, :] * b2[rows, at].astype(f32)).astype(bf)
            return 0
        row_loop(832, scale)
        vval[8 + z : 9 + z, :] = total(b2, 768 * z)
    reds[0].core_add()
    reds[0].first_go()
    get_two.wait()

    def columns(ref, step, j):
        return jnp.concatenate([ref[0:832, j * 384 : j * 384 + 384], ref[0:832, step + j * 384 : step + j * 384 + 384]], axis=1)
    for j in range(4):
        x0[:, :, :, j] = dot(two[...], columns(b2, 1536, j), 0, 0).astype(bf).reshape(4, 2, 2, 48, 768)
    reds[1].core_go()
    reds[0].first_add()
    reds[0].second_go()
    get_w1.wait()
    wide[...] = dot(columns(b2, 1536, 0), unit(x1, 0), 1, 1)
    for j in range(1, 4):
        wide[...] += dot(columns(b2, 1536, j), unit(x1, j), 1, 1)
    get_proj = fetch(proj_hbm, b2.at[:, 0:2304])
    get_normed = fetch(normed_hbm, b2.at[0:832, 2304:3072])
    reds[0].second_add()
    get_dy.wait()
    get_middle.wait()
    zero = jnp.zeros((8, 768), f32)

    def fold(value):
        return jnp.sum(value.reshape(CHUNK // 8, 8, 768), axis=0)

    def second_norm(rows, carry):
        grad = wide[rows, :]
        h, scale = norm_stats(middle[rows, :])
        e = grad * vec[5:6, :]
        mean = jnp.sum(e, axis=-1, keepdims=True) * (1.0 / 768)
        along = jnp.sum(e * h, axis=-1, keepdims=True) * (1.0 / 768)
        value = dy[rows, :] + scale * (e - mean - h * along)
        dy[rows, :] = value
        low = value.astype(bf)
        two[rows, :] = low
        return carry[0] + fold(grad * h), carry[1] + fold(grad), carry[2] + fold(low.astype(f32))
    sums = row_loop(832, second_norm, (zero, zero, zero))
    for row, part in zip((5, 6, 4), sums):
        vval[row : row + 1, :] = jnp.sum(part, axis=0, keepdims=True)
    reds[1].core_add()
    reds[1].first_go()
    get_mixed.wait()
    x1[:, :, :, 3] = dot(mixed[...], two[...], 0, 0).astype(bf).reshape(4, 2, 2, 48, 768)
    reds[2].core_go()
    squares = reds[0].line_add(False)
    get_w2.wait()
    dyl[...] = dot(two[...], unit(x2, 3), 1, 1).astype(bf)
    get_held = fetch(held_hbm, mixed)
    get_prob.wait()
    get_proj.wait()
    lane = lax.broadcasted_iota(jnp.int32, (1, 128), 1)
    masks = [jnp.where(lane < 64, 1.0, 0.0).astype(bf), jnp.where(lane < 64, 0.0, 1.0).astype(bf)]
    first = lax.broadcasted_iota(jnp.int32, (208, 128), 1) < 64
    for i in range(4):
        base = 208 * i

        def heads(pair, _, base=base):
            rows, deep = slice(base, base + 208), slice(base, base + 256)
            at_q, at_k, at_v = lanes(pair * 128, 128), lanes(768 + pair * 128, 128), lanes(1536 + pair * 128, 128)
            q, k, v = b2[rows, at_q], b2[deep, at_k], b2[deep, at_v]
            d = dyl[rows, at_q]
            dq, dk, dv = [], [], []
            for h in (0, 1):
                low = b1[rows, lanes(pair * 512 + h * 256, 256)]
                p = low.astype(f32)
                weighted = p * dot(d * masks[h], v, 1, 1)
                s = (weighted - p * jnp.sum(weighted, axis=-1, keepdims=True)).astype(bf)
                dq.append(dot(s, k, 1, 0))
                dk.append(dot(s, q, 0, 0)[0:208])
                dv.append(dot(low, d, 0, 0)[0:208])
            b2[rows, at_q] = (jnp.where(first, dq[0], dq[1]) * score_scale).astype(bf)
            b2[rows, at_k] = (jnp.where(first, dk[0], dk[1]) * score_scale).astype(bf)
            b2[rows, at_v] = jnp.where(first, dv[0], dv[1]).astype(bf)
            return 0
        lax.fori_loop(0, 6, heads, 0)
        if i == 0:
            reds[1].first_add()
            reds[1].second_go()
            reds[2].core_add()
            reds[2].first_go()
        if i == 2:
            reds[1].second_add()
            reds[2].first_add()
            reds[2].second_go()
    get_normed.wait()
    for j in range(3):
        x1[:, :, :, j] = dot(b2[0:832, 2304:3072], columns(b2, 1152, j), 0, 0).astype(bf).reshape(4, 2, 2, 48, 768)
    reds[3].core_go()
    reds[2].second_add()
    vval[2:3, :] = total(b2, 0)
    vval[3:4, :] = total(b2, 1536)
    wide[...] = dot(columns(b2, 1152, 0), unit(x2, 0), 1, 1)
    for j in range(1, 3):
        wide[...] += dot(columns(b2, 1152, j), unit(x2, j), 1, 1)
    reds[3].core_add()
    reds[3].first_go()
    squares = squares + reds[1].line_add(True)

    get_held.wait()

    def first_norm(rows, carry):
        grad = wide[rows, :]
        h, scale = norm_stats(mixed[rows, :].astype(f32))
        e = grad * vec[0:1, :]
        mean = jnp.sum(e, axis=-1, keepdims=True) * (1.0 / 768)
        along = jnp.sum(e * h, axis=-1, keepdims=True) * (1.0 / 768)
        dy[rows, :] = dy[rows, :] + scale * (e - mean - h * along)
        return carry[0] + fold(grad * h), carry[1] + fold(grad)
    sums = row_loop(832, first_norm, (zero, zero))
    for row, part in zip((0, 1), sums):
        vval[row : row + 1, :] = jnp.sum(part, axis=0, keepdims=True)
    for i in range(4):
        result[i] = dy[208 * i : 208 * i + 196, :]
    put = pltpu.make_async_copy(result, ig_hbm, local_sem.at[19])
    put.start()
    squares = squares + reds[2].line_add(True)
    reds[3].first_add()
    reds[3].second_go()
    vsum = SumAll(place, vval, vbuf, vz, sends, vsem).run()
    r_vec[...] = vsum
    reds[3].second_add()
    squares = squares + reds[3].line_add(True)
    nval[...] = squares
    whole = SumAll(place, nval, nbuf, nz, sends, nsem).run()
    r_norm[0, 0] = jnp.sum(whole) + jnp.sum(vsum * vsum)
    for red, out, step in ((reds[0], r_down, 0), (reds[1], r_up, 1536), (reds[2], r_out, 384), (reds[3], r_qkv, 1152)):
        red.wait(red.swap, 12)
        for j in range(red.swap.shape[0]):
            if step:
                out[:, lanes(place.c * step + j * 384, 384)] = red.final[j, pl.ds(pl.multiple_of(place.c * 24, 8), 24), :]
                out[:, lanes((1 - place.c) * step + j * 384, 384)] = red.swap[j]
            else:
                out[48 * j : 48 * (j + 1), place.col(place.c)] = red.final[place.c * 2 + j]
                out[48 * j : 48 * (j + 1), place.col(1 - place.c)] = red.swap[j]
    sends.drain()
    put.wait()


def backward(shape, vec, groups, kept, shards):
    dma = pltpu.SemaphoreType.DMA
    vm = pl.BlockSpec(memory_space=VMEM)
    anyspace = pl.BlockSpec(memory_space=pl.ANY)
    S = jax.ShapeDtypeStruct
    bufs = []
    for units, apart in ((4, False), (4, True), (1, True), (3, True)):
        block = (units, 48, 384)
        swap = (units, 24, 384) if apart else (units // 2, 48, 384)
        bufs += [
            VMEM((4, 2, 2) + block, bf), VMEM((4, 2) + block, bf), VMEM((4,) + block, bf), VMEM((3,) + block, bf),
            VMEM(block, f32), VMEM(swap, f32),
        ]
    return pl.pallas_call(
        backward_kernel,
        out_shape=[S(s, f32) for s in shards] + [S((16, 768), f32), S((1, 1), f32), S(shape, f32)],
        in_specs=[vm] + [anyspace] * 14,
        out_specs=[vm] * 5 + [pl.BlockSpec(memory_space=pltpu.SMEM), anyspace],
        scratch_shapes=[VMEM(UNIT, bf)] * 4
        + [
            VMEM((832, 3072), bf), VMEM((880, 3072), bf), VMEM((832, 768), f32), VMEM((832, 768), bf), VMEM((832, 768), bf),
            VMEM((832, 768), f32), VMEM((832, 768), bf), VMEM((832, 768), f32), VMEM(shape, f32),
        ]
        + bufs
        + [VMEM((16, 768), f32), VMEM((3, 16, 768), f32), VMEM((4, 16, 768), f32)]
        + [VMEM((8, 128), f32), VMEM((3, 8, 128), f32), VMEM((4, 8, 128), f32)]
        + [dma((80,)), dma((4, 13)), dma((7,)), dma((7,)), dma((20,))],
        compiler_params=pltpu.CompilerParams(collective_id=1, has_side_effects=True, vmem_limit_bytes=62 << 20),
        name="backward",
    )(vec, *groups, *kept)


def local_wide(
    images,
    pair_matrix,
    caption_grads,
    qkv_weight,
    out_weight,
    up_weight,
    down_weight,
    vector_rows,
    first_qkv,
    first_out,
    first_up,
    first_down,
    first_vectors,
    second_qkv,
    second_out,
    second_up,
    second_down,
    second_vectors,
):
    image_count, patches, model_width = images.shape
    row_count = image_count * patches
    head_count = model_width // HD
    qkv_low = qkv_weight.astype(jnp.bfloat16)
    out_low = out_weight.astype(jnp.bfloat16)
    up_low = up_weight.astype(jnp.bfloat16)
    down_low = down_weight.astype(jnp.bfloat16)
    vector_low = vector_rows.astype(jnp.bfloat16)
    gathered = (
        lax.all_gather(qkv_low, "dev", axis=0, tiled=True),
        lax.all_gather(out_low, "dev", axis=0, tiled=True),
        lax.all_gather(up_low, "dev", axis=0, tiled=True),
        lax.all_gather(down_low, "dev", axis=0, tiled=True),
        lax.all_gather(vector_low, "dev", axis=1, tiled=True),
    )
    result, unused_values = forward_pass(gathered, images)
    output = result.reshape(image_count, patches, model_width)
    gathered_again = (
        lax.all_gather(qkv_low, "dev", axis=0, tiled=True),
        lax.all_gather(out_low, "dev", axis=0, tiled=True),
        lax.all_gather(up_low, "dev", axis=0, tiled=True),
        lax.all_gather(down_low, "dev", axis=0, tiled=True),
        lax.all_gather(vector_low, "dev", axis=1, tiled=True),
    )
    qkv_full, out_full, up_full, down_full, vector_again = gathered_again
    vector_full = vector_again.astype(jnp.float32)
    recomputed, kept_values = forward_pass(gathered_again, images)
    (
        flat_inputs,
        normed_low,
        queries,
        keys_all,
        values_all,
        probabilities,
        prob_low,
        mixed_low,
        middle,
        normed_two_low,
        upward,
        active_low,
    ) = kept_values
    caption_flat = caption_grads.reshape(caption_grads.shape[0], patches * model_width)
    upstream = jnp.dot(
        pair_matrix.astype(jnp.bfloat16), caption_flat, preferred_element_type=jnp.float32
    ).reshape(row_count, model_width)
    down_grad_low = upstream.astype(jnp.bfloat16)
    raw_down = contract_first(active_low, down_grad_low)
    bias_down_grad = jnp.sum(down_grad_low.astype(jnp.float32), axis=0)
    active_grad = contract_last(down_grad_low, down_full)
    gelu_value, gelu_pull = jax.vjp(gelu_tanh, upward)
    upward_grad_low = gelu_pull(active_grad)[0].astype(jnp.bfloat16)
    raw_up = contract_first(normed_two_low, upward_grad_low)
    bias_up_grad = jnp.sum(upward_grad_low.astype(jnp.float32), axis=0)
    normed_two_grad = contract_last(upward_grad_low, up_full)
    second_norm_value, second_norm_pull = jax.vjp(
        layer_norm, middle, vector_full[5], vector_full[6]
    )
    middle_norm_grad, gain_two_grad, shift_two_grad = second_norm_pull(normed_two_grad)
    middle_grad = upstream + middle_norm_grad
    attended_low = middle_grad.astype(jnp.bfloat16)
    raw_out = contract_first(mixed_low, attended_low)
    bias_out_grad = jnp.sum(attended_low.astype(jnp.float32), axis=0)
    mixed_grad_low = (
        contract_last(attended_low, out_full)
        .astype(jnp.bfloat16)
        .reshape(image_count, patches, head_count, HD)
    )
    prob_grad = jnp.einsum(
        "bqhd,bkhd->bhqk", mixed_grad_low, values_all, preferred_element_type=jnp.float32
    )
    value_grad = jnp.einsum(
        "bhqk,bqhd->bkhd", prob_low, mixed_grad_low, preferred_element_type=jnp.float32
    )
    score_grad = probabilities * (
        prob_grad - jnp.sum(probabilities * prob_grad, axis=-1, keepdims=True)
    )
    score_grad_low = score_grad.astype(jnp.bfloat16)
    query_grad = (
        jnp.einsum("bhqk,bkhd->bqhd", score_grad_low, keys_all, preferred_element_type=jnp.float32)
        * score_scale
    )
    key_grad = (
        jnp.einsum("bhqk,bqhd->bkhd", score_grad_low, queries, preferred_element_type=jnp.float32)
        * score_scale
    )
    projected_grad_low = (
        jnp.stack([query_grad, key_grad, value_grad], axis=2)
        .astype(jnp.bfloat16)
        .reshape(row_count, 3 * model_width)
    )
    raw_qkv = contract_first(normed_low, projected_grad_low)
    bias_qkv_grad = jnp.sum(projected_grad_low.astype(jnp.float32), axis=0)
    normed_grad = contract_last(projected_grad_low, qkv_full)
    first_norm_value, first_norm_pull = jax.vjp(
        layer_norm, flat_inputs, vector_full[0], vector_full[1]
    )
    inputs_norm_grad, gain_one_grad, shift_one_grad = first_norm_pull(normed_grad)
    input_grads = (middle_grad + inputs_norm_grad).reshape(image_count, patches, model_width)
    small_rows = jnp.stack(
        [
            gain_one_grad,
            shift_one_grad,
            bias_qkv_grad[:model_width],
            bias_qkv_grad[2 * model_width :],
            bias_out_grad,
            gain_two_grad,
            shift_two_grad,
            bias_down_grad,
        ]
    )
    raw_vectors = jnp.concatenate([small_rows, bias_up_grad.reshape(-1, model_width)], axis=0)
    qkv_shard, out_shard, up_shard, down_shard, vector_shard = (
        lax.psum_scatter(raw_qkv, "dev", scatter_dimension=0, tiled=True),
        lax.psum_scatter(raw_out, "dev", scatter_dimension=0, tiled=True),
        lax.psum_scatter(raw_up, "dev", scatter_dimension=0, tiled=True),
        lax.psum_scatter(raw_down, "dev", scatter_dimension=0, tiled=True),
        lax.psum_scatter(raw_vectors, "dev", scatter_dimension=1, tiled=True),
    )
    local_squares = (
        jnp.sum(qkv_shard * qkv_shard)
        + jnp.sum(out_shard * out_shard)
        + jnp.sum(up_shard * up_shard)
        + jnp.sum(down_shard * down_shard)
        + jnp.sum(vector_shard * vector_shard)
    )
    grad_norm = jnp.sqrt(lax.psum(local_squares, "dev"))
    factor = clip_limit / jnp.maximum(grad_norm, clip_limit)
    qkv_parts = adam_update(
        qkv_weight, qkv_shard, first_qkv, second_qkv, factor, rate_matrix, decay_matrix
    )
    out_parts = adam_update(
        out_weight, out_shard, first_out, second_out, factor, rate_matrix, decay_matrix
    )
    up_parts = adam_update(
        up_weight, up_shard, first_up, second_up, factor, rate_matrix, decay_matrix
    )
    down_parts = adam_update(
        down_weight, down_shard, first_down, second_down, factor, rate_matrix, decay_matrix
    )
    vector_parts = adam_update(
        vector_rows, vector_shard, first_vectors, second_vectors, factor, rate_vector, 0.0
    )
    return (
        output,
        input_grads,
        grad_norm,
        qkv_parts[0],
        qkv_parts[1],
        qkv_parts[2],
        qkv_parts[3],
        out_parts[0],
        out_parts[1],
        out_parts[2],
        out_parts[3],
        up_parts[0],
        up_parts[1],
        up_parts[2],
        up_parts[3],
        down_parts[0],
        down_parts[1],
        down_parts[2],
        down_parts[3],
        vector_parts[0],
        vector_parts[1],
        vector_parts[2],
        vector_parts[3],
    )


def local_slice(
    images,
    pair_matrix,
    caption_grads,
    qkv_weight,
    out_weight,
    up_weight,
    down_weight,
    vector_rows,
    first_qkv,
    first_out,
    first_up,
    first_down,
    first_vectors,
    second_qkv,
    second_out,
    second_up,
    second_down,
    second_vectors,
):
    weights = (qkv_weight, out_weight, up_weight, down_weight)
    results = forward(images, pair_matrix, caption_grads, weights, vector_rows)
    groups, kept, output, vector_full = results[0:3], results[3:14], results[14], results[15]
    shapes = [w.shape for w in weights]
    qkv_shard, out_shard, up_shard, down_shard, vector_sum, squares, input_grads = backward(
        images.shape, vector_full, groups, kept, shapes
    )
    width = vector_rows.shape[1]
    vector_shard = lax.dynamic_slice(vector_sum, (0, lax.axis_index("dev") * width), (12, width))
    grad_norm = jnp.sqrt(squares[0, 0])
    factor = clip_limit / jnp.maximum(grad_norm, clip_limit)
    qkv_parts = adam_update(
        qkv_weight, qkv_shard, first_qkv, second_qkv, factor, rate_matrix, decay_matrix
    )
    out_parts = adam_update(
        out_weight, out_shard, first_out, second_out, factor, rate_matrix, decay_matrix
    )
    up_parts = adam_update(
        up_weight, up_shard, first_up, second_up, factor, rate_matrix, decay_matrix
    )
    down_parts = adam_update(
        down_weight, down_shard, first_down, second_down, factor, rate_matrix, decay_matrix
    )
    vector_parts = adam_update(
        vector_rows, vector_shard, first_vectors, second_vectors, factor, rate_vector, 0.0
    )
    return (
        output,
        input_grads,
        grad_norm,
        qkv_parts[0],
        qkv_parts[1],
        qkv_parts[2],
        qkv_parts[3],
        out_parts[0],
        out_parts[1],
        out_parts[2],
        out_parts[3],
        up_parts[0],
        up_parts[1],
        up_parts[2],
        up_parts[3],
        down_parts[0],
        down_parts[1],
        down_parts[2],
        down_parts[3],
        vector_parts[0],
        vector_parts[1],
        vector_parts[2],
        vector_parts[3],
    )


def solution(mesh):
    fits = mesh.shape["dev"] == 32
    return jax.shard_map(
        local_slice if fits else local_wide,
        mesh=mesh,
        in_specs=(
            P("dev", None, None),
            P("dev", None),
            P("dev", None, None),
            P("dev", None),
            P("dev", None),
            P("dev", None),
            P("dev", None),
            P(None, "dev"),
            P("dev", None),
            P("dev", None),
            P("dev", None),
            P("dev", None),
            P(None, "dev"),
            P("dev", None),
            P("dev", None),
            P("dev", None),
            P("dev", None),
            P(None, "dev"),
        ),
        out_specs=(
            P("dev", None, None),
            P("dev", None, None),
            P(),
            P("dev", None),
            P("dev", None),
            P("dev", None),
            P("dev", None),
            P("dev", None),
            P("dev", None),
            P("dev", None),
            P("dev", None),
            P("dev", None),
            P("dev", None),
            P("dev", None),
            P("dev", None),
            P("dev", None),
            P("dev", None),
            P("dev", None),
            P("dev", None),
            P(None, "dev"),
            P(None, "dev"),
            P(None, "dev"),
            P(None, "dev"),
        ),
        check_vma=False,
    )
```

```python
import functools

import jax
import jax.numpy as jnp
from jax import lax
from jax.experimental import pallas as pl
from jax.experimental.pallas import tpu as pltpu
from jax.sharding import PartitionSpec as P

HD = 64
STEP = 10


norm_eps = 1e-06
clip_limit = 1.0
beta_one = 0.9
beta_two = 0.999
adam_eps = 1e-08
rate_matrix = 0.08
rate_vector = 0.5
decay_matrix = 0.1
score_scale = 0.125


def layer_norm(values, gain_row, shift_row):
    centre = jnp.mean(values, axis=-1, keepdims=True)
    offset = values - centre
    spread = jnp.mean(offset * offset, axis=-1, keepdims=True)
    return offset * lax.rsqrt(spread + norm_eps) * gain_row + shift_row


def softmax_rows(scores):
    shifted = scores - jnp.max(scores, axis=-1, keepdims=True)
    weights = jnp.exp(shifted)
    return weights / jnp.sum(weights, axis=-1, keepdims=True)


def gelu_tanh(values):
    return jax.nn.gelu(values, approximate=True)


def contract_last(left_side, right_side):
    return lax.dot_general(
        left_side, right_side, (((1,), (1,)), ((), ())), preferred_element_type=jnp.float32
    )


def contract_first(left_side, right_side):
    return lax.dot_general(
        left_side, right_side, (((0,), (0,)), ((), ())), preferred_element_type=jnp.float32
    )


def forward_pass(gathered, inputs):
    qkv_full, out_full, up_full, down_full, vector_low = gathered
    vector_full = vector_low.astype(jnp.float32)
    image_count, patches, model_width = inputs.shape
    row_count = image_count * patches
    head_count = model_width // HD
    flat_inputs = inputs.astype(jnp.float32).reshape(row_count, model_width)
    normed_low = layer_norm(flat_inputs, vector_full[0], vector_full[1]).astype(jnp.bfloat16)
    bias_qkv = jnp.concatenate([vector_full[2], jnp.zeros_like(vector_full[2]), vector_full[3]])
    projected = jnp.dot(normed_low, qkv_full, preferred_element_type=jnp.float32) + bias_qkv
    projected_low = projected.astype(jnp.bfloat16).reshape(image_count, patches, 3, head_count, HD)
    queries = projected_low[:, :, 0]
    keys_all = projected_low[:, :, 1]
    values_all = projected_low[:, :, 2]
    scores = (
        jnp.einsum("bqhd,bkhd->bhqk", queries, keys_all, preferred_element_type=jnp.float32)
        * score_scale
    )
    probabilities = softmax_rows(scores)
    prob_low = probabilities.astype(jnp.bfloat16)
    mixed_heads = jnp.einsum(
        "bhqk,bkhd->bqhd", prob_low, values_all, preferred_element_type=jnp.float32
    )
    mixed_low = mixed_heads.reshape(row_count, model_width).astype(jnp.bfloat16)
    attended = jnp.dot(mixed_low, out_full, preferred_element_type=jnp.float32) + vector_full[4]
    middle = flat_inputs + attended
    normed_two_low = layer_norm(middle, vector_full[5], vector_full[6]).astype(jnp.bfloat16)
    upward = jnp.dot(normed_two_low, up_full, preferred_element_type=jnp.float32) + vector_full[
        8:
    ].reshape(-1)
    active_low = gelu_tanh(upward).astype(jnp.bfloat16)
    downward = jnp.dot(active_low, down_full, preferred_element_type=jnp.float32) + vector_full[7]
    result = middle + downward
    kept_values = (
        flat_inputs,
        normed_low,
        queries,
        keys_all,
        values_all,
        probabilities,
        prob_low,
        mixed_low,
        middle,
        normed_two_low,
        upward,
        active_low,
    )
    return (result, kept_values)


def adam_update(master, raw_grad, moment_one, moment_two, factor, step_rate, decay_rate):
    clipped = raw_grad * factor
    moment_one_new = beta_one * moment_one + (1.0 - beta_one) * clipped
    moment_two_new = beta_two * moment_two + (1.0 - beta_two) * clipped * clipped
    first_hat = moment_one_new / (1.0 - beta_one**STEP)
    second_hat = moment_two_new / (1.0 - beta_two**STEP)
    master_new = master - step_rate * (
        first_hat / (jnp.sqrt(second_hat) + adam_eps) + decay_rate * master
    )
    return (clipped, master_new, moment_one_new, moment_two_new)


MESH = pl.DeviceIdType.MESH
bf = jnp.bfloat16
f32 = jnp.float32
VMEM = pltpu.VMEM
ROWS = 208
UNIT = (4, 2, 2, 4, 48, 768)
CHUNKS = ((2, 0, 3, 0), (2, 3, 1, 1), (1, 0, 2, 2), (1, 2, 2, 2), (0, 0, 2, 3), (0, 2, 2, 3))


QKV_AT = ((0, 768), (1536, 384), (1152, 1920))


def column(weight, unit, c):
    if weight == 0:
        low, high = QKV_AT[unit]
        return low + c * (high - low)
    return c * (1536 if weight == 2 else 384) + (384 * unit if weight == 2 else 0)


class Place:
    def __init__(self):
        me = lax.axis_index("dev")
        self.me = me
        self.c = me % 2
        self.x = (me // 2) % 2
        self.y = (me // 4) % 2
        self.z = me // 8
        self.q = me // 2
        self.sib = me + 1 - 2 * self.c
        self.xn = me + 2 - 4 * self.x
        self.yn = me + 4 - 8 * self.y
        self.xo = 1 - self.x
        self.yo = 1 - self.y

    def zz(self, k):
        return (self.z + k) % 4

    def zp(self, k):
        return self.zz(k) * 8 + self.me % 8

    def col(self, c):
        return pl.ds(pl.multiple_of(c * 384, 128), 384)

    def greet(self):
        bar = pltpu.get_barrier_semaphore()
        for dev in (self.sib, self.xn, self.yn, self.zp(1), self.zp(2), self.zp(3)):
            pl.semaphore_signal(bar, inc=1, device_id=(dev,), device_id_type=MESH)

    def meet(self):
        pl.semaphore_wait(pltpu.get_barrier_semaphore(), 6)


class Sends:
    def __init__(self, sems):
        self.sems = sems
        self.used = 0
        self.open = []

    def go(self, src, dst, recv, dev):
        copy = pltpu.make_async_remote_copy(
            src_ref=src, dst_ref=dst, send_sem=self.sems.at[self.used], recv_sem=recv,
            device_id=(dev,), device_id_type=MESH,
        )
        self.used += 1
        copy.start()
        self.open.append(copy)

    def drain(self):
        for copy in self.open:
            copy.wait_send()
        self.open = []


def await_recv(place, ref, recv, spare):
    pltpu.make_async_remote_copy(
        src_ref=ref, dst_ref=ref, send_sem=spare, recv_sem=recv,
        device_id=(place.sib,), device_id_type=MESH,
    ).wait_recv()


class Gather:
    def __init__(self, place, chunk, group, sends, rail_sem, sib_sem):
        self.p, self.group, self.sends = place, group, sends
        self.number = chunk
        _, self.first, self.count, _ = CHUNKS[chunk]
        self.rail_sem, self.sib_sem = rail_sem.at[chunk], sib_sem.at[chunk]

    def at(self, k, y, x):
        return self.group.at[self.p.zz(k), y, x, pl.ds(self.first, self.count), :, self.p.col(self.p.c)]

    def sem(self, k, y, x):
        return self.rail_sem.at[self.p.zz(k) * 4 + y * 2 + x]

    def go(self, k, y, x, dev):
        ref = self.at(k, y, x)
        self.sends.go(ref, ref, self.sem(k, y, x), dev)

    def wait(self, k, y, x):
        await_recv(self.p, self.at(k, y, x), self.sem(k, y, x), self.sends.sems.at[0])

    def own(self):
        p = self.p
        for k in (2, 1, 3):
            self.go(0, p.y, p.x, p.zp(k))
        self.plane(0)

    def turn(self, k):
        return (k + self.number) % 2 == 0

    def plane(self, k):
        p = self.p
        for dev in (p.xn, p.yn) if self.turn(k) else (p.yn, p.xn):
            self.go(k, p.y, p.x, dev)

    def arrive(self, k):
        self.wait(k, self.p.y, self.p.x)
        self.plane(k)

    def forward(self, k):
        p = self.p
        if self.turn(k):
            self.wait(k, p.y, p.xo)
            self.go(k, p.y, p.xo, p.yn)
        else:
            self.wait(k, p.yo, p.x)
            self.go(k, p.yo, p.x, p.xn)


    def level(self, k, c):
        return self.group.at[self.p.zz(k), :, :, pl.ds(self.first, self.count), :, self.p.col(c)]

    def share(self):
        p = self.p
        for k in (0, 1, 3, 2):
            if self.turn(k):
                self.wait(k, p.yo, p.x)
            else:
                self.wait(k, p.y, p.xo)
            self.wait(k, p.yo, p.xo)
            ref = self.level(k, p.c)
            self.sends.go(ref, ref, self.sib_sem.at[p.zz(k)], p.sib)

    def finish(self):
        p = self.p
        for k in (0, 1, 3, 2):
            await_recv(p, self.level(k, 1 - p.c), self.sib_sem.at[p.zz(k)], self.sends.sems.at[0])


class GatherVectors:
    def __init__(self, place, slots, sends, rail_sem, sib_sem):
        self.p, self.slots, self.sends, self.rail_sem, self.sib_sem = place, slots, sends, rail_sem, sib_sem

    def at(self, k, y, x, c):
        return self.slots.at[self.p.zz(k), y, x, c]

    def sem(self, k, y, x):
        return self.rail_sem.at[self.p.zz(k) * 4 + y * 2 + x]

    def go(self, k, y, x, dev):
        ref = self.at(k, y, x, self.p.c)
        self.sends.go(ref, ref, self.sem(k, y, x), dev)

    def wait(self, k, y, x):
        await_recv(self.p, self.at(k, y, x, self.p.c), self.sem(k, y, x), self.sends.sems.at[0])

    def own(self):
        p = self.p
        for k in (1, 2, 3):
            self.go(0, p.y, p.x, p.zp(k))
        self.go(0, p.y, p.x, p.xn)
        self.go(0, p.y, p.x, p.yn)

    def rest(self):
        p = self.p
        for k in range(4):
            if k:
                self.wait(k, p.y, p.x)
                self.go(k, p.y, p.x, p.xn)
                self.go(k, p.y, p.x, p.yn)
        for k in range(4):
            self.wait(k, p.y, p.xo)
            self.go(k, p.y, p.xo, p.yn)
        for k in range(4):
            self.wait(k, p.yo, p.x)
            self.wait(k, p.yo, p.xo)
            ref = self.slots.at[p.zz(k), :, :, p.c]
            self.sends.go(ref, ref, self.sib_sem.at[p.zz(k)], p.sib)
        for k in range(4):
            await_recv(p, self.slots.at[p.zz(k), :, :, 1 - p.c], self.sib_sem.at[p.zz(k)], self.sends.sems.at[0])


def join_vectors(slots):
    lane = lax.broadcasted_iota(jnp.int32, (16, 128), 1)
    tiles = [jnp.zeros((16, 128), f32) for _ in range(7)]
    for d in range(32):
        tile, off = (24 * d) // 128, (24 * d) % 128
        held = slots[d // 8, (d // 4) % 2, (d // 2) % 2, d % 2]
        turned = pltpu.roll(held, off, 1) if off else held
        tiles[tile] = jnp.where((lane >= off) & (lane < off + 24), turned, tiles[tile])
        if off + 24 > 128:
            tiles[tile + 1] = jnp.where(lane < off - 104, turned, tiles[tile + 1])
    return jnp.concatenate(tiles[:6], axis=1).astype(bf).astype(f32)


class Reduce:
    def __init__(self, place, turn, grad, first, count, bufs, sends, sems):
        self.p, self.parity, self.grad, self.first, self.count = place, turn, grad, first, count
        self.cb, self.pb, self.qb, self.zb, self.final, self.swap = bufs
        self.sends, self.sems = sends, sems

    def at(self, z, y, x, c):
        return (z, y, x, pl.ds(self.first, self.count), slice(None), self.p.col(c))

    def turn(self, k):
        return (k + self.parity) % 2 == 0

    def wait(self, ref, n):
        await_recv(self.p, ref, self.sems.at[n], self.sends.sems.at[0])

    def go(self, index, dst, n, dev):
        self.sends.go(self.grad.at[index], dst, self.sems.at[n], dev)

    def add(self, index, buf, at):
        self.grad[index] = (self.grad[index].astype(f32) + buf[at].astype(f32)).astype(bf)

    def core_go(self):
        every = slice(None)
        self.go(self.at(every, every, every, 1 - self.p.c), self.cb, 0, self.p.sib)

    def core_add(self):
        self.wait(self.cb, 0)

        def body(i, _):
            z, y, x = i // 4, (i // 2) % 2, i % 2
            self.add(self.at(z, y, x, self.p.c), self.cb, (z, y, x))
            return 0
        lax.fori_loop(0, 16, body, 0)

    def first_go(self):
        p, every = self.p, slice(None)
        for k in range(4):
            if self.turn(k):
                self.go(self.at(p.zz(k), p.yo, every, p.c), self.pb.at[k], 1 + k, p.yn)
            else:
                self.go(self.at(p.zz(k), every, p.xo, p.c), self.pb.at[k], 1 + k, p.xn)

    def first_add(self):
        p = self.p
        for k in range(4):
            self.wait(self.pb.at[k], 1 + k)
            for o in (0, 1):
                y, x = (p.y, o) if self.turn(k) else (o, p.x)
                self.add(self.at(p.zz(k), y, x, p.c), self.pb, (k, o))

    def second_go(self):
        p = self.p
        for k in range(4):
            if self.turn(k):
                self.go(self.at(p.zz(k), p.y, p.xo, p.c), self.qb.at[k], 5 + k, p.xn)
            else:
                self.go(self.at(p.zz(k), p.yo, p.x, p.c), self.qb.at[k], 5 + k, p.yn)

    def second_add(self):
        p = self.p
        for k in (2, 1, 3, 0):
            self.wait(self.qb.at[k], 5 + k)
            self.add(self.at(p.zz(k), p.y, p.x, p.c), self.qb, (k,))
            if k:
                self.go(self.at(p.zz(k), p.y, p.x, p.c), self.zb.at[k - 1], 8 + k, p.zp(k))

    def line_add(self, rows_apart):
        p = self.p
        for k in (1, 2, 3):
            self.wait(self.zb.at[k - 1], 8 + k)
        total = self.grad[self.at(p.z, p.y, p.x, p.c)].astype(f32)
        for k in range(3):
            total = total + self.zb[k].astype(f32)
        self.final[...] = total
        if rows_apart:
            ref = self.final.at[:, pl.ds(pl.multiple_of((1 - p.c) * 24, 8), 24), :]
        else:
            ref = self.final.at[pl.ds((1 - p.c) * (self.count // 2), self.count // 2)]
        self.sends.go(ref, self.swap, self.sems.at[12], p.sib)
        square = total * total
        tile = jnp.sum(square.reshape(self.count * 6, 8, 384), axis=0)
        return tile[:, :128] + tile[:, 128:256] + tile[:, 256:384]


class SumAll:
    def __init__(self, place, value, buf, zbuf, sends, sems):
        self.p, self.value, self.buf, self.zbuf, self.sends, self.sems = place, value, buf, zbuf, sends, sems

    def go(self, n):
        self.sends.go(self.value, self.buf.at[n], self.sems.at[n], (self.p.sib, self.p.xn, self.p.yn)[n])
        self.copy = self.sends.open.pop()

    def add(self, n):
        await_recv(self.p, self.buf.at[n], self.sems.at[n], self.sends.sems.at[0])
        self.copy.wait_send()
        self.value[...] = self.value[...] + self.buf[n]

    def step(self, n):
        p = self.p
        if n:
            self.add(n - 1)
        if n < 3:
            self.go(n)
        else:
            self.zbuf[p.z] = self.value[...]
            for k in (2, 1, 3):
                self.sends.go(self.value, self.zbuf.at[p.z], self.sems.at[3 + p.z], p.zp(k))

    def total(self):
        p = self.p
        for k in (1, 2, 3):
            await_recv(p, self.zbuf.at[p.zz(k)], self.sems.at[3 + p.zz(k)], self.sends.sems.at[0])
        return (self.zbuf[0] + self.zbuf[1]) + (self.zbuf[2] + self.zbuf[3])


def dot(a, b, ca, cb):
    return lax.dot_general(a, b, (((ca,), (cb,)), ((), ())), preferred_element_type=f32)


def unit(group, j):
    return group[:, :, :, j].reshape(768, 768)


def lanes(start, size):
    return pl.ds(pl.multiple_of(start, 128), size)


CHUNK = 32


def row_loop(count, body, init=0):
    def step(i, carry):
        return body(pl.ds(pl.multiple_of(i * CHUNK, CHUNK), CHUNK), carry)
    return lax.fori_loop(0, count // CHUNK, step, init)


def norm_stats(rows):
    centre = jnp.sum(rows, axis=-1, keepdims=True) * (1.0 / 768)
    offset = rows - centre
    spread = jnp.sum(offset * offset, axis=-1, keepdims=True) * (1.0 / 768)
    scale = lax.rsqrt(spread + norm_eps)
    return offset * scale, scale


def pad_images(images, held):
    for i in range(4):
        held[208 * i + 192 : 208 * i + 208, :] = jnp.zeros((16, 768), bf)
        held[208 * i : 208 * i + 196, :] = images[i]


def upstream_sum(i, pair, captions, dy, dy_low):
    dy[208 * i + 192 : 208 * i + 208, :] = jnp.zeros((16, 768), f32)
    dy_low[208 * i + 192 : 208 * i + 208, :] = jnp.zeros((16, 768), bf)
    weights = [pair[i, c].astype(f32) for c in range(14)]

    def body(j, _):
        col = lanes(j * 128, 128)
        total = weights[0] * captions[0, :, col].astype(f32)
        for c in range(1, 14):
            total = total + weights[c] * captions[c, :, col].astype(f32)
        dy[208 * i : 208 * i + 196, col] = total
        dy_low[208 * i : 208 * i + 196, col] = total.astype(bf)
        return 0
    lax.fori_loop(0, 6, body, 0)


def attend(base, proj, prob, mixed):
    lane = lax.broadcasted_iota(jnp.int32, (1, 128), 1)
    masks = [jnp.where(lane < 64, score_scale, 0.0).astype(bf), jnp.where(lane < 64, 0.0, score_scale).astype(bf)]
    key = lax.broadcasted_iota(jnp.int32, (208, 256), 1)

    def body(pair, _):
        rows, wide = slice(base, base + 208), slice(base, base + 256)
        q = proj[rows, lanes(pair * 128, 128)]
        k = proj[wide, lanes(768 + pair * 128, 128)]
        v = proj[wide, lanes(1536 + pair * 128, 128)]
        parts = []
        for h in (0, 1):
            scores = dot(q * masks[h], k, 1, 1)
            scores = jnp.where(key < 196, scores, -1e30)
            weights = jnp.exp(scores - jnp.max(scores, axis=-1, keepdims=True))
            low = (weights * (1.0 / jnp.sum(weights, axis=-1, keepdims=True))).astype(bf)
            prob[rows, lanes(pair * 512 + h * 256, 256)] = low
            parts.append(dot(low, v, 1, 0))
        first = lax.broadcasted_iota(jnp.int32, (208, 128), 1) < 64
        mixed[rows, lanes(pair * 128, 128)] = jnp.where(first, parts[0], parts[1]).astype(bf)
        return 0
    lax.fori_loop(0, 6, body, 0)


def own_block(place, shard, stage, group, chunk):
    p = place
    _, first, count, weight = chunk
    low = p.c == 0
    for n in range(count):
        if weight == 3:
            rows = slice(48 * n, 48 * n + 48)
            block = jnp.where(p.c == first // 2, shard[rows, p.col(p.c)], stage[rows, :])
        else:
            j = first + n if weight != 1 else 0
            mine = shard[:, lanes(column(weight, j, p.c), 384)]
            other = stage[:, j * 384 : (j + 1) * 384]
            block = jnp.concatenate([jnp.where(low, mine, other), jnp.where(low, other, mine)], axis=0)
        group[p.z, p.y, p.x, first + n, :, p.col(p.c)] = block.astype(bf)


def forward_kernel(
    images_hbm, pair, captions_hbm, qkv_in, out_in, up_in, down_in, vec_in,
    w0_hbm, w1_hbm, w2_hbm, dy_hbm, dyl_hbm, normed_hbm, proj_hbm, prob_hbm, mixed_hbm, middle_hbm, two_hbm,
    active_hbm, slope_hbm, held_hbm, out_hbm, vec_out,
    g0, g1, g2, slots, s0, s1, s2, s3, captions, images, dy, dyl, normed, proj, prob, mixed, middle, two, active, slope, held,
    wide, result, send_sem, stage_sem, rail_sem, sib_sem, vrail_sem, vsib_sem, local_sem,
):
    place = Place()
    place.greet()
    sends = Sends(send_sem)
    groups = (g0, g1, g2)
    shards, stages = (qkv_in, out_in, up_in, down_in), (s0, s1, s2, s3)
    local = []

    def keep(ref, hbm):
        copy = pltpu.make_async_copy(ref, hbm, local_sem.at[len(local)])
        copy.start()
        local.append(copy)
    fetch = pltpu.make_async_copy(images_hbm, images, local_sem.at[30])
    load = pltpu.make_async_copy(captions_hbm, captions, local_sem.at[31])
    ags = [Gather(place, n, groups[CHUNKS[n][0]], sends, rail_sem, sib_sem) for n in range(6)]
    av = GatherVectors(place, slots, sends, vrail_sem, vsib_sem)

    def begin():
        fetch.start()
        load.start()
        slots[place.z, place.y, place.x, place.c] = jnp.zeros((16, 128), f32)
        slots[place.z, place.y, place.x, place.c, 0:12, 0:24] = vec_in[...]
        place.meet()

    def stage():
        for weight, units in enumerate((3, 1, 4, 1)):
            for j in range(units):
                sends.go(
                    shards[weight].at[:, lanes(column(weight, j, 1 - place.c), 384)],
                    stages[weight].at[:, j * 384 : (j + 1) * 384], stage_sem.at[weight, j], place.sib,
                )
        av.own()

    def own(n):
        def act():
            group, first, _, weight = CHUNKS[n]
            if n in (0, 1, 2, 4):
                for j in range(stages[weight].shape[1] // 384):
                    await_recv(place, stages[weight].at[:, j * 384 : (j + 1) * 384], stage_sem.at[weight, j], send_sem.at[0])
            own_block(place, shards[weight], stages[weight], groups[group], CHUNKS[n])
            ags[n].own()
        return act

    def arrive(n):
        def act():
            for k in (1, 3, 2):
                ags[n].arrive(k)
        return act

    def forward(n):
        def act():
            for k in (0, 1, 3, 2):
                ags[n].forward(k)
        return act

    def pad():
        fetch.wait()
        pad_images(images, held)
        keep(held, held_hbm)

    def vectors():
        vec_out[...] = join_vectors(slots)

    def first():
        def first_norm(rows, _):
            h, _scale = norm_stats(held[rows, :].astype(f32))
            normed[rows, :] = (h * vec_out[0:1, :] + vec_out[1:2, :]).astype(bf)
            return 0
        row_loop(832, first_norm)
        keep(normed, normed_hbm)

    def upstream(i):
        if i == 0:
            load.wait()
        upstream_sum(i, pair, captions, dy, dyl)
        if i == 3:
            keep(dy, dy_hbm)
            keep(dyl, dyl_hbm)

    def project(j):
        if j == 0:
            proj[832:880, :] = jnp.zeros((48, 2304), bf)
        value = dot(normed[...], unit(g2, j), 1, 0)
        for c in (0, 1):
            at = column(0, j, c)
            part = value[:, c * 384 : (c + 1) * 384]
            if at < 768:
                part = part + vec_out[2:3, at : at + 384]
            elif at >= 1536:
                part = part + vec_out[3:4, at - 1536 : at - 1152]
            proj[0:832, at : at + 384] = part.astype(bf)
        if j == 2:
            keep(proj, proj_hbm)

    def attention(i):
        attend(208 * i, proj, prob, mixed)

    def attended():
        keep(prob, prob_hbm)
        keep(mixed, mixed_hbm)
        wide[...] = dot(mixed[...], unit(g2, 3), 1, 0)

        def second_norm(rows, _):
            value = wide[rows, :] + held[rows, :].astype(f32) + vec_out[4:5, :]
            middle[rows, :] = value
            h, _scale = norm_stats(value)
            two[rows, :] = (h * vec_out[5:6, :] + vec_out[6:7, :]).astype(bf)
            return 0
        row_loop(832, second_norm)
        keep(middle, middle_hbm)
        keep(two, two_hbm)

    def up(j):
        wide[...] = dot(two[...], unit(g1, j), 1, 0)

        def bend(rows, _):
            for c in (0, 1):
                at = c * 1536 + j * 384
                u = wide[rows, c * 384 : (c + 1) * 384] + vec_out[8 + at // 768 : 9 + at // 768, at % 768 : at % 768 + 384]
                u2 = u * u
                t = jnp.tanh(u * (0.7978845608028654 + 0.035677408136300125 * u2))
                half = 0.5 * u
                active[rows, at : at + 384] = (half + half * t).astype(bf)
                slope[rows, at : at + 384] = (
                    0.5 + 0.5 * t + half * (1.0 - t * t) * (0.7978845608028654 + 0.10703222440890037 * u2)
                ).astype(bf)
            return 0
        row_loop(832, bend)
        if j == 3:
            keep(active, active_hbm)
            keep(slope, slope_hbm)

    def down():
        for n in range(3):
            wide[:, n * 256 : (n + 1) * 256] = dot(
                active[...], g0[:, :, :, :, :, n * 256 : (n + 1) * 256].reshape(3072, 256), 1, 0
            )
        for i in range(4):
            rows = slice(208 * i, 208 * i + 196)
            result[i] = wide[rows, :] + middle[rows, :] + vec_out[7:8, :]
        keep(result, out_hbm)

    def end():
        sends.drain()
        for copy in local:
            copy.wait()

    def finish(n):
        def act():
            ags[n].finish()
            if n in (1, 3, 5):
                keep((g2, g1, g0)[n // 2], (w2_hbm, w1_hbm, w0_hbm)[n // 2])
        return act

    def share(n):
        return ags[n].share
    acts = {
        "begin": begin, "stage": stage, "pad": pad, "rest": av.rest, "vectors": vectors, "first": first, "attended": attended,
        "down": down, "end": end,
    }
    for name, make, many in (
        ("own", own, 6), ("arrive", arrive, 6), ("forward", forward, 6), ("share", lambda n: ags[n].share, 6), ("finish", finish, 6),
        ("upstream", lambda n: lambda: upstream(n), 4), ("project", lambda n: lambda: project(n), 3),
        ("attention", lambda n: lambda: attention(n), 4), ("up", lambda n: lambda: up(n), 4),
    ):
        for n in range(many):
            acts[name + str(n)] = make(n)
    for name in FORWARD_STEPS:
        acts[name]()


FORWARD_STEPS = (
    "begin", "stage", "own0", "own1", "own2", "pad", "own3", "own4", "own5",
    "upstream0", "arrive0", "upstream1", "rest", "vectors", "arrive1", "forward0", "first", "arrive2", "forward1", "upstream2", "share0",
    "arrive3", "forward2", "upstream3", "finish0",
    "project0", "share1", "project1", "arrive4", "project2", "forward3", "attention0", "share2", "attention1", "arrive5",
    "attention2", "share3", "forward4", "attention3", "finish1", "attended", "forward5", "share4", "finish2",
    "up0", "up1", "share5", "finish3", "up2", "up3", "finish4", "finish5", "down", "end",
)


def forward(images, pair, captions, weights, vectors):
    dma = pltpu.SemaphoreType.DMA
    vm = pl.BlockSpec(memory_space=VMEM)
    anyspace = pl.BlockSpec(memory_space=pl.ANY)
    S = jax.ShapeDtypeStruct
    kept = [
        S((832, 768), f32), S((832, 768), bf), S((832, 768), bf), S((880, 2304), bf), S((832, 3072), bf), S((832, 768), bf),
        S((832, 768), f32), S((832, 768), bf), S((832, 3072), bf), S((832, 3072), bf), S((832, 768), bf),
    ]
    return pl.pallas_call(
        forward_kernel,
        out_shape=[S(UNIT, bf)] * 3 + kept + [S(images.shape, f32), S((16, 768), f32)],
        in_specs=[anyspace, pl.BlockSpec(memory_space=pltpu.SMEM), anyspace] + [vm] * 5,
        out_specs=[anyspace] * 15 + [vm],
        scratch_shapes=[VMEM(UNIT, bf)] * 3
        + [VMEM((4, 2, 2, 2, 16, 128), f32)]
        + [VMEM((w.shape[0], w.shape[1] // 2), f32) for w in weights]
        + [VMEM(captions.shape, bf), VMEM(images.shape, bf)]
        + [VMEM(s.shape, s.dtype) for s in kept]
        + [VMEM((832, 768), f32), VMEM(images.shape, f32)]
        + [dma((176,)), dma((4, 4)), dma((6, 16)), dma((6, 4)), dma((16,)), dma((4,)), dma((32,))],
        compiler_params=pltpu.CompilerParams(collective_id=0, has_side_effects=True, vmem_limit_bytes=62 << 20),
        name="forward",
    )(images, pair, captions, *weights, vectors)


def backward_kernel(
    vec, w0_hbm, w1_hbm, w2_hbm, dy_hbm, dyl_hbm, normed_hbm, proj_hbm, prob_hbm, mixed_hbm, middle_hbm, two_hbm,
    active_hbm, slope_hbm, held_hbm,
    r_qkv, r_out, r_up, r_down, r_vec, r_norm, ig_hbm,
    x0, x1, x2, gd, b1, b2, dy, dyl, two, middle, mixed, wide, result, *scratch,
):
    bufs, scratch = [scratch[6 * n : 6 * n + 6] for n in range(7)], scratch[42:]
    vval, vbuf, vz, nval, nbuf, nz, send_sem, red_sem, vsem, nsem, local_sem = scratch
    place = Place()
    place.greet()
    sends = Sends(send_sem)
    count = [0]

    def fetch(hbm, ref):
        copy = pltpu.make_async_copy(hbm, ref, local_sem.at[count[0]])
        count[0] += 1
        copy.start()
        return copy
    got = {}
    reds = [
        Reduce(place, n, group, first, units, bufs[n], sends, red_sem.at[n])
        for n, (group, first, units) in enumerate(
            ((gd, 0, 4), (x0, 0, 2), (x0, 2, 2), (x1, 3, 1), (x1, 0, 1), (x1, 1, 1), (x1, 2, 1))
        )
    ]
    ones = jnp.ones((16, 832), bf)

    def total(ref, at):
        return dot(ones, ref[0:832, at : at + 768], 1, 0)[0:1, :]

    def columns(weight, j):
        low, high = column(weight, j, 0), column(weight, j, 1)
        return jnp.concatenate([b2[0:832, low : low + 384], b2[0:832, high : high + 384]], axis=1)

    def begin():
        vval[12:16, :] = jnp.zeros((4, 768), f32)
        for name, hbm, ref in (
            ("dyl", dyl_hbm, dyl), ("active", active_hbm, b1), ("w0", w0_hbm, x0), ("slope", slope_hbm, b2.at[0:832]),
            ("two", two_hbm, two), ("w1", w1_hbm, x1), ("dy", dy_hbm, dy), ("middle", middle_hbm, middle),
            ("mixed", mixed_hbm, mixed), ("w2", w2_hbm, x2),
        ):
            got[name] = fetch(hbm, ref)

    def raw_down(z):
        if z == 0:
            got["dyl"].wait()
            got["active"].wait()
        gd[z] = dot(b1[:, 768 * z : 768 * (z + 1)], dyl[...], 0, 0).astype(bf).reshape(2, 2, 4, 48, 768)
        if z == 3:
            got["prob"] = fetch(prob_hbm, b1)
            vval[7:8, :] = total(dyl, 0)

    def active_grad(z):
        if z == 0:
            got["w0"].wait()
            got["slope"].wait()
        wide[...] = dot(dyl[...], x0[z].reshape(768, 768), 1, 1)

        def scale(rows, _):
            at = slice(768 * z, 768 * (z + 1))
            b2[rows, at] = (wide[rows, :] * b2[rows, at].astype(f32)).astype(bf)
            return 0
        row_loop(832, scale)
        vval[8 + z : 9 + z, :] = total(b2, 768 * z)

    def raw_up(j):
        if j == 0:
            got["two"].wait()
        x0[:, :, :, j] = dot(two[...], columns(2, j), 0, 0).astype(bf).reshape(4, 2, 2, 48, 768)

    def two_grad(j):
        if j == 0:
            got["w1"].wait()
            wide[...] = dot(columns(2, 0), unit(x1, 0), 1, 1)
        else:
            wide[...] += dot(columns(2, j), unit(x1, j), 1, 1)
        if j == 3:
            got["proj"] = fetch(proj_hbm, b2.at[:, 0:2304])
            got["normed"] = fetch(normed_hbm, b2.at[0:832, 2304:3072])
    zero = jnp.zeros((8, 768), f32)

    def fold(value):
        return jnp.sum(value.reshape(CHUNK // 8, 8, 768), axis=0)

    def second():
        got["dy"].wait()
        got["middle"].wait()

        def second_norm(rows, carry):
            grad = wide[rows, :]
            h, scale = norm_stats(middle[rows, :])
            e = grad * vec[5:6, :]
            mean = jnp.sum(e, axis=-1, keepdims=True) * (1.0 / 768)
            along = jnp.sum(e * h, axis=-1, keepdims=True) * (1.0 / 768)
            value = dy[rows, :] + scale * (e - mean - h * along)
            dy[rows, :] = value
            low = value.astype(bf)
            two[rows, :] = low
            return carry[0] + fold(grad * h), carry[1] + fold(grad), carry[2] + fold(low.astype(f32))
        sums = row_loop(832, second_norm, (zero, zero, zero))
        for row, part in zip((5, 6, 4), sums):
            vval[row : row + 1, :] = jnp.sum(part, axis=0, keepdims=True)

    def raw_out():
        got["mixed"].wait()
        x1[:, :, :, 3] = dot(mixed[...], two[...], 0, 0).astype(bf).reshape(4, 2, 2, 48, 768)
        got["held"] = fetch(held_hbm, mixed)

    def mixed_grad():
        got["w2"].wait()
        dyl[...] = dot(two[...], unit(x2, 3), 1, 1).astype(bf)
        got["prob"].wait()
        got["proj"].wait()

    def attention(half, i):
        base = 208 * i
        lane = lax.broadcasted_iota(jnp.int32, (1, 128), 1)
        masks = [jnp.where(lane < 64, 1.0, 0.0).astype(bf), jnp.where(lane < 64, 0.0, 1.0).astype(bf)]
        first = lax.broadcasted_iota(jnp.int32, (208, 128), 1) < 64

        def heads(pair, _):
            rows, deep = slice(base, base + 208), slice(base, base + 256)
            at_q, at_k, at_v = lanes(pair * 128, 128), lanes(768 + pair * 128, 128), lanes(1536 + pair * 128, 128)
            q, k, v = b2[rows, at_q], b2[deep, at_k], b2[deep, at_v]
            d = dyl[rows, at_q]
            dq, dk, dv = [], [], []
            for h in (0, 1):
                low = b1[rows, lanes(pair * 512 + h * 256, 256)]
                p = low.astype(f32)
                weighted = p * dot(d * masks[h], v, 1, 1)
                s = (weighted - p * jnp.sum(weighted, axis=-1, keepdims=True)).astype(bf)
                dq.append(dot(s, k, 1, 0))
                dk.append(dot(s, q, 0, 0)[0:208])
                dv.append(dot(low, d, 0, 0)[0:208])
            b2[rows, at_q] = (jnp.where(first, dq[0], dq[1]) * score_scale).astype(bf)
            b2[rows, at_k] = (jnp.where(first, dk[0], dk[1]) * score_scale).astype(bf)
            b2[rows, at_v] = jnp.where(first, dv[0], dv[1]).astype(bf)
            return 0
        lax.fori_loop(3 * half, 3 * half + 3, heads, 0)

    def raw_qkv(j):
        if j == 0:
            got["normed"].wait()
        x1[:, :, :, j] = dot(b2[0:832, 2304:3072], columns(0, j), 0, 0).astype(bf).reshape(4, 2, 2, 48, 768)

    def qkv_sums():
        vval[2:3, :] = total(b2, 0)
        vval[3:4, :] = total(b2, 1536)

    def normed_grad(j):
        if j == 0:
            wide[...] = dot(columns(0, 0), unit(x2, 0), 1, 1)
        else:
            wide[...] += dot(columns(0, j), unit(x2, j), 1, 1)

    def first():
        got["held"].wait()

        def first_norm(rows, carry):
            grad = wide[rows, :]
            h, scale = norm_stats(mixed[rows, :].astype(f32))
            e = grad * vec[0:1, :]
            mean = jnp.sum(e, axis=-1, keepdims=True) * (1.0 / 768)
            along = jnp.sum(e * h, axis=-1, keepdims=True) * (1.0 / 768)
            dy[rows, :] = dy[rows, :] + scale * (e - mean - h * along)
            return carry[0] + fold(grad * h), carry[1] + fold(grad)
        sums = row_loop(832, first_norm, (zero, zero))
        for row, part in zip((0, 1), sums):
            vval[row : row + 1, :] = jnp.sum(part, axis=0, keepdims=True)
        for i in range(4):
            result[i] = dy[208 * i : 208 * i + 196, :]
        got["put"] = pltpu.make_async_copy(result, ig_hbm, local_sem.at[19])
        got["put"].start()

    vsum = SumAll(place, vval, vbuf, vz, sends, vsem)
    nsum = SumAll(place, nval, nbuf, nz, sends, nsem)

    def line(n):
        got["squares"] = got.get("squares", 0.0) + reds[n].line_add(n > 0)

    def first_go(n):
        reds[n].core_add()
        reds[n].first_go()

    def second_go(n):
        reds[n].first_add()
        reds[n].second_go()

    def vectors():
        got["vsum"] = vsum.total()
        r_vec[...] = got["vsum"]

    def norm():
        nval[...] = got["squares"]
        nsum.step(0)

    def emit(n):
        red = reds[n]
        weight, unit0, out = ((3, 0, r_down), (2, 0, r_up), (2, 2, r_up), (1, 0, r_out), (0, 0, r_qkv), (0, 1, r_qkv), (0, 2, r_qkv))[n]
        red.wait(red.swap, 12)
        for j in range(red.swap.shape[0]):
            if weight == 3:
                out[48 * j : 48 * (j + 1), place.col(place.c)] = red.final[place.c * 2 + j]
                out[48 * j : 48 * (j + 1), place.col(1 - place.c)] = red.swap[j]
            else:
                mine = pl.ds(pl.multiple_of(place.c * 24, 8), 24)
                out[:, lanes(column(weight, unit0 + j, place.c), 384)] = red.final[j, mine, :]
                out[:, lanes(column(weight, unit0 + j, 1 - place.c), 384)] = red.swap[j]

    def finish():
        whole = nsum.total()
        r_norm[...] = jnp.zeros((8, 128), f32) + (jnp.sum(whole) + jnp.sum(got["vsum"] * got["vsum"]))

    def end():
        sends.drain()
        got["put"].wait()
    acts = {
        "begin": begin, "meet": place.meet, "second": second, "raw_out": raw_out, "mixed_grad": mixed_grad, "qkv_sums": qkv_sums,
        "first": first, "vectors": vectors, "norm": norm, "finish": finish, "end": end,
    }
    for name, act, many in (
        ("raw_down", raw_down, 4), ("active_grad", active_grad, 4), ("raw_up", raw_up, 4), ("two_grad", two_grad, 4),
        ("low", lambda i: attention(0, i), 4), ("high", lambda i: attention(1, i), 4), ("raw_qkv", raw_qkv, 3),
        ("normed_grad", normed_grad, 3), ("c", lambda n: reds[n].core_go(), 7), ("f", first_go, 7), ("s", second_go, 7),
        ("l", lambda n: reds[n].second_add(), 7), ("e", line, 7), ("emit", emit, 7), ("vsum", vsum.step, 4), ("nsum", nsum.step, 4),
    ):
        for n in range(many):
            acts[name + str(n)] = functools.partial(act, n)
    for name in BACKWARD_STEPS:
        acts[name]()


BACKWARD_STEPS = (
    "begin", "raw_down0", "raw_down1", "raw_down2", "raw_down3", "meet", "c0",
    "active_grad0", "active_grad1", "f0", "active_grad2", "active_grad3",
    "raw_up0", "raw_up1", "c1", "raw_up2", "raw_up3", "c2", "f1", "two_grad0", "two_grad1", "f2", "two_grad2", "two_grad3", "s0",
    "second", "s1", "l0", "raw_out", "c3", "mixed_grad", "s2", "low0", "f3", "low1", "l1", "e0", "low2", "s3", "l2", "low3",
    "raw_qkv0", "c4", "high0", "f4", "l3", "e1", "high1", "e2", "s4", "high2", "e3", "high3", "l4",
    "raw_qkv1", "c5", "raw_qkv2", "c6", "qkv_sums", "f5", "f6", "normed_grad0", "normed_grad1", "normed_grad2", "s5", "s6", "e4",
    "first", "vsum0", "l5", "l6", "vsum1", "emit0", "emit1", "vsum2", "emit2", "emit3", "emit4", "vsum3", "e5", "e6", "vectors",
    "norm", "emit5", "nsum1", "emit6", "nsum2", "nsum3", "finish", "end",
)


def backward(shape, vec, groups, kept, shards):
    dma = pltpu.SemaphoreType.DMA
    vm = pl.BlockSpec(memory_space=VMEM)
    anyspace = pl.BlockSpec(memory_space=pl.ANY)
    S = jax.ShapeDtypeStruct
    bufs = []
    for units, apart in ((4, False), (2, True), (2, True), (1, True), (1, True), (1, True), (1, True)):
        block = (units, 48, 384)
        swap = (units, 24, 384) if apart else (units // 2, 48, 384)
        bufs += [
            VMEM((4, 2, 2) + block, bf), VMEM((4, 2) + block, bf), VMEM((4,) + block, bf), VMEM((3,) + block, bf),
            VMEM(block, f32), VMEM(swap, f32),
        ]
    return pl.pallas_call(
        backward_kernel,
        out_shape=[S(s, f32) for s in shards] + [S((16, 768), f32), S((8, 128), f32), S(shape, f32)],
        in_specs=[vm] + [anyspace] * 14,
        out_specs=[vm] * 6 + [anyspace],
        scratch_shapes=[VMEM(UNIT, bf)] * 4
        + [
            VMEM((832, 3072), bf), VMEM((880, 3072), bf), VMEM((832, 768), f32), VMEM((832, 768), bf), VMEM((832, 768), bf),
            VMEM((832, 768), f32), VMEM((832, 768), bf), VMEM((832, 768), f32), VMEM(shape, f32),
        ]
        + bufs
        + [VMEM((16, 768), f32), VMEM((3, 16, 768), f32), VMEM((4, 16, 768), f32)]
        + [VMEM((8, 128), f32), VMEM((3, 8, 128), f32), VMEM((4, 8, 128), f32)]
        + [dma((128,)), dma((7, 13)), dma((7,)), dma((7,)), dma((20,))],
        compiler_params=pltpu.CompilerParams(collective_id=1, has_side_effects=True, vmem_limit_bytes=62 << 20),
        name="backward",
    )(vec, *groups, *kept)


def update_kernel(squares, vsum, *refs):
    grads, refs = refs[0:4], refs[4:]
    masters, first, second, refs = refs[0:5], refs[5:10], refs[10:15], refs[15:]
    sources, targets, refs = refs[0:2], refs[2:4], refs[4:]
    norm_out, outs, wide, sems = refs[0], refs[1:21], refs[21], refs[22]
    copies = [pltpu.make_async_copy(s, t, sems.at[n]) for n, (s, t) in enumerate(zip(sources, targets))]
    for copy in copies:
        copy.start()
    norm = jnp.sqrt(squares[0:1, 0:1])
    norm_out[...] = norm
    factor = clip_limit / jnp.maximum(norm, clip_limit)
    start = 24 * lax.axis_index("dev")
    wide[:, 0:768] = vsum[...]
    wide[:, 768:896] = jnp.zeros((16, 128), f32)
    window = wide[:, lanes((start // 128) * 128, 256)]
    shard = pltpu.roll(window, 256 - start % 128, 1)[0:12, 0:24]
    for n in range(5):
        rates = (rate_matrix, decay_matrix) if n < 4 else (rate_vector, 0.0)
        grad = grads[n][...] if n < 4 else shard
        parts = adam_update(masters[n][...], grad, first[n][...], second[n][...], factor, *rates)
        for k in range(4):
            outs[4 * n + k][...] = parts[k]
    for copy in copies:
        copy.wait()


def update(squares, vsum, grads, masters, first, second, kept):
    vm = pl.BlockSpec(memory_space=VMEM)
    anyspace = pl.BlockSpec(memory_space=pl.ANY)
    S = jax.ShapeDtypeStruct
    return pl.pallas_call(
        update_kernel,
        out_shape=[S(a.shape, f32) for a in kept] + [S((1, 1), f32)] + [S(m.shape, f32) for m in masters for _ in range(4)],
        in_specs=[vm] * 21 + [anyspace] * 2,
        out_specs=[anyspace] * 2 + [vm] * 21,
        scratch_shapes=[VMEM((16, 896), f32), pltpu.SemaphoreType.DMA((2,))],
        compiler_params=pltpu.CompilerParams(vmem_limit_bytes=40 << 20),
        name="update",
    )(squares, vsum, *grads, *masters, *first, *second, *kept)


def local_wide(
    images,
    pair_matrix,
    caption_grads,
    qkv_weight,
    out_weight,
    up_weight,
    down_weight,
    vector_rows,
    first_qkv,
    first_out,
    first_up,
    first_down,
    first_vectors,
    second_qkv,
    second_out,
    second_up,
    second_down,
    second_vectors,
):
    image_count, patches, model_width = images.shape
    row_count = image_count * patches
    head_count = model_width // HD
    qkv_low = qkv_weight.astype(jnp.bfloat16)
    out_low = out_weight.astype(jnp.bfloat16)
    up_low = up_weight.astype(jnp.bfloat16)
    down_low = down_weight.astype(jnp.bfloat16)
    vector_low = vector_rows.astype(jnp.bfloat16)
    gathered = (
        lax.all_gather(qkv_low, "dev", axis=0, tiled=True),
        lax.all_gather(out_low, "dev", axis=0, tiled=True),
        lax.all_gather(up_low, "dev", axis=0, tiled=True),
        lax.all_gather(down_low, "dev", axis=0, tiled=True),
        lax.all_gather(vector_low, "dev", axis=1, tiled=True),
    )
    result, unused_values = forward_pass(gathered, images)
    output = result.reshape(image_count, patches, model_width)
    gathered_again = (
        lax.all_gather(qkv_low, "dev", axis=0, tiled=True),
        lax.all_gather(out_low, "dev", axis=0, tiled=True),
        lax.all_gather(up_low, "dev", axis=0, tiled=True),
        lax.all_gather(down_low, "dev", axis=0, tiled=True),
        lax.all_gather(vector_low, "dev", axis=1, tiled=True),
    )
    qkv_full, out_full, up_full, down_full, vector_again = gathered_again
    vector_full = vector_again.astype(jnp.float32)
    recomputed, kept_values = forward_pass(gathered_again, images)
    (
        flat_inputs,
        normed_low,
        queries,
        keys_all,
        values_all,
        probabilities,
        prob_low,
        mixed_low,
        middle,
        normed_two_low,
        upward,
        active_low,
    ) = kept_values
    caption_flat = caption_grads.reshape(caption_grads.shape[0], patches * model_width)
    upstream = jnp.dot(
        pair_matrix.astype(jnp.bfloat16), caption_flat, preferred_element_type=jnp.float32
    ).reshape(row_count, model_width)
    down_grad_low = upstream.astype(jnp.bfloat16)
    raw_down = contract_first(active_low, down_grad_low)
    bias_down_grad = jnp.sum(down_grad_low.astype(jnp.float32), axis=0)
    active_grad = contract_last(down_grad_low, down_full)
    gelu_value, gelu_pull = jax.vjp(gelu_tanh, upward)
    upward_grad_low = gelu_pull(active_grad)[0].astype(jnp.bfloat16)
    raw_up = contract_first(normed_two_low, upward_grad_low)
    bias_up_grad = jnp.sum(upward_grad_low.astype(jnp.float32), axis=0)
    normed_two_grad = contract_last(upward_grad_low, up_full)
    second_norm_value, second_norm_pull = jax.vjp(
        layer_norm, middle, vector_full[5], vector_full[6]
    )
    middle_norm_grad, gain_two_grad, shift_two_grad = second_norm_pull(normed_two_grad)
    middle_grad = upstream + middle_norm_grad
    attended_low = middle_grad.astype(jnp.bfloat16)
    raw_out = contract_first(mixed_low, attended_low)
    bias_out_grad = jnp.sum(attended_low.astype(jnp.float32), axis=0)
    mixed_grad_low = (
        contract_last(attended_low, out_full)
        .astype(jnp.bfloat16)
        .reshape(image_count, patches, head_count, HD)
    )
    prob_grad = jnp.einsum(
        "bqhd,bkhd->bhqk", mixed_grad_low, values_all, preferred_element_type=jnp.float32
    )
    value_grad = jnp.einsum(
        "bhqk,bqhd->bkhd", prob_low, mixed_grad_low, preferred_element_type=jnp.float32
    )
    score_grad = probabilities * (
        prob_grad - jnp.sum(probabilities * prob_grad, axis=-1, keepdims=True)
    )
    score_grad_low = score_grad.astype(jnp.bfloat16)
    query_grad = (
        jnp.einsum("bhqk,bkhd->bqhd", score_grad_low, keys_all, preferred_element_type=jnp.float32)
        * score_scale
    )
    key_grad = (
        jnp.einsum("bhqk,bqhd->bkhd", score_grad_low, queries, preferred_element_type=jnp.float32)
        * score_scale
    )
    projected_grad_low = (
        jnp.stack([query_grad, key_grad, value_grad], axis=2)
        .astype(jnp.bfloat16)
        .reshape(row_count, 3 * model_width)
    )
    raw_qkv = contract_first(normed_low, projected_grad_low)
    bias_qkv_grad = jnp.sum(projected_grad_low.astype(jnp.float32), axis=0)
    normed_grad = contract_last(projected_grad_low, qkv_full)
    first_norm_value, first_norm_pull = jax.vjp(
        layer_norm, flat_inputs, vector_full[0], vector_full[1]
    )
    inputs_norm_grad, gain_one_grad, shift_one_grad = first_norm_pull(normed_grad)
    input_grads = (middle_grad + inputs_norm_grad).reshape(image_count, patches, model_width)
    small_rows = jnp.stack(
        [
            gain_one_grad,
            shift_one_grad,
            bias_qkv_grad[:model_width],
            bias_qkv_grad[2 * model_width :],
            bias_out_grad,
            gain_two_grad,
            shift_two_grad,
            bias_down_grad,
        ]
    )
    raw_vectors = jnp.concatenate([small_rows, bias_up_grad.reshape(-1, model_width)], axis=0)
    qkv_shard, out_shard, up_shard, down_shard, vector_shard = (
        lax.psum_scatter(raw_qkv, "dev", scatter_dimension=0, tiled=True),
        lax.psum_scatter(raw_out, "dev", scatter_dimension=0, tiled=True),
        lax.psum_scatter(raw_up, "dev", scatter_dimension=0, tiled=True),
        lax.psum_scatter(raw_down, "dev", scatter_dimension=0, tiled=True),
        lax.psum_scatter(raw_vectors, "dev", scatter_dimension=1, tiled=True),
    )
    local_squares = (
        jnp.sum(qkv_shard * qkv_shard)
        + jnp.sum(out_shard * out_shard)
        + jnp.sum(up_shard * up_shard)
        + jnp.sum(down_shard * down_shard)
        + jnp.sum(vector_shard * vector_shard)
    )
    grad_norm = jnp.sqrt(lax.psum(local_squares, "dev"))
    factor = clip_limit / jnp.maximum(grad_norm, clip_limit)
    qkv_parts = adam_update(
        qkv_weight, qkv_shard, first_qkv, second_qkv, factor, rate_matrix, decay_matrix
    )
    out_parts = adam_update(
        out_weight, out_shard, first_out, second_out, factor, rate_matrix, decay_matrix
    )
    up_parts = adam_update(
        up_weight, up_shard, first_up, second_up, factor, rate_matrix, decay_matrix
    )
    down_parts = adam_update(
        down_weight, down_shard, first_down, second_down, factor, rate_matrix, decay_matrix
    )
    vector_parts = adam_update(
        vector_rows, vector_shard, first_vectors, second_vectors, factor, rate_vector, 0.0
    )
    return (
        output,
        input_grads,
        grad_norm,
        qkv_parts[0],
        qkv_parts[1],
        qkv_parts[2],
        qkv_parts[3],
        out_parts[0],
        out_parts[1],
        out_parts[2],
        out_parts[3],
        up_parts[0],
        up_parts[1],
        up_parts[2],
        up_parts[3],
        down_parts[0],
        down_parts[1],
        down_parts[2],
        down_parts[3],
        vector_parts[0],
        vector_parts[1],
        vector_parts[2],
        vector_parts[3],
    )


def local_slice(
    images,
    pair_matrix,
    caption_grads,
    qkv_weight,
    out_weight,
    up_weight,
    down_weight,
    vector_rows,
    first_qkv,
    first_out,
    first_up,
    first_down,
    first_vectors,
    second_qkv,
    second_out,
    second_up,
    second_down,
    second_vectors,
):
    weights = (qkv_weight, out_weight, up_weight, down_weight)
    results = forward(images, pair_matrix, caption_grads, weights, vector_rows)
    groups, kept, output, vector_full = results[0:3], results[3:14], results[14], results[15]
    shapes = [w.shape for w in weights]
    qkv_shard, out_shard, up_shard, down_shard, vector_sum, squares, input_grads = backward(
        images.shape, vector_full, groups, kept, shapes
    )
    masters = (*weights, vector_rows)
    first = (first_qkv, first_out, first_up, first_down, first_vectors)
    second = (second_qkv, second_out, second_up, second_down, second_vectors)
    shards = (qkv_shard, out_shard, up_shard, down_shard)
    output, input_grads, norm, *parts = update(squares, vector_sum, shards, masters, first, second, (output, input_grads))
    return (output, input_grads, norm[0, 0], *parts)


def solution(mesh):
    fits = mesh.shape["dev"] == 32
    return jax.shard_map(
        local_slice if fits else local_wide,
        mesh=mesh,
        in_specs=(
            P("dev", None, None),
            P("dev", None),
            P("dev", None, None),
            P("dev", None),
            P("dev", None),
            P("dev", None),
            P("dev", None),
            P(None, "dev"),
            P("dev", None),
            P("dev", None),
            P("dev", None),
            P("dev", None),
            P(None, "dev"),
            P("dev", None),
            P("dev", None),
            P("dev", None),
            P("dev", None),
            P(None, "dev"),
        ),
        out_specs=(
            P("dev", None, None),
            P("dev", None, None),
            P(),
            P("dev", None),
            P("dev", None),
            P("dev", None),
            P("dev", None),
            P("dev", None),
            P("dev", None),
            P("dev", None),
            P("dev", None),
            P("dev", None),
            P("dev", None),
            P("dev", None),
            P("dev", None),
            P("dev", None),
            P("dev", None),
            P("dev", None),
            P("dev", None),
            P(None, "dev"),
            P(None, "dev"),
            P(None, "dev"),
            P(None, "dev"),
        ),
        check_vma=False,
    )
```

```python
import functools

import jax
import jax.numpy as jnp
from jax import lax
from jax.experimental import pallas as pl
from jax.experimental.pallas import tpu as pltpu
from jax.sharding import PartitionSpec as P

HD = 64
STEP = 10


norm_eps = 1e-06
clip_limit = 1.0
beta_one = 0.9
beta_two = 0.999
adam_eps = 1e-08
rate_matrix = 0.08
rate_vector = 0.5
decay_matrix = 0.1
score_scale = 0.125


def layer_norm(values, gain_row, shift_row):
    centre = jnp.mean(values, axis=-1, keepdims=True)
    offset = values - centre
    spread = jnp.mean(offset * offset, axis=-1, keepdims=True)
    return offset * lax.rsqrt(spread + norm_eps) * gain_row + shift_row


def softmax_rows(scores):
    shifted = scores - jnp.max(scores, axis=-1, keepdims=True)
    weights = jnp.exp(shifted)
    return weights / jnp.sum(weights, axis=-1, keepdims=True)


def gelu_tanh(values):
    return jax.nn.gelu(values, approximate=True)


def contract_last(left_side, right_side):
    return lax.dot_general(
        left_side, right_side, (((1,), (1,)), ((), ())), preferred_element_type=jnp.float32
    )


def contract_first(left_side, right_side):
    return lax.dot_general(
        left_side, right_side, (((0,), (0,)), ((), ())), preferred_element_type=jnp.float32
    )


def forward_pass(gathered, inputs):
    qkv_full, out_full, up_full, down_full, vector_low = gathered
    vector_full = vector_low.astype(jnp.float32)
    image_count, patches, model_width = inputs.shape
    row_count = image_count * patches
    head_count = model_width // HD
    flat_inputs = inputs.astype(jnp.float32).reshape(row_count, model_width)
    normed_low = layer_norm(flat_inputs, vector_full[0], vector_full[1]).astype(jnp.bfloat16)
    bias_qkv = jnp.concatenate([vector_full[2], jnp.zeros_like(vector_full[2]), vector_full[3]])
    projected = jnp.dot(normed_low, qkv_full, preferred_element_type=jnp.float32) + bias_qkv
    projected_low = projected.astype(jnp.bfloat16).reshape(image_count, patches, 3, head_count, HD)
    queries = projected_low[:, :, 0]
    keys_all = projected_low[:, :, 1]
    values_all = projected_low[:, :, 2]
    scores = (
        jnp.einsum("bqhd,bkhd->bhqk", queries, keys_all, preferred_element_type=jnp.float32)
        * score_scale
    )
    probabilities = softmax_rows(scores)
    prob_low = probabilities.astype(jnp.bfloat16)
    mixed_heads = jnp.einsum(
        "bhqk,bkhd->bqhd", prob_low, values_all, preferred_element_type=jnp.float32
    )
    mixed_low = mixed_heads.reshape(row_count, model_width).astype(jnp.bfloat16)
    attended = jnp.dot(mixed_low, out_full, preferred_element_type=jnp.float32) + vector_full[4]
    middle = flat_inputs + attended
    normed_two_low = layer_norm(middle, vector_full[5], vector_full[6]).astype(jnp.bfloat16)
    upward = jnp.dot(normed_two_low, up_full, preferred_element_type=jnp.float32) + vector_full[
        8:
    ].reshape(-1)
    active_low = gelu_tanh(upward).astype(jnp.bfloat16)
    downward = jnp.dot(active_low, down_full, preferred_element_type=jnp.float32) + vector_full[7]
    result = middle + downward
    kept_values = (
        flat_inputs,
        normed_low,
        queries,
        keys_all,
        values_all,
        probabilities,
        prob_low,
        mixed_low,
        middle,
        normed_two_low,
        upward,
        active_low,
    )
    return (result, kept_values)


def adam_update(master, raw_grad, moment_one, moment_two, factor, step_rate, decay_rate):
    clipped = raw_grad * factor
    moment_one_new = beta_one * moment_one + (1.0 - beta_one) * clipped
    moment_two_new = beta_two * moment_two + (1.0 - beta_two) * clipped * clipped
    first_hat = moment_one_new / (1.0 - beta_one**STEP)
    second_hat = moment_two_new / (1.0 - beta_two**STEP)
    master_new = master - step_rate * (
        first_hat / (jnp.sqrt(second_hat) + adam_eps) + decay_rate * master
    )
    return (clipped, master_new, moment_one_new, moment_two_new)


MESH = pl.DeviceIdType.MESH
bf = jnp.bfloat16
f32 = jnp.float32
VMEM = pltpu.VMEM
ROWS = 208
UNIT = (4, 2, 2, 4, 48, 768)
CHUNKS = ((2, 0, 3, 0), (2, 3, 1, 1), (1, 0, 2, 2), (1, 2, 2, 2), (0, 0, 2, 3), (0, 2, 2, 3))


QKV_AT = ((0, 768), (1536, 384), (1152, 1920))


def column(weight, unit, c):
    if weight == 0:
        low, high = QKV_AT[unit]
        return low + c * (high - low)
    return c * (1536 if weight == 2 else 384) + (384 * unit if weight == 2 else 0)


class Place:
    def __init__(self):
        me = lax.axis_index("dev")
        self.me = me
        self.c = me % 2
        self.x = (me // 2) % 2
        self.y = (me // 4) % 2
        self.z = me // 8
        self.q = me // 2
        self.sib = me + 1 - 2 * self.c
        self.xn = me + 2 - 4 * self.x
        self.yn = me + 4 - 8 * self.y
        self.xo = 1 - self.x
        self.yo = 1 - self.y

    def zz(self, k):
        return (self.z + k) % 4

    def zp(self, k):
        return self.zz(k) * 8 + self.me % 8

    def col(self, c):
        return pl.ds(pl.multiple_of(c * 384, 128), 384)

    def greet(self):
        bar = pltpu.get_barrier_semaphore()
        for dev in [self.near(n) for n in range(1, 8)] + [self.zp(1), self.zp(2), self.zp(3)]:
            pl.semaphore_signal(bar, inc=1, device_id=(dev,), device_id_type=MESH)

    def near(self, n):
        return self.z * 8 + (self.me + n) % 8

    def meet(self):
        pl.semaphore_wait(pltpu.get_barrier_semaphore(), 10)


class Sends:
    def __init__(self, sems):
        self.sems = sems
        self.used = 0
        self.open = []

    def go(self, src, dst, recv, dev):
        copy = pltpu.make_async_remote_copy(
            src_ref=src, dst_ref=dst, send_sem=self.sems.at[self.used], recv_sem=recv,
            device_id=(dev,), device_id_type=MESH,
        )
        self.used += 1
        copy.start()
        self.open.append(copy)

    def drain(self):
        for copy in self.open:
            copy.wait_send()
        self.open = []


def await_recv(place, ref, recv, spare):
    pltpu.make_async_remote_copy(
        src_ref=ref, dst_ref=ref, send_sem=spare, recv_sem=recv,
        device_id=(place.sib,), device_id_type=MESH,
    ).wait_recv()


class Gather:
    def __init__(self, place, chunk, group, sends, rail_sem, sib_sem):
        self.p, self.group, self.sends = place, group, sends
        self.number = chunk
        _, self.first, self.count, _ = CHUNKS[chunk]
        self.rail_sem, self.sib_sem = rail_sem.at[chunk], sib_sem.at[chunk]

    def at(self, k, y, x):
        return self.group.at[self.p.zz(k), y, x, pl.ds(self.first, self.count), :, self.p.col(self.p.c)]

    def sem(self, k, y, x):
        return self.rail_sem.at[self.p.zz(k) * 4 + y * 2 + x]

    def go(self, k, y, x, dev):
        ref = self.at(k, y, x)
        self.sends.go(ref, ref, self.sem(k, y, x), dev)

    def wait(self, k, y, x):
        await_recv(self.p, self.at(k, y, x), self.sem(k, y, x), self.sends.sems.at[0])

    def own(self):
        p = self.p
        for k in (2, 1, 3):
            self.go(0, p.y, p.x, p.zp(k))
        self.plane(0)

    def turn(self, k):
        return (k + self.number) % 2 == 0

    def plane(self, k):
        p = self.p
        for dev in (p.xn, p.yn) if self.turn(k) else (p.yn, p.xn):
            self.go(k, p.y, p.x, dev)

    def arrive(self, k):
        self.wait(k, self.p.y, self.p.x)
        self.plane(k)

    def forward(self, k):
        p = self.p
        if self.turn(k):
            self.wait(k, p.y, p.xo)
            self.go(k, p.y, p.xo, p.yn)
        else:
            self.wait(k, p.yo, p.x)
            self.go(k, p.yo, p.x, p.xn)


    def level(self, k, c):
        return self.group.at[self.p.zz(k), :, :, pl.ds(self.first, self.count), :, self.p.col(c)]

    def share(self):
        p = self.p
        for k in (0, 1, 3, 2):
            if self.turn(k):
                self.wait(k, p.yo, p.x)
            else:
                self.wait(k, p.y, p.xo)
            self.wait(k, p.yo, p.xo)
            ref = self.level(k, p.c)
            self.sends.go(ref, ref, self.sib_sem.at[p.zz(k)], p.sib)

    def finish(self):
        p = self.p
        for k in (0, 1, 3, 2):
            await_recv(p, self.level(k, 1 - p.c), self.sib_sem.at[p.zz(k)], self.sends.sems.at[0])


class GatherVectors:
    def __init__(self, place, slots, sends, rail_sem, sib_sem):
        self.p, self.slots, self.sends, self.rail_sem, self.sib_sem = place, slots, sends, rail_sem, sib_sem

    def at(self, k, y, x, c):
        return self.slots.at[self.p.zz(k), y, x, c]

    def sem(self, k, y, x):
        return self.rail_sem.at[self.p.zz(k) * 4 + y * 2 + x]

    def go(self, k, y, x, dev):
        ref = self.at(k, y, x, self.p.c)
        self.sends.go(ref, ref, self.sem(k, y, x), dev)

    def wait(self, k, y, x):
        await_recv(self.p, self.at(k, y, x, self.p.c), self.sem(k, y, x), self.sends.sems.at[0])

    def own(self):
        p = self.p
        for k in (1, 2, 3):
            self.go(0, p.y, p.x, p.zp(k))
        self.go(0, p.y, p.x, p.xn)
        self.go(0, p.y, p.x, p.yn)

    def rest(self):
        p = self.p
        for k in range(4):
            if k:
                self.wait(k, p.y, p.x)
                self.go(k, p.y, p.x, p.xn)
                self.go(k, p.y, p.x, p.yn)
        for k in range(4):
            self.wait(k, p.y, p.xo)
            self.go(k, p.y, p.xo, p.yn)
        for k in range(4):
            self.wait(k, p.yo, p.x)
            self.wait(k, p.yo, p.xo)
            ref = self.slots.at[p.zz(k), :, :, p.c]
            self.sends.go(ref, ref, self.sib_sem.at[p.zz(k)], p.sib)
        for k in range(4):
            await_recv(p, self.slots.at[p.zz(k), :, :, 1 - p.c], self.sib_sem.at[p.zz(k)], self.sends.sems.at[0])


def join_vectors(slots):
    lane = lax.broadcasted_iota(jnp.int32, (16, 128), 1)
    tiles = [jnp.zeros((16, 128), f32) for _ in range(7)]
    for d in range(32):
        tile, off = (24 * d) // 128, (24 * d) % 128
        held = slots[d // 8, (d // 4) % 2, (d // 2) % 2, d % 2]
        turned = pltpu.roll(held, off, 1) if off else held
        tiles[tile] = jnp.where((lane >= off) & (lane < off + 24), turned, tiles[tile])
        if off + 24 > 128:
            tiles[tile + 1] = jnp.where(lane < off - 104, turned, tiles[tile + 1])
    return jnp.concatenate(tiles[:6], axis=1).astype(bf).astype(f32)


ORDER = (2, 1, 3, 0)


class Reduce:
    def __init__(self, place, turn, grad, first, count, bufs, sends, sems):
        self.p, self.parity, self.grad, self.first, self.count = place, turn, grad, first, count
        self.cb, self.pb, self.qb, self.zb, self.final, self.swap = bufs
        self.sends, self.sems = sends, sems

    def at(self, z, y, x, c):
        return (z, y, x, pl.ds(self.first, self.count), slice(None), self.p.col(c))

    def turn(self, k):
        return (k + self.parity) % 2 == 0

    def wait(self, ref, n):
        await_recv(self.p, ref, self.sems.at[n], self.sends.sems.at[0])

    def go(self, index, dst, n, dev):
        self.sends.go(self.grad.at[index], dst, self.sems.at[n], dev)

    def add(self, index, buf, at):
        self.grad[index] = self.grad[index] + buf[at]

    def core_go(self, *ks):
        every = slice(None)
        for k in ks or ORDER:
            self.go(self.at(self.p.zz(k), every, every, 1 - self.p.c), self.cb.at[k], k, self.p.sib)

    def first_go(self, *ks):
        p, every = self.p, slice(None)
        for k in ks or ORDER:
            self.wait(self.cb.at[k], k)
            z = p.zz(k)

            def body(i, _, k=k, z=z):
                self.add(self.at(z, i // 2, i % 2, p.c), self.cb, (k, i // 2, i % 2))
                return 0
            lax.fori_loop(0, 4, body, 0)
            if self.turn(k):
                self.go(self.at(z, p.yo, every, p.c), self.pb.at[k], 4 + k, p.yn)
            else:
                self.go(self.at(z, every, p.xo, p.c), self.pb.at[k], 4 + k, p.xn)

    def second_go(self, *ks):
        p = self.p
        for k in ks or ORDER:
            self.wait(self.pb.at[k], 4 + k)
            z = p.zz(k)
            for o in (0, 1):
                y, x = (p.y, o) if self.turn(k) else (o, p.x)
                self.add(self.at(z, y, x, p.c), self.pb, (k, o))
            if self.turn(k):
                self.go(self.at(z, p.y, p.xo, p.c), self.qb.at[k], 8 + k, p.xn)
            else:
                self.go(self.at(z, p.yo, p.x, p.c), self.qb.at[k], 8 + k, p.yn)

    def line_go(self):
        p = self.p
        for k in ORDER:
            self.wait(self.qb.at[k], 8 + k)
            self.add(self.at(p.zz(k), p.y, p.x, p.c), self.qb, (k,))
            if k:
                self.go(self.at(p.zz(k), p.y, p.x, p.c), self.zb.at[k - 1], 11 + k, p.zp(k))

    def line_add(self, rows_apart):
        p = self.p
        for k in (1, 2, 3):
            self.wait(self.zb.at[k - 1], 11 + k)
        total = self.grad[self.at(p.z, p.y, p.x, p.c)].astype(f32)
        for k in range(3):
            total = total + self.zb[k].astype(f32)
        self.final[...] = total
        if rows_apart:
            ref = self.final.at[:, pl.ds(pl.multiple_of((1 - p.c) * 24, 8), 24), :]
        else:
            ref = self.final.at[pl.ds((1 - p.c) * (self.count // 2), self.count // 2)]
        self.sends.go(ref, self.swap, self.sems.at[15], p.sib)
        square = total * total
        tile = jnp.sum(square.reshape(self.count * 6, 8, 384), axis=0)
        return tile[:, :128] + tile[:, 128:256] + tile[:, 256:384]


class SumAll:
    def __init__(self, place, value, buf, zbuf, sends, sems):
        self.p, self.value, self.buf, self.zbuf, self.sends, self.sems = place, value, buf, zbuf, sends, sems

    def go(self, n):
        self.sends.go(self.value, self.buf.at[n], self.sems.at[n], (self.p.sib, self.p.xn, self.p.yn)[n])
        self.copy = self.sends.open.pop()

    def add(self, n):
        await_recv(self.p, self.buf.at[n], self.sems.at[n], self.sends.sems.at[0])
        self.copy.wait_send()
        self.value[...] = self.value[...] + self.buf[n]

    def step(self, n):
        p = self.p
        if n:
            self.add(n - 1)
        if n < 3:
            self.go(n)
        else:
            self.zbuf[p.z] = self.value[...]
            for k in (2, 1, 3):
                self.sends.go(self.value, self.zbuf.at[p.z], self.sems.at[3 + p.z], p.zp(k))

    def total(self):
        p = self.p
        for k in (1, 2, 3):
            await_recv(p, self.zbuf.at[p.zz(k)], self.sems.at[3 + p.zz(k)], self.sends.sems.at[0])
        return (self.zbuf[0] + self.zbuf[1]) + (self.zbuf[2] + self.zbuf[3])


class SumFew:
    def __init__(self, place, buf, zbuf, sends, sems):
        self.p, self.buf, self.zbuf, self.sends, self.sems = place, buf, zbuf, sends, sems

    def start(self, value):
        p = self.p
        mine = p.me % 8
        self.buf[mine] = value
        for n in range(1, 8):
            self.sends.go(self.buf.at[mine], self.buf.at[mine], self.sems.at[mine], p.near(n))

    def turn(self):
        p = self.p
        for n in range(1, 8):
            slot = (p.me + n) % 8
            await_recv(p, self.buf.at[slot], self.sems.at[slot], self.sends.sems.at[0])
        self.zbuf[p.z] = jnp.sum(self.buf[...], axis=0)
        for k in (2, 1, 3):
            self.sends.go(self.zbuf.at[p.z], self.zbuf.at[p.z], self.sems.at[8 + p.z], p.zp(k))

    def total(self):
        p = self.p
        for k in (1, 2, 3):
            await_recv(p, self.zbuf.at[p.zz(k)], self.sems.at[8 + p.zz(k)], self.sends.sems.at[0])
        return (self.zbuf[0] + self.zbuf[1]) + (self.zbuf[2] + self.zbuf[3])


def dot(a, b, ca, cb):
    return lax.dot_general(a, b, (((ca,), (cb,)), ((), ())), preferred_element_type=f32)


def unit(group, j):
    return group[:, :, :, j].reshape(768, 768)


def lanes(start, size):
    return pl.ds(pl.multiple_of(start, 128), size)


CHUNK = 32


def row_loop(count, body, init=0, unroll=2):
    def step(i, carry):
        return body(pl.ds(pl.multiple_of(i * CHUNK, CHUNK), CHUNK), carry)
    return lax.fori_loop(0, count // CHUNK, step, init, unroll=unroll)


def norm_stats(rows):
    centre = jnp.sum(rows, axis=-1, keepdims=True) * (1.0 / 768)
    offset = rows - centre
    spread = jnp.sum(offset * offset, axis=-1, keepdims=True) * (1.0 / 768)
    scale = lax.rsqrt(spread + norm_eps)
    return offset * scale, centre, scale


def keep_stats(stats, rows, centre, scale):
    stats[rows, 0:128] = jnp.broadcast_to(centre, (CHUNK, 128))
    stats[rows, 128:256] = jnp.broadcast_to(scale, (CHUNK, 128))


def normalized(values, stats, rows):
    scale = stats[rows, 128:129]
    return (values - stats[rows, 0:1]) * scale, scale


def pad_images(images, held):
    for i in range(4):
        held[208 * i + 192 : 208 * i + 208, :] = jnp.zeros((16, 768), bf)
        held[208 * i : 208 * i + 196, :] = images[:, i, :]


def upstream_sum(i, pair, captions, dy, dy_low):
    dy[208 * i + 192 : 208 * i + 208, :] = jnp.zeros((16, 768), f32)
    dy_low[208 * i + 192 : 208 * i + 208, :] = jnp.zeros((16, 768), bf)
    weights = [pair[i, c].astype(f32) for c in range(14)]

    def body(j, _):
        col = lanes(j * 128, 128)
        total = weights[0] * captions[0, :, col].astype(f32)
        for c in range(1, 14):
            total = total + weights[c] * captions[c, :, col].astype(f32)
        dy[208 * i : 208 * i + 196, col] = total
        dy_low[208 * i : 208 * i + 196, col] = total.astype(bf)
        return 0
    lax.fori_loop(0, 6, body, 0)


def head_masks(value):
    lane = lax.broadcasted_iota(jnp.int32, (1, 128), 1)
    return jnp.where(lane < 64, value, 0.0).astype(bf), jnp.where(lane < 64, 0.0, value).astype(bf)


def both_heads(rows, value=1.0):
    first, second = head_masks(value)
    return jnp.concatenate([rows * first, rows * second], axis=0)


def attend(base, proj, prob, mixed):
    valid = lax.broadcasted_iota(jnp.int32, (208, 128), 1) < 68

    def body(pair, _):
        rows, wide = pl.ds(base, 208), pl.ds(base, 256)
        q = proj[rows, lanes(pair * 128, 128)]
        k = both_heads(proj[wide, lanes(768 + pair * 128, 128)], score_scale)
        v = both_heads(proj[wide, lanes(1536 + pair * 128, 128)])
        scores = dot(q, k, 1, 1)
        lows = []
        for h in (0, 1):
            near = scores[:, h * 256 : h * 256 + 128]
            far = jnp.where(valid, scores[:, h * 256 + 128 : h * 256 + 256], -1e30)
            top = jnp.max(jnp.maximum(near, far), axis=-1, keepdims=True)
            near, far = jnp.exp(near - top), jnp.exp(far - top)
            factor = 1.0 / jnp.sum(near + far, axis=-1, keepdims=True)
            lows += [(near * factor).astype(bf), (far * factor).astype(bf)]
        low = jnp.concatenate(lows, axis=1)
        prob[rows, lanes(pair * 512, 512)] = low
        mixed[rows, lanes(pair * 128, 128)] = dot(low, v, 1, 0).astype(bf)
        return 0
    lax.fori_loop(0, 6, body, 0, unroll=2)


def own_block(place, shard, stage, group, chunk):
    p = place
    _, first, count, weight = chunk
    low = p.c == 0
    for n in range(count):
        if weight == 3:
            rows = slice(48 * n, 48 * n + 48)
            block = jnp.where(p.c == first // 2, shard[rows, p.col(p.c)], stage[rows, :])
        else:
            j = first + n if weight != 1 else 0
            mine = shard[:, lanes(column(weight, j, p.c), 384)]
            other = stage[:, j * 384 : (j + 1) * 384]
            block = jnp.concatenate([jnp.where(low, mine, other), jnp.where(low, other, mine)], axis=0)
        group[p.z, p.y, p.x, first + n, :, p.col(p.c)] = block.astype(bf)


def forward_kernel(
    images_hbm, pair, captions_hbm, qkv_in, out_in, up_in, down_in, vec_in,
    w0_hbm, w1_hbm, w2_hbm, dy_hbm, dyl_hbm, normed_hbm, proj_hbm, prob_hbm, mixed_hbm, middle_hbm, two_hbm,
    active_hbm, slope_hbm, held_hbm, stat_one_hbm, stat_two_hbm, out_hbm, vec_out,
    g0, g1, g2, slots, s0, s1, s2, s3, captions, images, dy, dyl, normed, proj, prob, mixed, middle, two, active, slope, held, stat_one, stat_two,
    wide, result, send_sem, stage_sem, rail_sem, sib_sem, vrail_sem, vsib_sem, local_sem,
):
    place = Place()
    place.greet()
    sends = Sends(send_sem)
    groups = (g0, g1, g2)
    shards, stages = (qkv_in, out_in, up_in, down_in), (s0, s1, s2, s3)
    local = []

    def keep(ref, hbm):
        copy = pltpu.make_async_copy(ref, hbm, local_sem.at[len(local)])
        copy.start()
        local.append(copy)
    fetch = pltpu.make_async_copy(images_hbm, images, local_sem.at[30])
    load = pltpu.make_async_copy(captions_hbm, captions, local_sem.at[31])
    ags = [Gather(place, n, groups[CHUNKS[n][0]], sends, rail_sem, sib_sem) for n in range(6)]
    av = GatherVectors(place, slots, sends, vrail_sem, vsib_sem)

    def begin():
        fetch.start()
        load.start()
        slots[place.z, place.y, place.x, place.c] = jnp.zeros((16, 128), f32)
        slots[place.z, place.y, place.x, place.c, 0:12, 0:24] = vec_in[...]
        place.meet()

    def stage():
        for weight, units in enumerate((3, 1, 4, 1)):
            for j in range(units):
                sends.go(
                    shards[weight].at[:, lanes(column(weight, j, 1 - place.c), 384)],
                    stages[weight].at[:, j * 384 : (j + 1) * 384], stage_sem.at[weight, j], place.sib,
                )
        av.own()

    def own(n):
        group, first, _, weight = CHUNKS[n]
        if n in (0, 1, 2, 4):
            for j in range(stages[weight].shape[1] // 384):
                await_recv(place, stages[weight].at[:, j * 384 : (j + 1) * 384], stage_sem.at[weight, j], send_sem.at[0])
        own_block(place, shards[weight], stages[weight], groups[group], CHUNKS[n])
        ags[n].own()

    def arrive(n):
        for k in (1, 3, 2):
            ags[n].arrive(k)

    def forward(n):
        for k in (0, 1, 3, 2):
            ags[n].forward(k)

    def pad():
        fetch.wait()
        pad_images(images, held)
        keep(held, held_hbm)

    def vectors():
        vec_out[...] = join_vectors(slots)

    def first():
        def first_norm(rows, _):
            h, centre, scale = norm_stats(held[rows, :].astype(f32))
            keep_stats(stat_one, rows, centre, scale)
            normed[rows, :] = (h * vec_out[0:1, :] + vec_out[1:2, :]).astype(bf)
            return 0
        row_loop(832, first_norm)
        keep(normed, normed_hbm)
        keep(stat_one, stat_one_hbm)

    def upstream(i):
        if i == 0:
            load.wait()
        upstream_sum(i, pair, captions, dy, dyl)
        if i == 3:
            keep(dy, dy_hbm)
            keep(dyl, dyl_hbm)

    def project(j):
        if j == 0:
            proj[832:880, :] = jnp.zeros((48, 2304), bf)
        value = dot(normed[...], unit(g2, j), 1, 0)
        for c in (0, 1):
            at = column(0, j, c)
            part = value[:, c * 384 : (c + 1) * 384]
            if at < 768:
                part = part + vec_out[2:3, at : at + 384]
            elif at >= 1536:
                part = part + vec_out[3:4, at - 1536 : at - 1152]
            proj[0:832, at : at + 384] = part.astype(bf)
        if j == 2:
            keep(proj, proj_hbm)

    def attention(i):
        attend(208 * i, proj, prob, mixed)

    def attended():
        keep(prob, prob_hbm)
        keep(mixed, mixed_hbm)
        wide[...] = dot(mixed[...], unit(g2, 3), 1, 0)

        def second_norm(rows, _):
            value = wide[rows, :] + held[rows, :].astype(f32) + vec_out[4:5, :]
            middle[rows, :] = value
            h, centre, scale = norm_stats(value)
            keep_stats(stat_two, rows, centre, scale)
            two[rows, :] = (h * vec_out[5:6, :] + vec_out[6:7, :]).astype(bf)
            return 0
        row_loop(832, second_norm)
        keep(middle, middle_hbm)
        keep(two, two_hbm)
        keep(stat_two, stat_two_hbm)

    def up(j):
        wide[...] = dot(two[...], unit(g1, j), 1, 0)

        def bend(rows, _):
            for c in (0, 1):
                at = c * 1536 + j * 384
                u = wide[rows, c * 384 : (c + 1) * 384] + vec_out[8 + at // 768 : 9 + at // 768, at % 768 : at % 768 + 384]
                u2 = u * u
                s = 0.5 + 0.5 * jnp.tanh(u * (0.7978845608028654 + 0.035677408136300125 * u2))
                bent = u * s
                active[rows, at : at + 384] = bent.astype(bf)
                slope[rows, at : at + 384] = (s + (1.5957691216057308 + 0.21406444881780074 * u2) * bent * (1.0 - s)).astype(bf)
            return 0
        row_loop(832, bend)
        if j == 3:
            keep(active, active_hbm)
            keep(slope, slope_hbm)

    def down():
        for n in range(3):
            wide[:, n * 256 : (n + 1) * 256] = dot(
                active[...], g0[:, :, :, :, :, n * 256 : (n + 1) * 256].reshape(3072, 256), 1, 0
            )
        for i in range(4):
            rows = slice(208 * i, 208 * i + 196)
            result[i] = wide[rows, :] + middle[rows, :] + vec_out[7:8, :]
        for i in range(4):
            keep(result.at[i], out_hbm.at[:, i, :])

    def end():
        sends.drain()
        for copy in local:
            copy.wait()

    def finish(n):
        ags[n].finish()
        if n in (1, 3, 5):
            keep((g2, g1, g0)[n // 2], (w2_hbm, w1_hbm, w0_hbm)[n // 2])

    begin()
    stage()
    own(0)
    own(1)
    own(2)
    pad()
    own(3)
    own(4)
    own(5)
    upstream(0)
    arrive(0)
    upstream(1)
    av.rest()
    vectors()
    arrive(1)
    forward(0)
    first()
    arrive(2)
    forward(1)
    upstream(2)
    ags[0].share()
    arrive(3)
    forward(2)
    upstream(3)
    finish(0)
    project(0)
    ags[1].share()
    project(1)
    arrive(4)
    project(2)
    forward(3)
    attention(0)
    ags[2].share()
    attention(1)
    arrive(5)
    attention(2)
    ags[3].share()
    forward(4)
    attention(3)
    finish(1)
    attended()
    forward(5)
    ags[4].share()
    finish(2)
    up(0)
    up(1)
    ags[5].share()
    finish(3)
    up(2)
    up(3)
    finish(4)
    finish(5)
    down()
    end()


def forward(images, pair, captions, weights, vectors):
    dma = pltpu.SemaphoreType.DMA
    vm = pl.BlockSpec(memory_space=VMEM)
    anyspace = pl.BlockSpec(memory_space=pl.ANY)
    S = jax.ShapeDtypeStruct
    kept = [
        S((832, 768), f32), S((832, 768), bf), S((832, 768), bf), S((880, 2304), bf), S((832, 3072), bf), S((832, 768), bf),
        S((832, 768), f32), S((832, 768), bf), S((832, 3072), bf), S((832, 3072), bf), S((832, 768), bf), S((832, 256), f32), S((832, 256), f32),
    ]
    return pl.pallas_call(
        forward_kernel,
        out_shape=[S(UNIT, bf)] * 3 + kept + [S(images.shape, f32), S((16, 768), f32)],
        in_specs=[anyspace, pl.BlockSpec(memory_space=pltpu.SMEM), anyspace] + [vm] * 5,
        out_specs=[anyspace] * 17 + [vm],
        scratch_shapes=[VMEM(UNIT, bf)] * 3
        + [VMEM((4, 2, 2, 2, 16, 128), f32)]
        + [VMEM((w.shape[0], w.shape[1] // 2), f32) for w in weights]
        + [VMEM(captions.shape, bf), VMEM(images.shape, bf)]
        + [VMEM(s.shape, s.dtype) for s in kept]
        + [VMEM((832, 768), f32), VMEM((4, 196, 768), f32)]
        + [dma((176,)), dma((4, 4)), dma((6, 16)), dma((6, 4)), dma((16,)), dma((4,)), dma((32,))],
        compiler_params=pltpu.CompilerParams(collective_id=0, has_side_effects=True, vmem_limit_bytes=62 << 20),
        name="forward",
    )(images, pair, captions, *weights, vectors)


def backward_kernel(
    vec, w0_hbm, w1_hbm, w2_hbm, dy_hbm, dyl_hbm, normed_hbm, proj_hbm, prob_hbm, mixed_hbm, middle_hbm, two_hbm,
    active_hbm, slope_hbm, held_hbm, stat_one_hbm, stat_two_hbm,
    r_qkv, r_out, r_up, r_down, r_vec, r_norm, ig_hbm,
    x0, x1, x2, gd, b1, b2, dy, dyl, two, middle, mixed, wide, stats, result, *scratch,
):
    bufs, scratch = [scratch[6 * n : 6 * n + 6] for n in range(7)], scratch[42:]
    vval, vbuf, vz, nbuf, nz, send_sem, red_sem, vsem, nsem, local_sem = scratch
    place = Place()
    place.greet()
    sends = Sends(send_sem)
    count = [0]

    def fetch(hbm, ref):
        copy = pltpu.make_async_copy(hbm, ref, local_sem.at[count[0]])
        count[0] += 1
        copy.start()
        return copy
    got = {}
    puts = []
    reds = [
        Reduce(place, n, group, first, units, bufs[n], sends, red_sem.at[n])
        for n, (group, first, units) in enumerate(
            ((gd, 0, 4), (x0, 0, 2), (x0, 2, 2), (x1, 3, 1), (x1, 0, 1), (x1, 1, 1), (x1, 2, 1))
        )
    ]
    ones = jnp.ones((16, 832), bf)

    def total(ref, at):
        return dot(ones, ref[0:832, lanes(at, 768)], 1, 0)[0:1, :]

    def columns(weight, j):
        low, high = column(weight, j, 0), column(weight, j, 1)
        return jnp.concatenate([b2[0:832, lanes(low, 384)], b2[0:832, lanes(high, 384)]], axis=1)

    def begin():
        vval[12:16, :] = jnp.zeros((4, 768), f32)
        for name, hbm, ref in (
            ("dyl", dyl_hbm, dyl), ("active", active_hbm, b1), ("w0", w0_hbm, x0), ("slope", slope_hbm, b2.at[0:832]),
            ("two", two_hbm, two), ("w1", w1_hbm, x1), ("dy", dy_hbm, dy), ("middle", middle_hbm, middle), ("stats", stat_two_hbm, stats),
            ("mixed", mixed_hbm, mixed), ("w2", w2_hbm, x2),
        ):
            got[name] = fetch(hbm, ref)

    def raw_down(k):
        if k == ORDER[0]:
            got["dyl"].wait()
            got["active"].wait()
        z = place.zz(k)
        gd[z] = dot(b1[:, lanes(768 * z, 768)], dyl[...], 0, 0).astype(bf).reshape(2, 2, 4, 48, 768)
        if k == ORDER[3]:
            got["prob"] = fetch(prob_hbm, b1)
            vval[7:8, :] = total(dyl, 0)

    def active_grad(start, stop):
        if start == 0:
            got["w0"].wait()
            got["slope"].wait()

        def body(z, _):
            at = lanes(768 * z, 768)
            b2[0:832, at] = (dot(dyl[...], x0[z].reshape(768, 768), 1, 1) * b2[0:832, at].astype(f32)).astype(bf)
            vval[pl.ds(8 + z, 1), :] = total(b2, 768 * z)
            return 0
        lax.fori_loop(start, stop, body, 0)

    def raw_up(start, stop):
        if start == 0:
            got["two"].wait()

        def body(j, _):
            x0[:, :, :, j] = dot(two[...], columns(2, j), 0, 0).astype(bf).reshape(4, 2, 2, 48, 768)
            return 0
        lax.fori_loop(start, stop, body, 0)

    def two_grad(start, stop):
        if start == 0:
            got["w1"].wait()
            wide[...] = dot(columns(2, 0), unit(x1, 0), 1, 1)

        def body(j, _):
            wide[...] += dot(columns(2, j), unit(x1, j), 1, 1)
            return 0
        lax.fori_loop(max(start, 1), stop, body, 0)
        if stop == 4:
            got["proj"] = fetch(proj_hbm, b2.at[:, 0:2304])
            got["normed"] = fetch(normed_hbm, b2.at[0:832, 2304:3072])
    zero = jnp.zeros((8, 768), f32)

    def fold(value):
        return jnp.sum(value.reshape(CHUNK // 8, 8, 768), axis=0)

    def second():
        got["dy"].wait()
        got["middle"].wait()
        got["stats"].wait()

        def second_norm(rows, carry):
            grad = wide[rows, :]
            h, scale = normalized(middle[rows, :], stats, rows)
            e = grad * vec[5:6, :]
            mean = jnp.sum(e, axis=-1, keepdims=True) * (1.0 / 768)
            along = jnp.sum(e * h, axis=-1, keepdims=True) * (1.0 / 768)
            value = dy[rows, :] + scale * (e - mean - h * along)
            dy[rows, :] = value
            low = value.astype(bf)
            two[rows, :] = low
            return carry[0] + fold(grad * h), carry[1] + fold(grad), carry[2] + fold(low.astype(f32))
        sums = row_loop(832, second_norm, (zero, zero, zero))
        for row, part in zip((5, 6, 4), sums):
            vval[row : row + 1, :] = jnp.sum(part, axis=0, keepdims=True)

    def raw_out():
        got["mixed"].wait()
        x1[:, :, :, 3] = dot(mixed[...], two[...], 0, 0).astype(bf).reshape(4, 2, 2, 48, 768)
        got["held"] = fetch(held_hbm, mixed)
        got["stats"] = fetch(stat_one_hbm, stats)

    def mixed_grad():
        got["w2"].wait()
        dyl[...] = dot(two[...], unit(x2, 3), 1, 1).astype(bf)
        got["prob"].wait()
        got["proj"].wait()

    def attention(half, i):
        base = 208 * i
        first = lax.broadcasted_iota(jnp.int32, (208, 128), 1) < 64

        def heads(pair, _):
            rows, deep = pl.ds(base, 208), pl.ds(base, 256)
            at_q, at_k, at_v = lanes(pair * 128, 128), lanes(768 + pair * 128, 128), lanes(1536 + pair * 128, 128)
            q, k, v = b2[rows, at_q], both_heads(b2[deep, at_k], score_scale), both_heads(b2[deep, at_v])
            d = dyl[rows, at_q]
            low = b1[rows, lanes(pair * 512, 512)]
            p = low.astype(f32)
            weighted = p * dot(d, v, 1, 1)
            parts = []
            for h in (0, 1):
                part = slice(h * 256, h * 256 + 256)
                parts.append((weighted[:, part] - p[:, part] * jnp.sum(weighted[:, part], axis=-1, keepdims=True)).astype(bf))
            s = jnp.concatenate(parts, axis=1)
            dk, dv = dot(s, q, 0, 0), dot(low, d, 0, 0)
            b2[rows, at_q] = dot(s, k, 1, 0).astype(bf)
            b2[rows, at_k] = (jnp.where(first, dk[0:208], dk[256:464]) * score_scale).astype(bf)
            b2[rows, at_v] = jnp.where(first, dv[0:208], dv[256:464]).astype(bf)
            return 0
        lax.fori_loop(3 * half, 3 * half + 3, heads, 0)

    def raw_qkv(j):
        if j == 0:
            got["normed"].wait()
        x1[:, :, :, j] = dot(b2[0:832, 2304:3072], columns(0, j), 0, 0).astype(bf).reshape(4, 2, 2, 48, 768)

    def qkv_sums():
        vval[2:3, :] = total(b2, 0)
        vval[3:4, :] = total(b2, 1536)

    def normed_grad():
        wide[...] = dot(columns(0, 0), unit(x2, 0), 1, 1)
        wide[...] += dot(columns(0, 1), unit(x2, 1), 1, 1)
        wide[...] += dot(columns(0, 2), unit(x2, 2), 1, 1)

    def first():
        got["held"].wait()
        got["stats"].wait()

        def first_norm(rows, carry):
            grad = wide[rows, :]
            h, scale = normalized(mixed[rows, :].astype(f32), stats, rows)
            e = grad * vec[0:1, :]
            mean = jnp.sum(e, axis=-1, keepdims=True) * (1.0 / 768)
            along = jnp.sum(e * h, axis=-1, keepdims=True) * (1.0 / 768)
            dy[rows, :] = dy[rows, :] + scale * (e - mean - h * along)
            return carry[0] + fold(grad * h), carry[1] + fold(grad)
        sums = row_loop(832, first_norm, (zero, zero))
        for row, part in zip((0, 1), sums):
            vval[row : row + 1, :] = jnp.sum(part, axis=0, keepdims=True)
        for i in range(4):
            result[i] = dy[208 * i : 208 * i + 196, :]
            put = pltpu.make_async_copy(result.at[i], ig_hbm.at[:, i, :], local_sem.at[24 + i])
            put.start()
            puts.append(put)

    vsum = SumAll(place, vval, vbuf, vz, sends, vsem)
    nsum = SumFew(place, nbuf, nz, sends, nsem)

    def line(n):
        got["squares"] = got.get("squares", 0.0) + reds[n].line_add(n > 0)

    def vectors():
        got["vsum"] = vsum.total()
        r_vec[...] = got["vsum"]

    def norm():
        nsum.start(got["squares"])

    def emit(n):
        red = reds[n]
        weight, unit0, out = ((3, 0, r_down), (2, 0, r_up), (2, 2, r_up), (1, 0, r_out), (0, 0, r_qkv), (0, 1, r_qkv), (0, 2, r_qkv))[n]
        red.wait(red.swap, 15)
        for j in range(red.swap.shape[0]):
            if weight == 3:
                out[48 * j : 48 * (j + 1), place.col(place.c)] = red.final[place.c * 2 + j]
                out[48 * j : 48 * (j + 1), place.col(1 - place.c)] = red.swap[j]
            else:
                mine = pl.ds(pl.multiple_of(place.c * 24, 8), 24)
                out[:, lanes(column(weight, unit0 + j, place.c), 384)] = red.final[j, mine, :]
                out[:, lanes(column(weight, unit0 + j, 1 - place.c), 384)] = red.swap[j]

    def finish():
        whole = nsum.total()
        r_norm[...] = jnp.zeros((8, 128), f32) + (jnp.sum(whole) + jnp.sum(got["vsum"] * got["vsum"]))

    def end():
        sends.drain()
        for put in puts:
            put.wait()
    begin()
    raw_down(2)
    place.meet()
    reds[0].core_go(2)
    raw_down(1)
    reds[0].core_go(1)
    reds[0].first_go(2)
    raw_down(3)
    reds[0].core_go(3)
    reds[0].first_go(1)
    raw_down(0)
    reds[0].core_go(0)
    reds[0].first_go(3)
    active_grad(0, 1)
    reds[0].first_go(0)
    active_grad(1, 4)
    raw_up(0, 2)
    reds[1].core_go()
    raw_up(2, 4)
    reds[2].core_go()
    reds[1].first_go()
    two_grad(0, 1)
    reds[2].first_go()
    two_grad(1, 3)
    reds[0].second_go()
    two_grad(3, 4)
    second()
    reds[1].second_go()
    raw_out()
    reds[3].core_go()
    mixed_grad()
    attention(0, 0)
    reds[3].first_go()
    attention(0, 1)
    reds[2].second_go()
    attention(0, 2)
    reds[0].line_go()
    attention(0, 3)
    raw_qkv(0)
    reds[4].core_go()
    attention(1, 0)
    reds[4].first_go()
    reds[1].line_go()
    attention(1, 1)
    reds[2].line_go()
    reds[3].second_go()
    attention(1, 2)
    attention(1, 3)
    reds[3].line_go()
    reds[4].second_go()
    raw_qkv(1)
    reds[5].core_go()
    raw_qkv(2)
    reds[6].core_go()
    line(0)
    qkv_sums()
    reds[5].first_go()
    reds[6].first_go()
    normed_grad()
    reds[4].line_go()
    line(1)
    line(2)
    first()
    line(3)
    vsum.step(0)
    reds[5].second_go()
    reds[6].second_go()
    vsum.step(1)
    line(4)
    emit(0)
    reds[5].line_go()
    vsum.step(2)
    reds[6].line_go()
    emit(1)
    emit(2)
    vsum.step(3)
    line(5)
    line(6)
    vectors()
    norm()
    emit(3)
    emit(4)
    nsum.turn()
    emit(5)
    emit(6)
    finish()
    end()


def backward(shape, vec, groups, kept, shards):
    dma = pltpu.SemaphoreType.DMA
    vm = pl.BlockSpec(memory_space=VMEM)
    anyspace = pl.BlockSpec(memory_space=pl.ANY)
    S = jax.ShapeDtypeStruct
    bufs = []
    for units, apart in ((4, False), (2, True), (2, True), (1, True), (1, True), (1, True), (1, True)):
        block = (units, 48, 384)
        swap = (units, 24, 384) if apart else (units // 2, 48, 384)
        bufs += [
            VMEM((4, 2, 2) + block, bf), VMEM((4, 2) + block, bf), VMEM((4,) + block, bf), VMEM((3,) + block, bf),
            VMEM(block, f32), VMEM(swap, f32),
        ]
    return pl.pallas_call(
        backward_kernel,
        out_shape=[S(s, f32) for s in shards] + [S((16, 768), f32), S((8, 128), f32), S(shape, f32)],
        in_specs=[vm] + [anyspace] * 16,
        out_specs=[vm] * 6 + [anyspace],
        scratch_shapes=[VMEM(UNIT, bf)] * 4
        + [
            VMEM((832, 3072), bf), VMEM((880, 3072), bf), VMEM((832, 768), f32), VMEM((832, 768), bf), VMEM((832, 768), bf),
            VMEM((832, 768), f32), VMEM((832, 768), bf), VMEM((832, 768), f32), VMEM((832, 256), f32), VMEM((4, 196, 768), f32),
        ]
        + bufs
        + [VMEM((16, 768), f32), VMEM((3, 16, 768), f32), VMEM((4, 16, 768), f32)]
        + [VMEM((8, 8, 128), f32), VMEM((4, 8, 128), f32)]
        + [dma((168,)), dma((7, 16)), dma((7,)), dma((12,)), dma((28,))],
        compiler_params=pltpu.CompilerParams(collective_id=1, has_side_effects=True, vmem_limit_bytes=62 << 20),
        name="backward",
    )(vec, *groups, *kept)


def update_kernel(squares, vsum, *refs):
    loads, stores, norm_out = refs[0:21], refs[21:43], refs[43]
    held, made, wide, sems = refs[44:65], refs[65:85], refs[85], refs[86]
    moves = [pltpu.make_async_copy(s, t, sems.at[n]) for n, (s, t) in enumerate(zip(loads, held))]
    for move in moves:
        move.start()
    norm = jnp.sqrt(squares[0:1, 0:1])
    norm_out[...] = norm
    factor = clip_limit / jnp.maximum(norm, clip_limit)
    start = 24 * lax.axis_index("dev")
    wide[:, 0:768] = vsum[...]
    wide[:, 768:896] = jnp.zeros((16, 128), f32)
    window = wide[:, lanes((start // 128) * 128, 256)]
    shard = pltpu.roll(window, 256 - start % 128, 1)[0:12, 0:24]
    puts = []

    def put(ref, n):
        move = pltpu.make_async_copy(ref, stores[n], sems.at[21 + n])
        move.start()
        puts.append(move)
    for n in range(2):
        moves[n].wait()
        put(held[n], n)
    for n in range(5):
        rates = (rate_matrix, decay_matrix) if n < 4 else (rate_vector, 0.0)
        own = range(2 + 4 * n, 6 + 4 * n if n < 4 else 21)
        for m in own:
            moves[m].wait()
        values = [held[m][...] for m in own]
        master, first, second = values[:3]
        parts = adam_update(master, values[3] if n < 4 else shard, first, second, factor, *rates)
        for k in range(4):
            made[4 * n + k][...] = parts[k]
            put(made[4 * n + k], 2 + 4 * n + k)
    for move in puts:
        move.wait()


def update(squares, vsum, grads, masters, first, second, kept):
    vm = pl.BlockSpec(memory_space=VMEM)
    anyspace = pl.BlockSpec(memory_space=pl.ANY)
    S = jax.ShapeDtypeStruct
    loads = list(kept)
    for n in range(5):
        loads += [masters[n], first[n], second[n]] + ([grads[n]] if n < 4 else [])
    made = [m.shape for m in masters for _ in range(4)]
    return pl.pallas_call(
        update_kernel,
        out_shape=[S(a.shape, f32) for a in kept] + [S(m, f32) for m in made] + [S((1, 1), f32)],
        in_specs=[vm] * 2 + [anyspace] * 21,
        out_specs=[anyspace] * 22 + [vm],
        scratch_shapes=[VMEM(a.shape, f32) for a in loads] + [VMEM(m, f32) for m in made]
        + [VMEM((16, 896), f32), pltpu.SemaphoreType.DMA((43,))],
        compiler_params=pltpu.CompilerParams(vmem_limit_bytes=62 << 20),
        name="update",
    )(squares, vsum, *loads)


def local_wide(
    images,
    pair_matrix,
    caption_grads,
    qkv_weight,
    out_weight,
    up_weight,
    down_weight,
    vector_rows,
    first_qkv,
    first_out,
    first_up,
    first_down,
    first_vectors,
    second_qkv,
    second_out,
    second_up,
    second_down,
    second_vectors,
):
    image_count, patches, model_width = images.shape
    row_count = image_count * patches
    head_count = model_width // HD
    qkv_low = qkv_weight.astype(jnp.bfloat16)
    out_low = out_weight.astype(jnp.bfloat16)
    up_low = up_weight.astype(jnp.bfloat16)
    down_low = down_weight.astype(jnp.bfloat16)
    vector_low = vector_rows.astype(jnp.bfloat16)
    gathered = (
        lax.all_gather(qkv_low, "dev", axis=0, tiled=True),
        lax.all_gather(out_low, "dev", axis=0, tiled=True),
        lax.all_gather(up_low, "dev", axis=0, tiled=True),
        lax.all_gather(down_low, "dev", axis=0, tiled=True),
        lax.all_gather(vector_low, "dev", axis=1, tiled=True),
    )
    result, unused_values = forward_pass(gathered, images)
    output = result.reshape(image_count, patches, model_width)
    gathered_again = (
        lax.all_gather(qkv_low, "dev", axis=0, tiled=True),
        lax.all_gather(out_low, "dev", axis=0, tiled=True),
        lax.all_gather(up_low, "dev", axis=0, tiled=True),
        lax.all_gather(down_low, "dev", axis=0, tiled=True),
        lax.all_gather(vector_low, "dev", axis=1, tiled=True),
    )
    qkv_full, out_full, up_full, down_full, vector_again = gathered_again
    vector_full = vector_again.astype(jnp.float32)
    recomputed, kept_values = forward_pass(gathered_again, images)
    (
        flat_inputs,
        normed_low,
        queries,
        keys_all,
        values_all,
        probabilities,
        prob_low,
        mixed_low,
        middle,
        normed_two_low,
        upward,
        active_low,
    ) = kept_values
    caption_flat = caption_grads.reshape(caption_grads.shape[0], patches * model_width)
    upstream = jnp.dot(
        pair_matrix.astype(jnp.bfloat16), caption_flat, preferred_element_type=jnp.float32
    ).reshape(row_count, model_width)
    down_grad_low = upstream.astype(jnp.bfloat16)
    raw_down = contract_first(active_low, down_grad_low)
    bias_down_grad = jnp.sum(down_grad_low.astype(jnp.float32), axis=0)
    active_grad = contract_last(down_grad_low, down_full)
    gelu_value, gelu_pull = jax.vjp(gelu_tanh, upward)
    upward_grad_low = gelu_pull(active_grad)[0].astype(jnp.bfloat16)
    raw_up = contract_first(normed_two_low, upward_grad_low)
    bias_up_grad = jnp.sum(upward_grad_low.astype(jnp.float32), axis=0)
    normed_two_grad = contract_last(upward_grad_low, up_full)
    second_norm_value, second_norm_pull = jax.vjp(
        layer_norm, middle, vector_full[5], vector_full[6]
    )
    middle_norm_grad, gain_two_grad, shift_two_grad = second_norm_pull(normed_two_grad)
    middle_grad = upstream + middle_norm_grad
    attended_low = middle_grad.astype(jnp.bfloat16)
    raw_out = contract_first(mixed_low, attended_low)
    bias_out_grad = jnp.sum(attended_low.astype(jnp.float32), axis=0)
    mixed_grad_low = (
        contract_last(attended_low, out_full)
        .astype(jnp.bfloat16)
        .reshape(image_count, patches, head_count, HD)
    )
    prob_grad = jnp.einsum(
        "bqhd,bkhd->bhqk", mixed_grad_low, values_all, preferred_element_type=jnp.float32
    )
    value_grad = jnp.einsum(
        "bhqk,bqhd->bkhd", prob_low, mixed_grad_low, preferred_element_type=jnp.float32
    )
    score_grad = probabilities * (
        prob_grad - jnp.sum(probabilities * prob_grad, axis=-1, keepdims=True)
    )
    score_grad_low = score_grad.astype(jnp.bfloat16)
    query_grad = (
        jnp.einsum("bhqk,bkhd->bqhd", score_grad_low, keys_all, preferred_element_type=jnp.float32)
        * score_scale
    )
    key_grad = (
        jnp.einsum("bhqk,bqhd->bkhd", score_grad_low, queries, preferred_element_type=jnp.float32)
        * score_scale
    )
    projected_grad_low = (
        jnp.stack([query_grad, key_grad, value_grad], axis=2)
        .astype(jnp.bfloat16)
        .reshape(row_count, 3 * model_width)
    )
    raw_qkv = contract_first(normed_low, projected_grad_low)
    bias_qkv_grad = jnp.sum(projected_grad_low.astype(jnp.float32), axis=0)
    normed_grad = contract_last(projected_grad_low, qkv_full)
    first_norm_value, first_norm_pull = jax.vjp(
        layer_norm, flat_inputs, vector_full[0], vector_full[1]
    )
    inputs_norm_grad, gain_one_grad, shift_one_grad = first_norm_pull(normed_grad)
    input_grads = (middle_grad + inputs_norm_grad).reshape(image_count, patches, model_width)
    small_rows = jnp.stack(
        [
            gain_one_grad,
            shift_one_grad,
            bias_qkv_grad[:model_width],
            bias_qkv_grad[2 * model_width :],
            bias_out_grad,
            gain_two_grad,
            shift_two_grad,
            bias_down_grad,
        ]
    )
    raw_vectors = jnp.concatenate([small_rows, bias_up_grad.reshape(-1, model_width)], axis=0)
    qkv_shard, out_shard, up_shard, down_shard, vector_shard = (
        lax.psum_scatter(raw_qkv, "dev", scatter_dimension=0, tiled=True),
        lax.psum_scatter(raw_out, "dev", scatter_dimension=0, tiled=True),
        lax.psum_scatter(raw_up, "dev", scatter_dimension=0, tiled=True),
        lax.psum_scatter(raw_down, "dev", scatter_dimension=0, tiled=True),
        lax.psum_scatter(raw_vectors, "dev", scatter_dimension=1, tiled=True),
    )
    local_squares = (
        jnp.sum(qkv_shard * qkv_shard)
        + jnp.sum(out_shard * out_shard)
        + jnp.sum(up_shard * up_shard)
        + jnp.sum(down_shard * down_shard)
        + jnp.sum(vector_shard * vector_shard)
    )
    grad_norm = jnp.sqrt(lax.psum(local_squares, "dev"))
    factor = clip_limit / jnp.maximum(grad_norm, clip_limit)
    qkv_parts = adam_update(
        qkv_weight, qkv_shard, first_qkv, second_qkv, factor, rate_matrix, decay_matrix
    )
    out_parts = adam_update(
        out_weight, out_shard, first_out, second_out, factor, rate_matrix, decay_matrix
    )
    up_parts = adam_update(
        up_weight, up_shard, first_up, second_up, factor, rate_matrix, decay_matrix
    )
    down_parts = adam_update(
        down_weight, down_shard, first_down, second_down, factor, rate_matrix, decay_matrix
    )
    vector_parts = adam_update(
        vector_rows, vector_shard, first_vectors, second_vectors, factor, rate_vector, 0.0
    )
    return (
        output,
        input_grads,
        grad_norm,
        qkv_parts[0],
        qkv_parts[1],
        qkv_parts[2],
        qkv_parts[3],
        out_parts[0],
        out_parts[1],
        out_parts[2],
        out_parts[3],
        up_parts[0],
        up_parts[1],
        up_parts[2],
        up_parts[3],
        down_parts[0],
        down_parts[1],
        down_parts[2],
        down_parts[3],
        vector_parts[0],
        vector_parts[1],
        vector_parts[2],
        vector_parts[3],
    )


def local_slice(
    images,
    pair_matrix,
    caption_grads,
    qkv_weight,
    out_weight,
    up_weight,
    down_weight,
    vector_rows,
    first_qkv,
    first_out,
    first_up,
    first_down,
    first_vectors,
    second_qkv,
    second_out,
    second_up,
    second_down,
    second_vectors,
):
    weights = (qkv_weight, out_weight, up_weight, down_weight)
    results = forward(images.transpose(1, 0, 2), pair_matrix, caption_grads, weights, vector_rows)
    groups, kept, output, vector_full = results[0:3], results[3:16], results[16], results[17]
    shapes = [w.shape for w in weights]
    qkv_shard, out_shard, up_shard, down_shard, vector_sum, squares, input_grads = backward(
        output.shape, vector_full, groups, kept, shapes
    )
    masters = (*weights, vector_rows)
    first = (first_qkv, first_out, first_up, first_down, first_vectors)
    second = (second_qkv, second_out, second_up, second_down, second_vectors)
    shards = (qkv_shard, out_shard, up_shard, down_shard)
    output, input_grads, *parts, norm = update(squares, vector_sum, shards, masters, first, second, (output, input_grads))
    return (output.transpose(1, 0, 2), input_grads.transpose(1, 0, 2), norm[0, 0], *parts)


def solution(mesh):
    fits = mesh.shape["dev"] == 32
    return jax.shard_map(
        local_slice if fits else local_wide,
        mesh=mesh,
        in_specs=(
            P("dev", None, None),
            P("dev", None),
            P("dev", None, None),
            P("dev", None),
            P("dev", None),
            P("dev", None),
            P("dev", None),
            P(None, "dev"),
            P("dev", None),
            P("dev", None),
            P("dev", None),
            P("dev", None),
            P(None, "dev"),
            P("dev", None),
            P("dev", None),
            P("dev", None),
            P("dev", None),
            P(None, "dev"),
        ),
        out_specs=(
            P("dev", None, None),
            P("dev", None, None),
            P(),
            P("dev", None),
            P("dev", None),
            P("dev", None),
            P("dev", None),
            P("dev", None),
            P("dev", None),
            P("dev", None),
            P("dev", None),
            P("dev", None),
            P("dev", None),
            P("dev", None),
            P("dev", None),
            P("dev", None),
            P("dev", None),
            P("dev", None),
            P("dev", None),
            P(None, "dev"),
            P(None, "dev"),
            P(None, "dev"),
            P(None, "dev"),
        ),
        check_vma=False,
    )
```

```python
import functools

import jax
import jax.numpy as jnp
from jax import lax
from jax.experimental import pallas as pl
from jax.experimental.pallas import tpu as pltpu
from jax.sharding import PartitionSpec as P

HD = 64
STEP = 10


norm_eps = 1e-06
clip_limit = 1.0
beta_one = 0.9
beta_two = 0.999
adam_eps = 1e-08
rate_matrix = 0.08
rate_vector = 0.5
decay_matrix = 0.1
score_scale = 0.125


def layer_norm(values, gain_row, shift_row):
    centre = jnp.mean(values, axis=-1, keepdims=True)
    offset = values - centre
    spread = jnp.mean(offset * offset, axis=-1, keepdims=True)
    return offset * lax.rsqrt(spread + norm_eps) * gain_row + shift_row


def softmax_rows(scores):
    shifted = scores - jnp.max(scores, axis=-1, keepdims=True)
    weights = jnp.exp(shifted)
    return weights / jnp.sum(weights, axis=-1, keepdims=True)


def gelu_tanh(values):
    return jax.nn.gelu(values, approximate=True)


def contract_last(left_side, right_side):
    return lax.dot_general(
        left_side, right_side, (((1,), (1,)), ((), ())), preferred_element_type=jnp.float32
    )


def contract_first(left_side, right_side):
    return lax.dot_general(
        left_side, right_side, (((0,), (0,)), ((), ())), preferred_element_type=jnp.float32
    )


def forward_pass(gathered, inputs):
    qkv_full, out_full, up_full, down_full, vector_low = gathered
    vector_full = vector_low.astype(jnp.float32)
    image_count, patches, model_width = inputs.shape
    row_count = image_count * patches
    head_count = model_width // HD
    flat_inputs = inputs.astype(jnp.float32).reshape(row_count, model_width)
    normed_low = layer_norm(flat_inputs, vector_full[0], vector_full[1]).astype(jnp.bfloat16)
    bias_qkv = jnp.concatenate([vector_full[2], jnp.zeros_like(vector_full[2]), vector_full[3]])
    projected = jnp.dot(normed_low, qkv_full, preferred_element_type=jnp.float32) + bias_qkv
    projected_low = projected.astype(jnp.bfloat16).reshape(image_count, patches, 3, head_count, HD)
    queries = projected_low[:, :, 0]
    keys_all = projected_low[:, :, 1]
    values_all = projected_low[:, :, 2]
    scores = (
        jnp.einsum("bqhd,bkhd->bhqk", queries, keys_all, preferred_element_type=jnp.float32)
        * score_scale
    )
    probabilities = softmax_rows(scores)
    prob_low = probabilities.astype(jnp.bfloat16)
    mixed_heads = jnp.einsum(
        "bhqk,bkhd->bqhd", prob_low, values_all, preferred_element_type=jnp.float32
    )
    mixed_low = mixed_heads.reshape(row_count, model_width).astype(jnp.bfloat16)
    attended = jnp.dot(mixed_low, out_full, preferred_element_type=jnp.float32) + vector_full[4]
    middle = flat_inputs + attended
    normed_two_low = layer_norm(middle, vector_full[5], vector_full[6]).astype(jnp.bfloat16)
    upward = jnp.dot(normed_two_low, up_full, preferred_element_type=jnp.float32) + vector_full[
        8:
    ].reshape(-1)
    active_low = gelu_tanh(upward).astype(jnp.bfloat16)
    downward = jnp.dot(active_low, down_full, preferred_element_type=jnp.float32) + vector_full[7]
    result = middle + downward
    kept_values = (
        flat_inputs,
        normed_low,
        queries,
        keys_all,
        values_all,
        probabilities,
        prob_low,
        mixed_low,
        middle,
        normed_two_low,
        upward,
        active_low,
    )
    return (result, kept_values)


def adam_update(master, raw_grad, moment_one, moment_two, factor, step_rate, decay_rate):
    clipped = raw_grad * factor
    moment_one_new = beta_one * moment_one + (1.0 - beta_one) * clipped
    moment_two_new = beta_two * moment_two + (1.0 - beta_two) * clipped * clipped
    first_hat = moment_one_new / (1.0 - beta_one**STEP)
    second_hat = moment_two_new / (1.0 - beta_two**STEP)
    master_new = master - step_rate * (
        first_hat / (jnp.sqrt(second_hat) + adam_eps) + decay_rate * master
    )
    return (clipped, master_new, moment_one_new, moment_two_new)


MESH = pl.DeviceIdType.MESH
bf = jnp.bfloat16
f32 = jnp.float32
VMEM = pltpu.VMEM
ROWS = 208
UNIT = (4, 2, 2, 4, 48, 768)
CHUNKS = ((2, 0, 3, 0), (2, 3, 1, 1), (1, 0, 2, 2), (1, 2, 2, 2), (0, 0, 2, 3), (0, 2, 2, 3))


QKV_AT = ((0, 768), (1536, 384), (1152, 1920))


def column(weight, unit, c):
    if weight == 0:
        low, high = QKV_AT[unit]
        return low + c * (high - low)
    return c * (1536 if weight == 2 else 384) + (384 * unit if weight == 2 else 0)


class Place:
    def __init__(self):
        me = lax.axis_index("dev")
        self.me = me
        self.c = me % 2
        self.x = (me // 2) % 2
        self.y = (me // 4) % 2
        self.z = me // 8
        self.q = me // 2
        self.sib = me + 1 - 2 * self.c
        self.xn = me + 2 - 4 * self.x
        self.yn = me + 4 - 8 * self.y
        self.xo = 1 - self.x
        self.yo = 1 - self.y

    def zz(self, k):
        return (self.z + k) % 4

    def zp(self, k):
        return self.zz(k) * 8 + self.me % 8

    def col(self, c):
        return pl.ds(pl.multiple_of(c * 384, 128), 384)

    def greet(self):
        bar = pltpu.get_barrier_semaphore()
        for dev in [self.near(n) for n in range(1, 8)] + [self.zp(1), self.zp(2), self.zp(3)]:
            pl.semaphore_signal(bar, inc=1, device_id=(dev,), device_id_type=MESH)

    def near(self, n):
        return self.z * 8 + (self.me + n) % 8

    def meet(self):
        pl.semaphore_wait(pltpu.get_barrier_semaphore(), 10)


class Sends:
    def __init__(self, sems):
        self.sems = sems
        self.used = 0
        self.open = []

    def go(self, src, dst, recv, dev):
        copy = pltpu.make_async_remote_copy(
            src_ref=src, dst_ref=dst, send_sem=self.sems.at[self.used], recv_sem=recv,
            device_id=(dev,), device_id_type=MESH,
        )
        self.used += 1
        copy.start()
        self.open.append(copy)

    def drain(self):
        for copy in self.open:
            copy.wait_send()
        self.open = []


def await_recv(place, ref, recv, spare):
    pltpu.make_async_remote_copy(
        src_ref=ref, dst_ref=ref, send_sem=spare, recv_sem=recv,
        device_id=(place.sib,), device_id_type=MESH,
    ).wait_recv()


class Gather:
    def __init__(self, place, chunk, group, sends, rail_sem, sib_sem):
        self.p, self.group, self.sends = place, group, sends
        self.number = chunk
        _, self.first, self.count, _ = CHUNKS[chunk]
        self.rail_sem, self.sib_sem = rail_sem.at[chunk], sib_sem.at[chunk]

    def at(self, k, y, x):
        return self.group.at[self.p.zz(k), y, x, pl.ds(self.first, self.count), :, self.p.col(self.p.c)]

    def sem(self, k, y, x):
        return self.rail_sem.at[self.p.zz(k) * 4 + y * 2 + x]

    def go(self, k, y, x, dev):
        ref = self.at(k, y, x)
        self.sends.go(ref, ref, self.sem(k, y, x), dev)

    def wait(self, k, y, x):
        await_recv(self.p, self.at(k, y, x), self.sem(k, y, x), self.sends.sems.at[0])

    def own(self):
        p = self.p
        for k in (2, 1, 3):
            self.go(0, p.y, p.x, p.zp(k))
        self.plane(0)

    def turn(self, k):
        return (k + self.number) % 2 == 0

    def plane(self, k):
        p = self.p
        for dev in (p.xn, p.yn) if self.turn(k) else (p.yn, p.xn):
            self.go(k, p.y, p.x, dev)

    def arrive(self, k):
        self.wait(k, self.p.y, self.p.x)
        self.plane(k)

    def forward(self, k):
        p = self.p
        if self.turn(k):
            self.wait(k, p.y, p.xo)
            self.go(k, p.y, p.xo, p.yn)
        else:
            self.wait(k, p.yo, p.x)
            self.go(k, p.yo, p.x, p.xn)


    def level(self, k, c):
        return self.group.at[self.p.zz(k), :, :, pl.ds(self.first, self.count), :, self.p.col(c)]

    def share(self):
        p = self.p
        for k in (0, 1, 3, 2):
            if self.turn(k):
                self.wait(k, p.yo, p.x)
            else:
                self.wait(k, p.y, p.xo)
            self.wait(k, p.yo, p.xo)
            ref = self.level(k, p.c)
            self.sends.go(ref, ref, self.sib_sem.at[p.zz(k)], p.sib)

    def finish(self):
        p = self.p
        for k in (0, 1, 3, 2):
            await_recv(p, self.level(k, 1 - p.c), self.sib_sem.at[p.zz(k)], self.sends.sems.at[0])


class GatherVectors:
    def __init__(self, place, slots, sends, rail_sem, sib_sem):
        self.p, self.slots, self.sends, self.rail_sem, self.sib_sem = place, slots, sends, rail_sem, sib_sem

    def at(self, k, y, x, c):
        return self.slots.at[self.p.zz(k), y, x, c]

    def sem(self, k, y, x):
        return self.rail_sem.at[self.p.zz(k) * 4 + y * 2 + x]

    def go(self, k, y, x, dev):
        ref = self.at(k, y, x, self.p.c)
        self.sends.go(ref, ref, self.sem(k, y, x), dev)

    def wait(self, k, y, x):
        await_recv(self.p, self.at(k, y, x, self.p.c), self.sem(k, y, x), self.sends.sems.at[0])

    def own(self):
        p = self.p
        for k in (1, 2, 3):
            self.go(0, p.y, p.x, p.zp(k))
        self.go(0, p.y, p.x, p.xn)
        self.go(0, p.y, p.x, p.yn)

    def rest(self):
        p = self.p
        for k in range(4):
            if k:
                self.wait(k, p.y, p.x)
                self.go(k, p.y, p.x, p.xn)
                self.go(k, p.y, p.x, p.yn)
        for k in range(4):
            self.wait(k, p.y, p.xo)
            self.go(k, p.y, p.xo, p.yn)
        for k in range(4):
            self.wait(k, p.yo, p.x)
            self.wait(k, p.yo, p.xo)
            ref = self.slots.at[p.zz(k), :, :, p.c]
            self.sends.go(ref, ref, self.sib_sem.at[p.zz(k)], p.sib)
        for k in range(4):
            await_recv(p, self.slots.at[p.zz(k), :, :, 1 - p.c], self.sib_sem.at[p.zz(k)], self.sends.sems.at[0])


def join_vectors(slots):
    lane = lax.broadcasted_iota(jnp.int32, (16, 128), 1)
    tiles = [jnp.zeros((16, 128), f32) for _ in range(7)]
    for d in range(32):
        tile, off = (24 * d) // 128, (24 * d) % 128
        held = slots[d // 8, (d // 4) % 2, (d // 2) % 2, d % 2]
        turned = pltpu.roll(held, off, 1) if off else held
        tiles[tile] = jnp.where((lane >= off) & (lane < off + 24), turned, tiles[tile])
        if off + 24 > 128:
            tiles[tile + 1] = jnp.where(lane < off - 104, turned, tiles[tile + 1])
    return jnp.concatenate(tiles[:6], axis=1).astype(bf).astype(f32)


ORDER = (2, 1, 3, 0)


class Reduce:
    def __init__(self, place, turn, grad, first, count, bufs, sends, sems):
        self.p, self.parity, self.grad, self.first, self.count = place, turn, grad, first, count
        self.cb, self.pb, self.qb, self.zb, self.final, self.swap = bufs
        self.sends, self.sems = sends, sems

    def at(self, z, y, x, c):
        return (z, y, x, pl.ds(self.first, self.count), slice(None), self.p.col(c))

    def turn(self, k):
        return (k + self.parity) % 2 == 0

    def wait(self, ref, n):
        await_recv(self.p, ref, self.sems.at[n], self.sends.sems.at[0])

    def go(self, index, dst, n, dev):
        self.sends.go(self.grad.at[index], dst, self.sems.at[n], dev)

    def add(self, index, buf, at):
        self.grad[index] = self.grad[index] + buf[at]

    def core_go(self, *ks):
        every = slice(None)
        for k in ks or ORDER:
            self.go(self.at(self.p.zz(k), every, every, 1 - self.p.c), self.cb.at[k], k, self.p.sib)

    def first_go(self, *ks):
        p, every = self.p, slice(None)
        for k in ks or ORDER:
            self.wait(self.cb.at[k], k)
            z = p.zz(k)

            def body(i, _, k=k, z=z):
                self.add(self.at(z, i // 2, i % 2, p.c), self.cb, (k, i // 2, i % 2))
                return 0
            lax.fori_loop(0, 4, body, 0)
            if self.turn(k):
                self.go(self.at(z, p.yo, every, p.c), self.pb.at[k], 4 + k, p.yn)
            else:
                self.go(self.at(z, every, p.xo, p.c), self.pb.at[k], 4 + k, p.xn)

    def second_go(self, *ks):
        p = self.p
        for k in ks or ORDER:
            self.wait(self.pb.at[k], 4 + k)
            z = p.zz(k)
            for o in (0, 1):
                y, x = (p.y, o) if self.turn(k) else (o, p.x)
                self.add(self.at(z, y, x, p.c), self.pb, (k, o))
            if self.turn(k):
                self.go(self.at(z, p.y, p.xo, p.c), self.qb.at[k], 8 + k, p.xn)
            else:
                self.go(self.at(z, p.yo, p.x, p.c), self.qb.at[k], 8 + k, p.yn)

    def line_go(self):
        p = self.p
        for k in ORDER:
            self.wait(self.qb.at[k], 8 + k)
            self.add(self.at(p.zz(k), p.y, p.x, p.c), self.qb, (k,))
            if k:
                self.go(self.at(p.zz(k), p.y, p.x, p.c), self.zb.at[k - 1], 11 + k, p.zp(k))

    def line_add(self, rows_apart):
        p = self.p
        for k in (1, 2, 3):
            self.wait(self.zb.at[k - 1], 11 + k)
        total = self.grad[self.at(p.z, p.y, p.x, p.c)].astype(f32)
        for k in range(3):
            total = total + self.zb[k].astype(f32)
        self.final[...] = total
        if rows_apart:
            ref = self.final.at[:, pl.ds(pl.multiple_of((1 - p.c) * 24, 8), 24), :]
        else:
            ref = self.final.at[pl.ds((1 - p.c) * (self.count // 2), self.count // 2)]
        self.sends.go(ref, self.swap, self.sems.at[15], p.sib)
        square = total * total
        tile = jnp.sum(square.reshape(self.count * 6, 8, 384), axis=0)
        return tile[:, :128] + tile[:, 128:256] + tile[:, 256:384]


class SumAll:
    def __init__(self, place, value, buf, zbuf, sends, sems):
        self.p, self.value, self.buf, self.zbuf, self.sends, self.sems = place, value, buf, zbuf, sends, sems

    def go(self, n):
        self.sends.go(self.value, self.buf.at[n], self.sems.at[n], (self.p.sib, self.p.xn, self.p.yn)[n])
        self.copy = self.sends.open.pop()

    def add(self, n):
        await_recv(self.p, self.buf.at[n], self.sems.at[n], self.sends.sems.at[0])
        self.copy.wait_send()
        self.value[...] = self.value[...] + self.buf[n]

    def step(self, n):
        p = self.p
        if n:
            self.add(n - 1)
        if n < 3:
            self.go(n)
        else:
            self.zbuf[p.z] = self.value[...]
            for k in (2, 1, 3):
                self.sends.go(self.value, self.zbuf.at[p.z], self.sems.at[3 + p.z], p.zp(k))

    def total(self):
        p = self.p
        for k in (1, 2, 3):
            await_recv(p, self.zbuf.at[p.zz(k)], self.sems.at[3 + p.zz(k)], self.sends.sems.at[0])
        return (self.zbuf[0] + self.zbuf[1]) + (self.zbuf[2] + self.zbuf[3])


class SumFew:
    def __init__(self, place, buf, zbuf, sends, sems):
        self.p, self.buf, self.zbuf, self.sends, self.sems = place, buf, zbuf, sends, sems

    def start(self, value):
        p = self.p
        mine = p.me % 8
        self.buf[mine] = value
        for n in range(1, 8):
            self.sends.go(self.buf.at[mine], self.buf.at[mine], self.sems.at[mine], p.near(n))

    def turn(self):
        p = self.p
        for n in range(1, 8):
            slot = (p.me + n) % 8
            await_recv(p, self.buf.at[slot], self.sems.at[slot], self.sends.sems.at[0])
        self.zbuf[p.z] = jnp.sum(self.buf[...], axis=0)
        for k in (2, 1, 3):
            self.sends.go(self.zbuf.at[p.z], self.zbuf.at[p.z], self.sems.at[8 + p.z], p.zp(k))

    def total(self):
        p = self.p
        for k in (1, 2, 3):
            await_recv(p, self.zbuf.at[p.zz(k)], self.sems.at[8 + p.zz(k)], self.sends.sems.at[0])
        return (self.zbuf[0] + self.zbuf[1]) + (self.zbuf[2] + self.zbuf[3])


def dot(a, b, ca, cb):
    return lax.dot_general(a, b, (((ca,), (cb,)), ((), ())), preferred_element_type=f32)


def unit(group, j):
    return group[:, :, :, j].reshape(768, 768)


def lanes(start, size):
    return pl.ds(pl.multiple_of(start, 128), size)


CHUNK = 32


def row_loop(count, body, init=0, unroll=2):
    def step(i, carry):
        return body(pl.ds(pl.multiple_of(i * CHUNK, CHUNK), CHUNK), carry)
    return lax.fori_loop(0, count // CHUNK, step, init, unroll=unroll)


def norm_stats(rows):
    centre = jnp.sum(rows, axis=-1, keepdims=True) * (1.0 / 768)
    offset = rows - centre
    spread = jnp.sum(offset * offset, axis=-1, keepdims=True) * (1.0 / 768)
    scale = lax.rsqrt(spread + norm_eps)
    return offset * scale, centre, scale


def keep_stats(stats, rows, centre, scale):
    stats[rows, 0:128] = jnp.broadcast_to(centre, (CHUNK, 128))
    stats[rows, 128:256] = jnp.broadcast_to(scale, (CHUNK, 128))


def normalized(values, stats, rows):
    scale = stats[rows, 128:129]
    return (values - stats[rows, 0:1]) * scale, scale


def pad_images(images, held):
    for i in range(4):
        held[208 * i + 192 : 208 * i + 208, :] = jnp.zeros((16, 768), bf)
        held[208 * i : 208 * i + 196, :] = images[:, i, :]


def upstream_sum(i, pair, captions, dy, dy_low):
    dy[208 * i + 192 : 208 * i + 208, :] = jnp.zeros((16, 768), f32)
    dy_low[208 * i + 192 : 208 * i + 208, :] = jnp.zeros((16, 768), bf)
    weights = [pair[i, c].astype(f32) for c in range(14)]

    def body(j, _):
        col = lanes(j * 128, 128)
        total = weights[0] * captions[0, :, col].astype(f32)
        for c in range(1, 14):
            total = total + weights[c] * captions[c, :, col].astype(f32)
        dy[208 * i : 208 * i + 196, col] = total
        dy_low[208 * i : 208 * i + 196, col] = total.astype(bf)
        return 0
    lax.fori_loop(0, 6, body, 0)


def head_masks(value):
    lane = lax.broadcasted_iota(jnp.int32, (1, 128), 1)
    return jnp.where(lane < 64, value, 0.0).astype(bf), jnp.where(lane < 64, 0.0, value).astype(bf)


def both_heads(rows, value=1.0):
    first, second = head_masks(value)
    return jnp.concatenate([rows * first, rows * second], axis=0)


def attend(base, proj, prob, mixed):
    valid = lax.broadcasted_iota(jnp.int32, (208, 128), 1) < 68

    def body(pair, _):
        rows, wide = pl.ds(base, 208), pl.ds(base, 256)
        q = proj[rows, lanes(pair * 128, 128)]
        k = both_heads(proj[wide, lanes(768 + pair * 128, 128)], score_scale)
        v = both_heads(proj[wide, lanes(1536 + pair * 128, 128)])
        scores = dot(q, k, 1, 1)
        lows = []
        for h in (0, 1):
            near = scores[:, h * 256 : h * 256 + 128]
            far = jnp.where(valid, scores[:, h * 256 + 128 : h * 256 + 256], -1e30)
            top = jnp.max(jnp.maximum(near, far), axis=-1, keepdims=True)
            near, far = jnp.exp(near - top), jnp.exp(far - top)
            factor = 1.0 / jnp.sum(near + far, axis=-1, keepdims=True)
            lows += [(near * factor).astype(bf), (far * factor).astype(bf)]
        low = jnp.concatenate(lows, axis=1)
        prob[rows, lanes(pair * 512, 512)] = low
        mixed[rows, lanes(pair * 128, 128)] = dot(low, v, 1, 0).astype(bf)
        return 0
    lax.fori_loop(0, 6, body, 0, unroll=2)


def own_block(place, shard, stage, group, chunk):
    p = place
    _, first, count, weight = chunk
    low = p.c == 0
    for n in range(count):
        if weight == 3:
            rows = slice(48 * n, 48 * n + 48)
            block = jnp.where(p.c == first // 2, shard[rows, p.col(p.c)], stage[rows, :])
        else:
            j = first + n if weight != 1 else 0
            mine = shard[:, lanes(column(weight, j, p.c), 384)]
            other = stage[:, j * 384 : (j + 1) * 384]
            block = jnp.concatenate([jnp.where(low, mine, other), jnp.where(low, other, mine)], axis=0)
        group[p.z, p.y, p.x, first + n, :, p.col(p.c)] = block.astype(bf)


def forward_kernel(
    images_hbm, pair, captions_hbm, qkv_in, out_in, up_in, down_in, vec_in,
    w0_hbm, w1_hbm, w2_hbm, dy_hbm, dyl_hbm, normed_hbm, proj_hbm, prob_hbm, mixed_hbm, middle_hbm, two_hbm,
    active_hbm, slope_hbm, held_hbm, stat_one_hbm, stat_two_hbm, grad_hbm, out_hbm, vec_out,
    g0, g1, g2, slots, s0, s1, s2, s3, captions, images, dy, dyl, normed, proj, prob, mixed, middle, two, active, slope, held, stat_one, stat_two, grad,
    wide, result, send_sem, stage_sem, rail_sem, sib_sem, vrail_sem, vsib_sem, local_sem,
):
    place = Place()
    place.greet()
    sends = Sends(send_sem)
    groups = (g0, g1, g2)
    shards, stages = (qkv_in, out_in, up_in, down_in), (s0, s1, s2, s3)
    local = []

    def keep(ref, hbm):
        copy = pltpu.make_async_copy(ref, hbm, local_sem.at[len(local)])
        copy.start()
        local.append(copy)
    fetch = pltpu.make_async_copy(images_hbm, images, local_sem.at[30])
    load = pltpu.make_async_copy(captions_hbm, captions, local_sem.at[31])
    ags = [Gather(place, n, groups[CHUNKS[n][0]], sends, rail_sem, sib_sem) for n in range(6)]
    av = GatherVectors(place, slots, sends, vrail_sem, vsib_sem)

    def begin():
        fetch.start()
        load.start()
        slots[place.z, place.y, place.x, place.c] = jnp.zeros((16, 128), f32)
        slots[place.z, place.y, place.x, place.c, 0:12, 0:24] = vec_in[...]
        place.meet()

    def stage():
        for weight, units in enumerate((3, 1, 4, 1)):
            for j in range(units):
                sends.go(
                    shards[weight].at[:, lanes(column(weight, j, 1 - place.c), 384)],
                    stages[weight].at[:, j * 384 : (j + 1) * 384], stage_sem.at[weight, j], place.sib,
                )
        av.own()

    def own(n):
        group, first, _, weight = CHUNKS[n]
        if n in (0, 1, 2, 4):
            for j in range(stages[weight].shape[1] // 384):
                await_recv(place, stages[weight].at[:, j * 384 : (j + 1) * 384], stage_sem.at[weight, j], send_sem.at[0])
        own_block(place, shards[weight], stages[weight], groups[group], CHUNKS[n])
        ags[n].own()

    def arrive(n):
        for k in (1, 3, 2):
            ags[n].arrive(k)

    def forward(n):
        for k in (0, 1, 3, 2):
            ags[n].forward(k)

    def pad():
        fetch.wait()
        pad_images(images, held)
        keep(held, held_hbm)

    def vectors():
        vec_out[...] = join_vectors(slots)

    def first():
        def first_norm(rows, _):
            h, centre, scale = norm_stats(held[rows, :].astype(f32))
            keep_stats(stat_one, rows, centre, scale)
            normed[rows, :] = (h * vec_out[0:1, :] + vec_out[1:2, :]).astype(bf)
            return 0
        row_loop(832, first_norm)
        keep(normed, normed_hbm)
        keep(stat_one, stat_one_hbm)

    def upstream(i):
        if i == 0:
            load.wait()
        upstream_sum(i, pair, captions, dy, dyl)
        if i == 3:
            keep(dy, dy_hbm)
            keep(dyl, dyl_hbm)

    def project(j):
        if j == 0:
            proj[832:880, :] = jnp.zeros((48, 2304), bf)
        value = dot(normed[...], unit(g2, j), 1, 0)
        for c in (0, 1):
            at = column(0, j, c)
            part = value[:, c * 384 : (c + 1) * 384]
            if at < 768:
                part = part + vec_out[2:3, at : at + 384]
            elif at >= 1536:
                part = part + vec_out[3:4, at - 1536 : at - 1152]
            proj[0:832, at : at + 384] = part.astype(bf)
        if j == 2:
            keep(proj, proj_hbm)

    def attention(i):
        attend(208 * i, proj, prob, mixed)

    def attended():
        keep(prob, prob_hbm)
        keep(mixed, mixed_hbm)
        wide[...] = dot(mixed[...], unit(g2, 3), 1, 0)

        def second_norm(rows, _):
            value = wide[rows, :] + held[rows, :].astype(f32) + vec_out[4:5, :]
            middle[rows, :] = value
            h, centre, scale = norm_stats(value)
            keep_stats(stat_two, rows, centre, scale)
            two[rows, :] = (h * vec_out[5:6, :] + vec_out[6:7, :]).astype(bf)
            return 0
        row_loop(832, second_norm)
        keep(middle, middle_hbm)
        keep(two, two_hbm)
        keep(stat_two, stat_two_hbm)

    def up(j):
        wide[...] = dot(two[...], unit(g1, j), 1, 0)

        def bend(rows, _):
            for c in (0, 1):
                at = c * 1536 + j * 384
                u = wide[rows, c * 384 : (c + 1) * 384] + vec_out[8 + at // 768 : 9 + at // 768, at % 768 : at % 768 + 384]
                u2 = u * u
                s = 0.5 + 0.5 * jnp.tanh(u * (0.7978845608028654 + 0.035677408136300125 * u2))
                bent = u * s
                active[rows, at : at + 384] = bent.astype(bf)
                slope[rows, at : at + 384] = (s + (1.5957691216057308 + 0.21406444881780074 * u2) * bent * (1.0 - s)).astype(bf)
            return 0
        row_loop(832, bend)
        if j == 3:
            keep(active, active_hbm)
            keep(slope, slope_hbm)

    def raw_down(start, stop):
        def body(z, _):
            grad[z] = dot(active[:, lanes(768 * z, 768)], dyl[...], 0, 0).astype(bf).reshape(2, 2, 4, 48, 768)
            return 0
        lax.fori_loop(start, stop, body, 0)
        if stop == 4:
            keep(grad, grad_hbm)

    def down():
        for n in range(3):
            wide[:, n * 256 : (n + 1) * 256] = dot(
                active[...], g0[:, :, :, :, :, n * 256 : (n + 1) * 256].reshape(3072, 256), 1, 0
            )
        for i in range(4):
            rows = slice(208 * i, 208 * i + 196)
            result[i] = wide[rows, :] + middle[rows, :] + vec_out[7:8, :]
        for i in range(4):
            keep(result.at[i], out_hbm.at[:, i, :])

    def end():
        sends.drain()
        for copy in local:
            copy.wait()

    def finish(n):
        ags[n].finish()
        if n in (1, 3, 5):
            keep((g2, g1, g0)[n // 2], (w2_hbm, w1_hbm, w0_hbm)[n // 2])

    begin()
    stage()
    own(0)
    own(1)
    own(2)
    pad()
    own(3)
    own(4)
    own(5)
    upstream(0)
    arrive(0)
    upstream(1)
    av.rest()
    vectors()
    arrive(1)
    forward(0)
    first()
    arrive(2)
    forward(1)
    upstream(2)
    ags[0].share()
    arrive(3)
    forward(2)
    upstream(3)
    finish(0)
    project(0)
    ags[1].share()
    project(1)
    arrive(4)
    project(2)
    forward(3)
    attention(0)
    ags[2].share()
    attention(1)
    arrive(5)
    attention(2)
    ags[3].share()
    forward(4)
    attention(3)
    finish(1)
    attended()
    forward(5)
    ags[4].share()
    finish(2)
    up(0)
    up(1)
    ags[5].share()
    finish(3)
    up(2)
    up(3)
    raw_down(0, 4)
    finish(4)
    finish(5)
    down()
    end()


def forward(images, pair, captions, weights, vectors):
    dma = pltpu.SemaphoreType.DMA
    vm = pl.BlockSpec(memory_space=VMEM)
    anyspace = pl.BlockSpec(memory_space=pl.ANY)
    S = jax.ShapeDtypeStruct
    kept = [
        S((832, 768), f32), S((832, 768), bf), S((832, 768), bf), S((880, 2304), bf), S((832, 3072), bf), S((832, 768), bf),
        S((832, 768), f32), S((832, 768), bf), S((832, 3072), bf), S((832, 3072), bf), S((832, 768), bf), S((832, 256), f32), S((832, 256), f32), S(UNIT, bf),
    ]
    return pl.pallas_call(
        forward_kernel,
        out_shape=[S(UNIT, bf)] * 3 + kept + [S(images.shape, f32), S((16, 768), f32)],
        in_specs=[anyspace, pl.BlockSpec(memory_space=pltpu.SMEM), anyspace] + [vm] * 5,
        out_specs=[anyspace] * 18 + [vm],
        scratch_shapes=[VMEM(UNIT, bf)] * 3
        + [VMEM((4, 2, 2, 2, 16, 128), f32)]
        + [VMEM((w.shape[0], w.shape[1] // 2), f32) for w in weights]
        + [VMEM(captions.shape, bf), VMEM(images.shape, bf)]
        + [VMEM(s.shape, s.dtype) for s in kept]
        + [VMEM((832, 768), f32), VMEM((4, 196, 768), f32)]
        + [dma((176,)), dma((4, 4)), dma((6, 16)), dma((6, 4)), dma((16,)), dma((4,)), dma((32,))],
        compiler_params=pltpu.CompilerParams(collective_id=0, has_side_effects=True, vmem_limit_bytes=63 << 20),
        name="forward",
    )(images, pair, captions, *weights, vectors)


def backward_kernel(
    vec, w0_hbm, w1_hbm, w2_hbm, dy_hbm, dyl_hbm, normed_hbm, proj_hbm, prob_hbm, mixed_hbm, middle_hbm, two_hbm,
    slope_hbm, held_hbm, stat_one_hbm, stat_two_hbm, grad_hbm,
    r_qkv, r_out, r_up, r_down, r_vec, r_norm, ig_hbm,
    x0, x1, x2, gd, b1, b2, dy, dyl, two, middle, mixed, wide, stats, result, *scratch,
):
    bufs, scratch = [scratch[6 * n : 6 * n + 6] for n in range(7)], scratch[42:]
    vval, vbuf, vz, nbuf, nz, send_sem, red_sem, vsem, nsem, local_sem = scratch
    place = Place()
    place.greet()
    sends = Sends(send_sem)
    count = [0]

    def fetch(hbm, ref):
        copy = pltpu.make_async_copy(hbm, ref, local_sem.at[count[0]])
        count[0] += 1
        copy.start()
        return copy
    got = {}
    puts = []
    reds = [
        Reduce(place, n, group, first, units, bufs[n], sends, red_sem.at[n])
        for n, (group, first, units) in enumerate(
            ((gd, 0, 4), (x0, 0, 2), (x0, 2, 2), (x1, 3, 1), (x1, 0, 1), (x1, 1, 1), (x1, 2, 1))
        )
    ]
    ones = jnp.ones((16, 832), bf)

    def total(ref, at):
        return dot(ones, ref[0:832, lanes(at, 768)], 1, 0)[0:1, :]

    def columns(weight, j):
        low, high = column(weight, j, 0), column(weight, j, 1)
        return jnp.concatenate([b2[0:832, lanes(low, 384)], b2[0:832, lanes(high, 384)]], axis=1)

    def begin():
        vval[12:16, :] = jnp.zeros((4, 768), f32)
        for name, hbm, ref in (
            ("grad", grad_hbm, gd), ("dyl", dyl_hbm, dyl), ("w0", w0_hbm, x0), ("slope", slope_hbm, b2.at[0:832]),
            ("two", two_hbm, two), ("w1", w1_hbm, x1), ("dy", dy_hbm, dy), ("middle", middle_hbm, middle), ("stats", stat_two_hbm, stats),
            ("mixed", mixed_hbm, mixed), ("w2", w2_hbm, x2), ("prob", prob_hbm, b1),
        ):
            got[name] = fetch(hbm, ref)

    def dy_sums():
        vval[7:8, :] = total(dyl, 0)

    def active_grad(start, stop):
        if start == 0:
            got["dyl"].wait()
            got["w0"].wait()
            got["slope"].wait()

        def body(z, _):
            at = lanes(768 * z, 768)
            low = (dot(dyl[...], x0[z].reshape(768, 768), 1, 1) * b2[0:832, at].astype(f32)).astype(bf)
            b2[0:832, at] = low
            vval[pl.ds(8 + z, 1), :] = jnp.sum(low.astype(f32), axis=0, keepdims=True)
            return 0
        lax.fori_loop(start, stop, body, 0)

    def raw_up(start, stop):
        if start == 0:
            got["two"].wait()

        def body(j, _):
            x0[:, :, :, j] = dot(two[...], columns(2, j), 0, 0).astype(bf).reshape(4, 2, 2, 48, 768)
            return 0
        lax.fori_loop(start, stop, body, 0)

    def two_grad(start, stop):
        if start == 0:
            got["w1"].wait()
            wide[...] = dot(columns(2, 0), unit(x1, 0), 1, 1)

        def body(j, _):
            wide[...] += dot(columns(2, j), unit(x1, j), 1, 1)
            return 0
        lax.fori_loop(max(start, 1), stop, body, 0)
        if stop == 4:
            got["proj"] = fetch(proj_hbm, b2.at[:, 0:2304])
            got["normed"] = fetch(normed_hbm, b2.at[0:832, 2304:3072])
    zero = jnp.zeros((8, 768), f32)

    def fold(value):
        return jnp.sum(value.reshape(CHUNK // 8, 8, 768), axis=0)

    def second():
        got["dy"].wait()
        got["middle"].wait()
        got["stats"].wait()

        def second_norm(rows, carry):
            grad = wide[rows, :]
            h, scale = normalized(middle[rows, :], stats, rows)
            e = grad * vec[5:6, :]
            mean = jnp.sum(e, axis=-1, keepdims=True) * (1.0 / 768)
            along = jnp.sum(e * h, axis=-1, keepdims=True) * (1.0 / 768)
            value = dy[rows, :] + scale * (e - mean - h * along)
            dy[rows, :] = value
            low = value.astype(bf)
            two[rows, :] = low
            return carry[0] + fold(grad * h), carry[1] + fold(grad), carry[2] + fold(low.astype(f32))
        sums = row_loop(832, second_norm, (zero, zero, zero))
        for row, part in zip((5, 6, 4), sums):
            vval[row : row + 1, :] = jnp.sum(part, axis=0, keepdims=True)

    def raw_out():
        got["mixed"].wait()
        x1[:, :, :, 3] = dot(mixed[...], two[...], 0, 0).astype(bf).reshape(4, 2, 2, 48, 768)
        got["held"] = fetch(held_hbm, mixed)
        got["stats"] = fetch(stat_one_hbm, stats)

    def mixed_grad():
        got["w2"].wait()
        dyl[...] = dot(two[...], unit(x2, 3), 1, 1).astype(bf)
        got["prob"].wait()
        got["proj"].wait()

    def attention(half, start, stop):
        first = lax.broadcasted_iota(jnp.int32, (208, 128), 1) < 64

        def heads(pair, base):
            rows, deep = pl.ds(base, 208), pl.ds(base, 256)
            at_q, at_k, at_v = lanes(pair * 128, 128), lanes(768 + pair * 128, 128), lanes(1536 + pair * 128, 128)
            q, k, v = b2[rows, at_q], both_heads(b2[deep, at_k], score_scale), both_heads(b2[deep, at_v])
            d = dyl[rows, at_q]
            low = b1[rows, lanes(pair * 512, 512)]
            p = low.astype(f32)
            weighted = p * dot(d, v, 1, 1)
            parts = []
            for h in (0, 1):
                part = slice(h * 256, h * 256 + 256)
                parts.append((weighted[:, part] - p[:, part] * jnp.sum(weighted[:, part], axis=-1, keepdims=True)).astype(bf))
            s = jnp.concatenate(parts, axis=1)
            dk, dv = dot(s, q, 0, 0), dot(low, d, 0, 0)
            b2[rows, at_q] = dot(s, k, 1, 0).astype(bf)
            b2[rows, at_k] = (jnp.where(first, dk[0:208], dk[256:464]) * score_scale).astype(bf)
            b2[rows, at_v] = jnp.where(first, dv[0:208], dv[256:464]).astype(bf)

        def body(i, _):
            for pair in range(3 * half, 3 * half + 3):
                heads(pair, pl.multiple_of(208 * i, 16))
            return 0
        lax.fori_loop(start, stop, body, 0)

    def raw_qkv(j):
        if j == 0:
            got["normed"].wait()
        x1[:, :, :, j] = dot(b2[0:832, 2304:3072], columns(0, j), 0, 0).astype(bf).reshape(4, 2, 2, 48, 768)

    def qkv_sums():
        vval[2:3, :] = total(b2, 0)
        vval[3:4, :] = total(b2, 1536)

    def normed_grad():
        wide[...] = dot(columns(0, 0), unit(x2, 0), 1, 1)
        wide[...] += dot(columns(0, 1), unit(x2, 1), 1, 1)
        wide[...] += dot(columns(0, 2), unit(x2, 2), 1, 1)

    def first():
        got["held"].wait()
        got["stats"].wait()

        def first_norm(rows, carry):
            grad = wide[rows, :]
            h, scale = normalized(mixed[rows, :].astype(f32), stats, rows)
            e = grad * vec[0:1, :]
            mean = jnp.sum(e, axis=-1, keepdims=True) * (1.0 / 768)
            along = jnp.sum(e * h, axis=-1, keepdims=True) * (1.0 / 768)
            dy[rows, :] = dy[rows, :] + scale * (e - mean - h * along)
            return carry[0] + fold(grad * h), carry[1] + fold(grad)
        sums = row_loop(832, first_norm, (zero, zero))
        for row, part in zip((0, 1), sums):
            vval[row : row + 1, :] = jnp.sum(part, axis=0, keepdims=True)
        for i in range(4):
            result[i] = dy[208 * i : 208 * i + 196, :]
            put = pltpu.make_async_copy(result.at[i], ig_hbm.at[:, i, :], local_sem.at[24 + i])
            put.start()
            puts.append(put)

    vsum = SumAll(place, vval, vbuf, vz, sends, vsem)
    nsum = SumFew(place, nbuf, nz, sends, nsem)

    def line(n):
        got["squares"] = got.get("squares", 0.0) + reds[n].line_add(n > 0)

    def vectors():
        got["vsum"] = vsum.total()
        r_vec[...] = got["vsum"]

    def norm():
        nsum.start(got["squares"])

    def emit(n):
        red = reds[n]
        weight, unit0, out = ((3, 0, r_down), (2, 0, r_up), (2, 2, r_up), (1, 0, r_out), (0, 0, r_qkv), (0, 1, r_qkv), (0, 2, r_qkv))[n]
        red.wait(red.swap, 15)
        for j in range(red.swap.shape[0]):
            if weight == 3:
                out[48 * j : 48 * (j + 1), place.col(place.c)] = red.final[place.c * 2 + j]
                out[48 * j : 48 * (j + 1), place.col(1 - place.c)] = red.swap[j]
            else:
                mine = pl.ds(pl.multiple_of(place.c * 24, 8), 24)
                out[:, lanes(column(weight, unit0 + j, place.c), 384)] = red.final[j, mine, :]
                out[:, lanes(column(weight, unit0 + j, 1 - place.c), 384)] = red.swap[j]

    def finish():
        whole = nsum.total()
        r_norm[...] = jnp.zeros((8, 128), f32) + (jnp.sum(whole) + jnp.sum(got["vsum"] * got["vsum"]))

    def end():
        sends.drain()
        for put in puts:
            put.wait()
    begin()
    place.meet()
    got["grad"].wait()
    active_grad(0, 1)
    active_grad(1, 2)
    reds[0].core_go()
    active_grad(2, 4)
    dy_sums()
    reds[0].first_go(2, 1)
    raw_up(0, 2)
    reds[1].core_go()
    raw_up(2, 4)
    reds[0].first_go(3, 0)
    two_grad(0, 1)
    reds[1].first_go()
    reds[2].core_go()
    two_grad(1, 3)
    two_grad(3, 4)
    reds[0].second_go()
    reds[2].first_go()
    second()
    raw_out()
    mixed_grad()
    attention(0, 0, 2)
    reds[3].core_go()
    reds[0].line_go()
    reds[1].second_go()
    attention(0, 2, 4)
    reds[3].first_go()
    raw_qkv(0)
    reds[4].core_go()
    attention(1, 0, 2)
    reds[2].second_go()
    reds[1].line_go()
    reds[4].first_go()
    attention(1, 2, 4)
    raw_qkv(1)
    reds[5].core_go()
    reds[3].second_go()
    reds[2].line_go()
    reds[5].first_go()
    reds[4].second_go()
    raw_qkv(2)
    reds[6].core_go()
    qkv_sums()
    normed_grad()
    reds[5].second_go()
    reds[3].line_go()
    reds[6].first_go()
    reds[4].line_go()
    first()
    reds[5].line_go()
    vsum.step(0)
    reds[6].second_go()
    vsum.step(1)
    line(1)
    reds[6].line_go()
    line(4)
    line(2)
    vsum.step(2)
    line(0)
    line(5)
    line(3)
    vsum.step(3)
    line(6)
    norm()
    nsum.turn()
    emit(5)
    emit(2)
    emit(3)
    emit(4)
    emit(0)
    vectors()
    emit(1)
    emit(6)
    finish()
    end()


def backward(shape, vec, groups, kept, shards):
    dma = pltpu.SemaphoreType.DMA
    vm = pl.BlockSpec(memory_space=VMEM)
    anyspace = pl.BlockSpec(memory_space=pl.ANY)
    S = jax.ShapeDtypeStruct
    bufs = []
    for units, apart in ((4, False), (2, True), (2, True), (1, True), (1, True), (1, True), (1, True)):
        block = (units, 48, 384)
        swap = (units, 24, 384) if apart else (units // 2, 48, 384)
        bufs += [
            VMEM((4, 2, 2) + block, bf), VMEM((4, 2) + block, bf), VMEM((4,) + block, bf), VMEM((3,) + block, bf),
            VMEM(block, f32), VMEM(swap, f32),
        ]
    return pl.pallas_call(
        backward_kernel,
        out_shape=[S(s, f32) for s in shards] + [S((16, 768), f32), S((8, 128), f32), S(shape, f32)],
        in_specs=[vm] + [anyspace] * 16,
        out_specs=[vm] * 6 + [anyspace],
        scratch_shapes=[VMEM(UNIT, bf)] * 4
        + [
            VMEM((832, 3072), bf), VMEM((880, 3072), bf), VMEM((832, 768), f32), VMEM((832, 768), bf), VMEM((832, 768), bf),
            VMEM((832, 768), f32), VMEM((832, 768), bf), VMEM((832, 768), f32), VMEM((832, 256), f32), VMEM((4, 196, 768), f32),
        ]
        + bufs
        + [VMEM((16, 768), f32), VMEM((3, 16, 768), f32), VMEM((4, 16, 768), f32)]
        + [VMEM((8, 8, 128), f32), VMEM((4, 8, 128), f32)]
        + [dma((168,)), dma((7, 16)), dma((7,)), dma((12,)), dma((28,))],
        compiler_params=pltpu.CompilerParams(collective_id=1, has_side_effects=True, vmem_limit_bytes=62 << 20),
        name="backward",
    )(vec, *groups, *kept)


def update_kernel(squares, vsum, *refs):
    loads, stores, norm_out = refs[0:21], refs[21:43], refs[43]
    held, made, wide, sems = refs[44:65], refs[65:85], refs[85], refs[86]
    moves = [pltpu.make_async_copy(s, t, sems.at[n]) for n, (s, t) in enumerate(zip(loads, held))]
    for move in moves:
        move.start()
    norm = jnp.sqrt(squares[0:1, 0:1])
    norm_out[...] = norm
    factor = clip_limit / jnp.maximum(norm, clip_limit)
    start = 24 * lax.axis_index("dev")
    wide[:, 0:768] = vsum[...]
    wide[:, 768:896] = jnp.zeros((16, 128), f32)
    window = wide[:, lanes((start // 128) * 128, 256)]
    shard = pltpu.roll(window, 256 - start % 128, 1)[0:12, 0:24]
    puts = []

    def put(ref, n):
        move = pltpu.make_async_copy(ref, stores[n], sems.at[21 + n])
        move.start()
        puts.append(move)
    for n in range(2):
        moves[n].wait()
        put(held[n], n)
    for n in range(5):
        rates = (rate_matrix, decay_matrix) if n < 4 else (rate_vector, 0.0)
        own = range(2 + 4 * n, 6 + 4 * n if n < 4 else 21)
        for m in own:
            moves[m].wait()
        values = [held[m][...] for m in own]
        master, first, second = values[:3]
        parts = adam_update(master, values[3] if n < 4 else shard, first, second, factor, *rates)
        for k in range(4):
            made[4 * n + k][...] = parts[k]
            put(made[4 * n + k], 2 + 4 * n + k)
    for move in puts:
        move.wait()


def update(squares, vsum, grads, masters, first, second, kept):
    vm = pl.BlockSpec(memory_space=VMEM)
    anyspace = pl.BlockSpec(memory_space=pl.ANY)
    S = jax.ShapeDtypeStruct
    loads = list(kept)
    for n in range(5):
        loads += [masters[n], first[n], second[n]] + ([grads[n]] if n < 4 else [])
    made = [m.shape for m in masters for _ in range(4)]
    return pl.pallas_call(
        update_kernel,
        out_shape=[S(a.shape, f32) for a in kept] + [S(m, f32) for m in made] + [S((1, 1), f32)],
        in_specs=[vm] * 2 + [anyspace] * 21,
        out_specs=[anyspace] * 22 + [vm],
        scratch_shapes=[VMEM(a.shape, f32) for a in loads] + [VMEM(m, f32) for m in made]
        + [VMEM((16, 896), f32), pltpu.SemaphoreType.DMA((43,))],
        compiler_params=pltpu.CompilerParams(vmem_limit_bytes=62 << 20),
        name="update",
    )(squares, vsum, *loads)


def local_wide(
    images,
    pair_matrix,
    caption_grads,
    qkv_weight,
    out_weight,
    up_weight,
    down_weight,
    vector_rows,
    first_qkv,
    first_out,
    first_up,
    first_down,
    first_vectors,
    second_qkv,
    second_out,
    second_up,
    second_down,
    second_vectors,
):
    image_count, patches, model_width = images.shape
    row_count = image_count * patches
    head_count = model_width // HD
    qkv_low = qkv_weight.astype(jnp.bfloat16)
    out_low = out_weight.astype(jnp.bfloat16)
    up_low = up_weight.astype(jnp.bfloat16)
    down_low = down_weight.astype(jnp.bfloat16)
    vector_low = vector_rows.astype(jnp.bfloat16)
    gathered = (
        lax.all_gather(qkv_low, "dev", axis=0, tiled=True),
        lax.all_gather(out_low, "dev", axis=0, tiled=True),
        lax.all_gather(up_low, "dev", axis=0, tiled=True),
        lax.all_gather(down_low, "dev", axis=0, tiled=True),
        lax.all_gather(vector_low, "dev", axis=1, tiled=True),
    )
    result, unused_values = forward_pass(gathered, images)
    output = result.reshape(image_count, patches, model_width)
    gathered_again = (
        lax.all_gather(qkv_low, "dev", axis=0, tiled=True),
        lax.all_gather(out_low, "dev", axis=0, tiled=True),
        lax.all_gather(up_low, "dev", axis=0, tiled=True),
        lax.all_gather(down_low, "dev", axis=0, tiled=True),
        lax.all_gather(vector_low, "dev", axis=1, tiled=True),
    )
    qkv_full, out_full, up_full, down_full, vector_again = gathered_again
    vector_full = vector_again.astype(jnp.float32)
    recomputed, kept_values = forward_pass(gathered_again, images)
    (
        flat_inputs,
        normed_low,
        queries,
        keys_all,
        values_all,
        probabilities,
        prob_low,
        mixed_low,
        middle,
        normed_two_low,
        upward,
        active_low,
    ) = kept_values
    caption_flat = caption_grads.reshape(caption_grads.shape[0], patches * model_width)
    upstream = jnp.dot(
        pair_matrix.astype(jnp.bfloat16), caption_flat, preferred_element_type=jnp.float32
    ).reshape(row_count, model_width)
    down_grad_low = upstream.astype(jnp.bfloat16)
    raw_down = contract_first(active_low, down_grad_low)
    bias_down_grad = jnp.sum(down_grad_low.astype(jnp.float32), axis=0)
    active_grad = contract_last(down_grad_low, down_full)
    gelu_value, gelu_pull = jax.vjp(gelu_tanh, upward)
    upward_grad_low = gelu_pull(active_grad)[0].astype(jnp.bfloat16)
    raw_up = contract_first(normed_two_low, upward_grad_low)
    bias_up_grad = jnp.sum(upward_grad_low.astype(jnp.float32), axis=0)
    normed_two_grad = contract_last(upward_grad_low, up_full)
    second_norm_value, second_norm_pull = jax.vjp(
        layer_norm, middle, vector_full[5], vector_full[6]
    )
    middle_norm_grad, gain_two_grad, shift_two_grad = second_norm_pull(normed_two_grad)
    middle_grad = upstream + middle_norm_grad
    attended_low = middle_grad.astype(jnp.bfloat16)
    raw_out = contract_first(mixed_low, attended_low)
    bias_out_grad = jnp.sum(attended_low.astype(jnp.float32), axis=0)
    mixed_grad_low = (
        contract_last(attended_low, out_full)
        .astype(jnp.bfloat16)
        .reshape(image_count, patches, head_count, HD)
    )
    prob_grad = jnp.einsum(
        "bqhd,bkhd->bhqk", mixed_grad_low, values_all, preferred_element_type=jnp.float32
    )
    value_grad = jnp.einsum(
        "bhqk,bqhd->bkhd", prob_low, mixed_grad_low, preferred_element_type=jnp.float32
    )
    score_grad = probabilities * (
        prob_grad - jnp.sum(probabilities * prob_grad, axis=-1, keepdims=True)
    )
    score_grad_low = score_grad.astype(jnp.bfloat16)
    query_grad = (
        jnp.einsum("bhqk,bkhd->bqhd", score_grad_low, keys_all, preferred_element_type=jnp.float32)
        * score_scale
    )
    key_grad = (
        jnp.einsum("bhqk,bqhd->bkhd", score_grad_low, queries, preferred_element_type=jnp.float32)
        * score_scale
    )
    projected_grad_low = (
        jnp.stack([query_grad, key_grad, value_grad], axis=2)
        .astype(jnp.bfloat16)
        .reshape(row_count, 3 * model_width)
    )
    raw_qkv = contract_first(normed_low, projected_grad_low)
    bias_qkv_grad = jnp.sum(projected_grad_low.astype(jnp.float32), axis=0)
    normed_grad = contract_last(projected_grad_low, qkv_full)
    first_norm_value, first_norm_pull = jax.vjp(
        layer_norm, flat_inputs, vector_full[0], vector_full[1]
    )
    inputs_norm_grad, gain_one_grad, shift_one_grad = first_norm_pull(normed_grad)
    input_grads = (middle_grad + inputs_norm_grad).reshape(image_count, patches, model_width)
    small_rows = jnp.stack(
        [
            gain_one_grad,
            shift_one_grad,
            bias_qkv_grad[:model_width],
            bias_qkv_grad[2 * model_width :],
            bias_out_grad,
            gain_two_grad,
            shift_two_grad,
            bias_down_grad,
        ]
    )
    raw_vectors = jnp.concatenate([small_rows, bias_up_grad.reshape(-1, model_width)], axis=0)
    qkv_shard, out_shard, up_shard, down_shard, vector_shard = (
        lax.psum_scatter(raw_qkv, "dev", scatter_dimension=0, tiled=True),
        lax.psum_scatter(raw_out, "dev", scatter_dimension=0, tiled=True),
        lax.psum_scatter(raw_up, "dev", scatter_dimension=0, tiled=True),
        lax.psum_scatter(raw_down, "dev", scatter_dimension=0, tiled=True),
        lax.psum_scatter(raw_vectors, "dev", scatter_dimension=1, tiled=True),
    )
    local_squares = (
        jnp.sum(qkv_shard * qkv_shard)
        + jnp.sum(out_shard * out_shard)
        + jnp.sum(up_shard * up_shard)
        + jnp.sum(down_shard * down_shard)
        + jnp.sum(vector_shard * vector_shard)
    )
    grad_norm = jnp.sqrt(lax.psum(local_squares, "dev"))
    factor = clip_limit / jnp.maximum(grad_norm, clip_limit)
    qkv_parts = adam_update(
        qkv_weight, qkv_shard, first_qkv, second_qkv, factor, rate_matrix, decay_matrix
    )
    out_parts = adam_update(
        out_weight, out_shard, first_out, second_out, factor, rate_matrix, decay_matrix
    )
    up_parts = adam_update(
        up_weight, up_shard, first_up, second_up, factor, rate_matrix, decay_matrix
    )
    down_parts = adam_update(
        down_weight, down_shard, first_down, second_down, factor, rate_matrix, decay_matrix
    )
    vector_parts = adam_update(
        vector_rows, vector_shard, first_vectors, second_vectors, factor, rate_vector, 0.0
    )
    return (
        output,
        input_grads,
        grad_norm,
        qkv_parts[0],
        qkv_parts[1],
        qkv_parts[2],
        qkv_parts[3],
        out_parts[0],
        out_parts[1],
        out_parts[2],
        out_parts[3],
        up_parts[0],
        up_parts[1],
        up_parts[2],
        up_parts[3],
        down_parts[0],
        down_parts[1],
        down_parts[2],
        down_parts[3],
        vector_parts[0],
        vector_parts[1],
        vector_parts[2],
        vector_parts[3],
    )


def local_slice(
    images,
    pair_matrix,
    caption_grads,
    qkv_weight,
    out_weight,
    up_weight,
    down_weight,
    vector_rows,
    first_qkv,
    first_out,
    first_up,
    first_down,
    first_vectors,
    second_qkv,
    second_out,
    second_up,
    second_down,
    second_vectors,
):
    weights = (qkv_weight, out_weight, up_weight, down_weight)
    results = forward(images.transpose(1, 0, 2), pair_matrix, caption_grads, weights, vector_rows)
    groups, kept, output, vector_full = results[0:3], results[3:17], results[17], results[18]
    shapes = [w.shape for w in weights]
    qkv_shard, out_shard, up_shard, down_shard, vector_sum, squares, input_grads = backward(
        output.shape, vector_full, groups, (*kept[:8], *kept[9:]), shapes
    )
    masters = (*weights, vector_rows)
    first = (first_qkv, first_out, first_up, first_down, first_vectors)
    second = (second_qkv, second_out, second_up, second_down, second_vectors)
    shards = (qkv_shard, out_shard, up_shard, down_shard)
    output, input_grads, *parts, norm = update(squares, vector_sum, shards, masters, first, second, (output, input_grads))
    return (output.transpose(1, 0, 2), input_grads.transpose(1, 0, 2), norm[0, 0], *parts)


def solution(mesh):
    fits = mesh.shape["dev"] == 32
    return jax.shard_map(
        local_slice if fits else local_wide,
        mesh=mesh,
        in_specs=(
            P("dev", None, None),
            P("dev", None),
            P("dev", None, None),
            P("dev", None),
            P("dev", None),
            P("dev", None),
            P("dev", None),
            P(None, "dev"),
            P("dev", None),
            P("dev", None),
            P("dev", None),
            P("dev", None),
            P(None, "dev"),
            P("dev", None),
            P("dev", None),
            P("dev", None),
            P("dev", None),
            P(None, "dev"),
        ),
        out_specs=(
            P("dev", None, None),
            P("dev", None, None),
            P(),
            P("dev", None),
            P("dev", None),
            P("dev", None),
            P("dev", None),
            P("dev", None),
            P("dev", None),
            P("dev", None),
            P("dev", None),
            P("dev", None),
            P("dev", None),
            P("dev", None),
            P("dev", None),
            P("dev", None),
            P("dev", None),
            P("dev", None),
            P("dev", None),
            P(None, "dev"),
            P(None, "dev"),
            P(None, "dev"),
            P(None, "dev"),
        ),
        check_vma=False,
    )
```

```python
import functools

import jax
import jax.numpy as jnp
from jax import lax
from jax.experimental import pallas as pl
from jax.experimental.pallas import tpu as pltpu
from jax.sharding import PartitionSpec as P

HD = 64
STEP = 10


norm_eps = 1e-06
clip_limit = 1.0
beta_one = 0.9
beta_two = 0.999
adam_eps = 1e-08
rate_matrix = 0.08
rate_vector = 0.5
decay_matrix = 0.1
score_scale = 0.125


def layer_norm(values, gain_row, shift_row):
    centre = jnp.mean(values, axis=-1, keepdims=True)
    offset = values - centre
    spread = jnp.mean(offset * offset, axis=-1, keepdims=True)
    return offset * lax.rsqrt(spread + norm_eps) * gain_row + shift_row


def softmax_rows(scores):
    shifted = scores - jnp.max(scores, axis=-1, keepdims=True)
    weights = jnp.exp(shifted)
    return weights / jnp.sum(weights, axis=-1, keepdims=True)


def gelu_tanh(values):
    return jax.nn.gelu(values, approximate=True)


def contract_last(left_side, right_side):
    return lax.dot_general(
        left_side, right_side, (((1,), (1,)), ((), ())), preferred_element_type=jnp.float32
    )


def contract_first(left_side, right_side):
    return lax.dot_general(
        left_side, right_side, (((0,), (0,)), ((), ())), preferred_element_type=jnp.float32
    )


def forward_pass(gathered, inputs):
    qkv_full, out_full, up_full, down_full, vector_low = gathered
    vector_full = vector_low.astype(jnp.float32)
    image_count, patches, model_width = inputs.shape
    row_count = image_count * patches
    head_count = model_width // HD
    flat_inputs = inputs.astype(jnp.float32).reshape(row_count, model_width)
    normed_low = layer_norm(flat_inputs, vector_full[0], vector_full[1]).astype(jnp.bfloat16)
    bias_qkv = jnp.concatenate([vector_full[2], jnp.zeros_like(vector_full[2]), vector_full[3]])
    projected = jnp.dot(normed_low, qkv_full, preferred_element_type=jnp.float32) + bias_qkv
    projected_low = projected.astype(jnp.bfloat16).reshape(image_count, patches, 3, head_count, HD)
    queries = projected_low[:, :, 0]
    keys_all = projected_low[:, :, 1]
    values_all = projected_low[:, :, 2]
    scores = (
        jnp.einsum("bqhd,bkhd->bhqk", queries, keys_all, preferred_element_type=jnp.float32)
        * score_scale
    )
    probabilities = softmax_rows(scores)
    prob_low = probabilities.astype(jnp.bfloat16)
    mixed_heads = jnp.einsum(
        "bhqk,bkhd->bqhd", prob_low, values_all, preferred_element_type=jnp.float32
    )
    mixed_low = mixed_heads.reshape(row_count, model_width).astype(jnp.bfloat16)
    attended = jnp.dot(mixed_low, out_full, preferred_element_type=jnp.float32) + vector_full[4]
    middle = flat_inputs + attended
    normed_two_low = layer_norm(middle, vector_full[5], vector_full[6]).astype(jnp.bfloat16)
    upward = jnp.dot(normed_two_low, up_full, preferred_element_type=jnp.float32) + vector_full[
        8:
    ].reshape(-1)
    active_low = gelu_tanh(upward).astype(jnp.bfloat16)
    downward = jnp.dot(active_low, down_full, preferred_element_type=jnp.float32) + vector_full[7]
    result = middle + downward
    kept_values = (
        flat_inputs,
        normed_low,
        queries,
        keys_all,
        values_all,
        probabilities,
        prob_low,
        mixed_low,
        middle,
        normed_two_low,
        upward,
        active_low,
    )
    return (result, kept_values)


def adam_update(master, raw_grad, moment_one, moment_two, factor, step_rate, decay_rate):
    clipped = raw_grad * factor
    moment_one_new = beta_one * moment_one + (1.0 - beta_one) * clipped
    moment_two_new = beta_two * moment_two + (1.0 - beta_two) * clipped * clipped
    first_hat = moment_one_new / (1.0 - beta_one**STEP)
    second_hat = moment_two_new / (1.0 - beta_two**STEP)
    master_new = master - step_rate * (
        first_hat / (jnp.sqrt(second_hat) + adam_eps) + decay_rate * master
    )
    return (clipped, master_new, moment_one_new, moment_two_new)


MESH = pl.DeviceIdType.MESH
bf = jnp.bfloat16
f32 = jnp.float32
VMEM = pltpu.VMEM
ROWS = 208
UNIT = (4, 2, 2, 4, 48, 768)
CHUNKS = ((2, 0, 3, 0), (2, 3, 1, 1), (1, 0, 2, 2), (1, 2, 2, 2), (0, 0, 2, 3), (0, 2, 2, 3))


QKV_AT = ((0, 768), (1536, 384), (1152, 1920))


def column(weight, unit, c):
    if weight == 0:
        low, high = QKV_AT[unit]
        return low + c * (high - low)
    return c * (1536 if weight == 2 else 384) + (384 * unit if weight == 2 else 0)


class Place:
    def __init__(self):
        me = lax.axis_index("dev")
        self.me = me
        self.c = me % 2
        self.x = (me // 2) % 2
        self.y = (me // 4) % 2
        self.z = me // 8
        self.q = me // 2
        self.sib = me + 1 - 2 * self.c
        self.xn = me + 2 - 4 * self.x
        self.yn = me + 4 - 8 * self.y
        self.xo = 1 - self.x
        self.yo = 1 - self.y

    def zz(self, k):
        return (self.z + k) % 4

    def zp(self, k):
        return self.zz(k) * 8 + self.me % 8

    def col(self, c):
        return pl.ds(pl.multiple_of(c * 384, 128), 384)

    def greet(self):
        bar = pltpu.get_barrier_semaphore()
        for dev in [self.near(n) for n in range(1, 8)] + [self.zp(1), self.zp(2), self.zp(3)]:
            pl.semaphore_signal(bar, inc=1, device_id=(dev,), device_id_type=MESH)

    def near(self, n):
        return self.z * 8 + (self.me + n) % 8

    def meet(self):
        pl.semaphore_wait(pltpu.get_barrier_semaphore(), 10)


class Sends:
    def __init__(self, sems):
        self.sems = sems
        self.used = 0
        self.open = []

    def go(self, src, dst, recv, dev):
        copy = pltpu.make_async_remote_copy(
            src_ref=src, dst_ref=dst, send_sem=self.sems.at[self.used], recv_sem=recv,
            device_id=(dev,), device_id_type=MESH,
        )
        self.used += 1
        copy.start()
        self.open.append(copy)

    def drain(self):
        for copy in self.open:
            copy.wait_send()
        self.open = []


def await_recv(place, ref, recv, spare):
    pltpu.make_async_remote_copy(
        src_ref=ref, dst_ref=ref, send_sem=spare, recv_sem=recv,
        device_id=(place.sib,), device_id_type=MESH,
    ).wait_recv()


class Gather:
    def __init__(self, place, chunk, group, sends, rail_sem, sib_sem):
        self.p, self.group, self.sends = place, group, sends
        self.number = chunk
        _, self.first, self.count, _ = CHUNKS[chunk]
        self.rail_sem, self.sib_sem = rail_sem.at[chunk], sib_sem.at[chunk]

    def at(self, k, y, x):
        return self.group.at[self.p.zz(k), y, x, pl.ds(self.first, self.count), :, self.p.col(self.p.c)]

    def sem(self, k, y, x):
        return self.rail_sem.at[self.p.zz(k) * 4 + y * 2 + x]

    def go(self, k, y, x, dev):
        ref = self.at(k, y, x)
        self.sends.go(ref, ref, self.sem(k, y, x), dev)

    def wait(self, k, y, x):
        await_recv(self.p, self.at(k, y, x), self.sem(k, y, x), self.sends.sems.at[0])

    def own(self):
        p = self.p
        for k in (2, 1, 3):
            self.go(0, p.y, p.x, p.zp(k))
        self.plane(0)

    def turn(self, k):
        return (k + self.number) % 2 == 0

    def plane(self, k):
        p = self.p
        for dev in (p.xn, p.yn) if self.turn(k) else (p.yn, p.xn):
            self.go(k, p.y, p.x, dev)

    def arrive(self, k):
        self.wait(k, self.p.y, self.p.x)
        self.plane(k)

    def forward(self, k):
        p = self.p
        if self.turn(k):
            self.wait(k, p.y, p.xo)
            self.go(k, p.y, p.xo, p.yn)
        else:
            self.wait(k, p.yo, p.x)
            self.go(k, p.yo, p.x, p.xn)


    def level(self, k, c):
        return self.group.at[self.p.zz(k), :, :, pl.ds(self.first, self.count), :, self.p.col(c)]

    def share(self):
        p = self.p
        for k in (0, 1, 3, 2):
            if self.turn(k):
                self.wait(k, p.yo, p.x)
            else:
                self.wait(k, p.y, p.xo)
            self.wait(k, p.yo, p.xo)
            ref = self.level(k, p.c)
            self.sends.go(ref, ref, self.sib_sem.at[p.zz(k)], p.sib)

    def finish(self):
        p = self.p
        for k in (0, 1, 3, 2):
            await_recv(p, self.level(k, 1 - p.c), self.sib_sem.at[p.zz(k)], self.sends.sems.at[0])


class GatherVectors:
    def __init__(self, place, slots, sends, rail_sem, sib_sem):
        self.p, self.slots, self.sends, self.rail_sem, self.sib_sem = place, slots, sends, rail_sem, sib_sem

    def at(self, k, y, x, c):
        return self.slots.at[self.p.zz(k), y, x, c]

    def sem(self, k, y, x):
        return self.rail_sem.at[self.p.zz(k) * 4 + y * 2 + x]

    def go(self, k, y, x, dev):
        ref = self.at(k, y, x, self.p.c)
        self.sends.go(ref, ref, self.sem(k, y, x), dev)

    def wait(self, k, y, x):
        await_recv(self.p, self.at(k, y, x, self.p.c), self.sem(k, y, x), self.sends.sems.at[0])

    def own(self):
        p = self.p
        for k in (1, 2, 3):
            self.go(0, p.y, p.x, p.zp(k))
        self.go(0, p.y, p.x, p.xn)
        self.go(0, p.y, p.x, p.yn)

    def rest(self):
        p = self.p
        for k in range(4):
            if k:
                self.wait(k, p.y, p.x)
                self.go(k, p.y, p.x, p.xn)
                self.go(k, p.y, p.x, p.yn)
        for k in range(4):
            self.wait(k, p.y, p.xo)
            self.go(k, p.y, p.xo, p.yn)
        for k in range(4):
            self.wait(k, p.yo, p.x)
            self.wait(k, p.yo, p.xo)
            ref = self.slots.at[p.zz(k), :, :, p.c]
            self.sends.go(ref, ref, self.sib_sem.at[p.zz(k)], p.sib)
        for k in range(4):
            await_recv(p, self.slots.at[p.zz(k), :, :, 1 - p.c], self.sib_sem.at[p.zz(k)], self.sends.sems.at[0])


def join_vectors(slots):
    lane = lax.broadcasted_iota(jnp.int32, (16, 128), 1)
    tiles = [jnp.zeros((16, 128), f32) for _ in range(7)]
    for d in range(32):
        tile, off = (24 * d) // 128, (24 * d) % 128
        held = slots[d // 8, (d // 4) % 2, (d // 2) % 2, d % 2]
        turned = pltpu.roll(held, off, 1) if off else held
        tiles[tile] = jnp.where((lane >= off) & (lane < off + 24), turned, tiles[tile])
        if off + 24 > 128:
            tiles[tile + 1] = jnp.where(lane < off - 104, turned, tiles[tile + 1])
    return jnp.concatenate(tiles[:6], axis=1).astype(bf).astype(f32)


ORDER = (2, 1, 3, 0)


class Reduce:
    def __init__(self, place, turn, grad, first, count, bufs, sends, sems):
        self.p, self.parity, self.grad, self.first, self.count = place, turn, grad, first, count
        self.cb, self.pb, self.qb, self.zb, self.final, self.swap = bufs
        self.sends, self.sems = sends, sems

    def at(self, z, y, x, c):
        return (z, y, x, pl.ds(self.first, self.count), slice(None), self.p.col(c))

    def turn(self, k):
        return (k + self.parity) % 2 == 0

    def wait(self, ref, n):
        await_recv(self.p, ref, self.sems.at[n], self.sends.sems.at[0])

    def go(self, index, dst, n, dev):
        self.sends.go(self.grad.at[index], dst, self.sems.at[n], dev)

    def add(self, index, buf, at):
        self.grad[index] = self.grad[index] + buf[at]

    def core_go(self, *ks):
        every = slice(None)
        for k in ks or ORDER:
            self.go(self.at(self.p.zz(k), every, every, 1 - self.p.c), self.cb.at[k], k, self.p.sib)

    def first_go(self, *ks):
        p, every = self.p, slice(None)
        for k in ks or ORDER:
            self.wait(self.cb.at[k], k)
            z = p.zz(k)

            def body(i, _, k=k, z=z):
                self.add(self.at(z, i // 2, i % 2, p.c), self.cb, (k, i // 2, i % 2))
                return 0
            lax.fori_loop(0, 4, body, 0)
            if self.turn(k):
                self.go(self.at(z, p.yo, every, p.c), self.pb.at[k], 4 + k, p.yn)
            else:
                self.go(self.at(z, every, p.xo, p.c), self.pb.at[k], 4 + k, p.xn)

    def second_go(self, *ks):
        p = self.p
        for k in ks or ORDER:
            self.wait(self.pb.at[k], 4 + k)
            z = p.zz(k)
            for o in (0, 1):
                y, x = (p.y, o) if self.turn(k) else (o, p.x)
                self.add(self.at(z, y, x, p.c), self.pb, (k, o))
            if self.turn(k):
                self.go(self.at(z, p.y, p.xo, p.c), self.qb.at[k], 8 + k, p.xn)
            else:
                self.go(self.at(z, p.yo, p.x, p.c), self.qb.at[k], 8 + k, p.yn)

    def line_go(self):
        p = self.p
        for k in ORDER:
            self.wait(self.qb.at[k], 8 + k)
            self.add(self.at(p.zz(k), p.y, p.x, p.c), self.qb, (k,))
            if k:
                self.go(self.at(p.zz(k), p.y, p.x, p.c), self.zb.at[k - 1], 11 + k, p.zp(k))

    def line_add(self, rows_apart):
        p = self.p
        for k in (1, 2, 3):
            self.wait(self.zb.at[k - 1], 11 + k)
        total = self.grad[self.at(p.z, p.y, p.x, p.c)].astype(f32)
        for k in range(3):
            total = total + self.zb[k].astype(f32)
        self.final[...] = total
        if rows_apart:
            ref = self.final.at[:, pl.ds(pl.multiple_of((1 - p.c) * 24, 8), 24), :]
        else:
            ref = self.final.at[pl.ds((1 - p.c) * (self.count // 2), self.count // 2)]
        self.sends.go(ref, self.swap, self.sems.at[15], p.sib)
        square = total * total
        tile = jnp.sum(square.reshape(self.count * 6, 8, 384), axis=0)
        return tile[:, :128] + tile[:, 128:256] + tile[:, 256:384]


class SumAll:
    def __init__(self, place, value, buf, zbuf, sends, sems):
        self.p, self.value, self.buf, self.zbuf, self.sends, self.sems = place, value, buf, zbuf, sends, sems

    def go(self, n):
        self.sends.go(self.value, self.buf.at[n], self.sems.at[n], (self.p.sib, self.p.xn, self.p.yn)[n])
        self.copy = self.sends.open.pop()

    def add(self, n):
        await_recv(self.p, self.buf.at[n], self.sems.at[n], self.sends.sems.at[0])
        self.copy.wait_send()
        self.value[...] = self.value[...] + self.buf[n]

    def step(self, n):
        p = self.p
        if n:
            self.add(n - 1)
        if n < 3:
            self.go(n)
        else:
            self.zbuf[p.z] = self.value[...]
            for k in (2, 1, 3):
                self.sends.go(self.value, self.zbuf.at[p.z], self.sems.at[3 + p.z], p.zp(k))

    def total(self):
        p = self.p
        for k in (1, 2, 3):
            await_recv(p, self.zbuf.at[p.zz(k)], self.sems.at[3 + p.zz(k)], self.sends.sems.at[0])
        return (self.zbuf[0] + self.zbuf[1]) + (self.zbuf[2] + self.zbuf[3])


class SumFew:
    def __init__(self, place, buf, zbuf, sends, sems):
        self.p, self.buf, self.zbuf, self.sends, self.sems = place, buf, zbuf, sends, sems

    def start(self, value):
        p = self.p
        mine = p.me % 8
        self.buf[mine] = value
        for n in range(1, 8):
            self.sends.go(self.buf.at[mine], self.buf.at[mine], self.sems.at[mine], p.near(n))

    def turn(self):
        p = self.p
        for n in range(1, 8):
            slot = (p.me + n) % 8
            await_recv(p, self.buf.at[slot], self.sems.at[slot], self.sends.sems.at[0])
        self.zbuf[p.z] = jnp.sum(self.buf[...], axis=0)
        for k in (2, 1, 3):
            self.sends.go(self.zbuf.at[p.z], self.zbuf.at[p.z], self.sems.at[8 + p.z], p.zp(k))

    def total(self):
        p = self.p
        for k in (1, 2, 3):
            await_recv(p, self.zbuf.at[p.zz(k)], self.sems.at[8 + p.zz(k)], self.sends.sems.at[0])
        return (self.zbuf[0] + self.zbuf[1]) + (self.zbuf[2] + self.zbuf[3])


def dot(a, b, ca, cb):
    return lax.dot_general(a, b, (((ca,), (cb,)), ((), ())), preferred_element_type=f32)


def unit(group, j):
    return group[:, :, :, j].reshape(768, 768)


def lanes(start, size):
    return pl.ds(pl.multiple_of(start, 128), size)


CHUNK = 32


def row_loop(count, body, init=0, unroll=2):
    def step(i, carry):
        return body(pl.ds(pl.multiple_of(i * CHUNK, CHUNK), CHUNK), carry)
    return lax.fori_loop(0, count // CHUNK, step, init, unroll=unroll)


def norm_stats(rows):
    centre = jnp.sum(rows, axis=-1, keepdims=True) * (1.0 / 768)
    offset = rows - centre
    spread = jnp.sum(offset * offset, axis=-1, keepdims=True) * (1.0 / 768)
    scale = lax.rsqrt(spread + norm_eps)
    return offset * scale, centre, scale


def keep_stats(stats, rows, centre, scale):
    stats[rows, 0:128] = jnp.broadcast_to(centre, (CHUNK, 128))
    stats[rows, 128:256] = jnp.broadcast_to(scale, (CHUNK, 128))


def normalized(values, stats, rows):
    scale = stats[rows, 128:129]
    return (values - stats[rows, 0:1]) * scale, scale


def pad_images(images, held):
    for i in range(4):
        held[208 * i + 192 : 208 * i + 208, :] = jnp.zeros((16, 768), bf)
        held[208 * i : 208 * i + 196, :] = images[:, i, :]


def upstream_sum(i, pair, captions, dy, dy_low):
    dy[208 * i + 192 : 208 * i + 208, :] = jnp.zeros((16, 768), f32)
    dy_low[208 * i + 192 : 208 * i + 208, :] = jnp.zeros((16, 768), bf)
    weights = [pair[i, c].astype(f32) for c in range(14)]

    def body(j, _):
        col = lanes(j * 128, 128)
        total = weights[0] * captions[0, :, col].astype(f32)
        for c in range(1, 14):
            total = total + weights[c] * captions[c, :, col].astype(f32)
        dy[208 * i : 208 * i + 196, col] = total
        dy_low[208 * i : 208 * i + 196, col] = total.astype(bf)
        return 0
    lax.fori_loop(0, 6, body, 0)


def head_masks(value):
    lane = lax.broadcasted_iota(jnp.int32, (1, 128), 1)
    return jnp.where(lane < 64, value, 0.0).astype(bf), jnp.where(lane < 64, 0.0, value).astype(bf)


def both_heads(rows, value=1.0):
    first, second = head_masks(value)
    return jnp.concatenate([rows * first, rows * second], axis=0)


def attend(base, proj, prob, mixed):
    valid = lax.broadcasted_iota(jnp.int32, (208, 128), 1) < 68

    def body(pair, _):
        rows, wide = pl.ds(base, 208), pl.ds(base, 256)
        q = proj[rows, lanes(pair * 128, 128)]
        k = both_heads(proj[wide, lanes(768 + pair * 128, 128)], score_scale)
        v = both_heads(proj[wide, lanes(1536 + pair * 128, 128)])
        scores = dot(q, k, 1, 1)
        lows = []
        for h in (0, 1):
            near = scores[:, h * 256 : h * 256 + 128]
            far = jnp.where(valid, scores[:, h * 256 + 128 : h * 256 + 256], -1e30)
            top = jnp.max(jnp.maximum(near, far), axis=-1, keepdims=True)
            near, far = jnp.exp(near - top), jnp.exp(far - top)
            factor = 1.0 / jnp.sum(near + far, axis=-1, keepdims=True)
            lows += [(near * factor).astype(bf), (far * factor).astype(bf)]
        low = jnp.concatenate(lows, axis=1)
        prob[rows, lanes(pair * 512, 512)] = low
        mixed[rows, lanes(pair * 128, 128)] = dot(low, v, 1, 0).astype(bf)
        return 0
    lax.fori_loop(0, 6, body, 0, unroll=2)


def own_block(place, shard, stage, group, chunk):
    p = place
    _, first, count, weight = chunk
    low = p.c == 0
    for n in range(count):
        if weight == 3:
            rows = slice(48 * n, 48 * n + 48)
            block = jnp.where(p.c == first // 2, shard[rows, p.col(p.c)], stage[rows, :])
        else:
            j = first + n if weight != 1 else 0
            mine = shard[:, lanes(column(weight, j, p.c), 384)]
            other = stage[:, j * 384 : (j + 1) * 384]
            block = jnp.concatenate([jnp.where(low, mine, other), jnp.where(low, other, mine)], axis=0)
        group[p.z, p.y, p.x, first + n, :, p.col(p.c)] = block.astype(bf)


def forward_kernel(
    images_hbm, pair, captions_hbm, qkv_in, out_in, up_in, down_in, vec_in,
    w0_hbm, w1_hbm, w2_hbm, dy_hbm, dyl_hbm, normed_hbm, proj_hbm, prob_hbm, mixed_hbm, middle_hbm, two_hbm,
    active_hbm, slope_hbm, held_hbm, stat_one_hbm, stat_two_hbm, grad_hbm, out_hbm, vec_out,
    g0, g1, g2, slots, s0, s1, s2, s3, captions, images, dy, dyl, normed, proj, prob, mixed, middle, two, active, slope, held, stat_one, stat_two, grad,
    wide, result, send_sem, stage_sem, rail_sem, sib_sem, vrail_sem, vsib_sem, local_sem,
):
    place = Place()
    place.greet()
    sends = Sends(send_sem)
    groups = (g0, g1, g2)
    shards, stages = (qkv_in, out_in, up_in, down_in), (s0, s1, s2, s3)
    local = []

    def keep(ref, hbm):
        copy = pltpu.make_async_copy(ref, hbm, local_sem.at[len(local)])
        copy.start()
        local.append(copy)
    fetch = pltpu.make_async_copy(images_hbm, images, local_sem.at[30])
    load = pltpu.make_async_copy(captions_hbm, captions, local_sem.at[31])
    ags = [Gather(place, n, groups[CHUNKS[n][0]], sends, rail_sem, sib_sem) for n in range(6)]
    av = GatherVectors(place, slots, sends, vrail_sem, vsib_sem)

    def begin():
        fetch.start()
        load.start()
        slots[place.z, place.y, place.x, place.c] = jnp.zeros((16, 128), f32)
        slots[place.z, place.y, place.x, place.c, 0:12, 0:24] = vec_in[...]
        place.meet()

    def stage():
        for weight, units in enumerate((3, 1, 4, 1)):
            for j in range(units):
                sends.go(
                    shards[weight].at[:, lanes(column(weight, j, 1 - place.c), 384)],
                    stages[weight].at[:, j * 384 : (j + 1) * 384], stage_sem.at[weight, j], place.sib,
                )
        av.own()

    def own(n):
        group, first, _, weight = CHUNKS[n]
        if n in (0, 1, 2, 4):
            for j in range(stages[weight].shape[1] // 384):
                await_recv(place, stages[weight].at[:, j * 384 : (j + 1) * 384], stage_sem.at[weight, j], send_sem.at[0])
        own_block(place, shards[weight], stages[weight], groups[group], CHUNKS[n])
        ags[n].own()

    def arrive(n):
        for k in (1, 3, 2):
            ags[n].arrive(k)

    def forward(n):
        for k in (0, 1, 3, 2):
            ags[n].forward(k)

    def pad():
        fetch.wait()
        pad_images(images, held)
        keep(held, held_hbm)

    def vectors():
        vec_out[...] = join_vectors(slots)

    def first():
        def first_norm(rows, _):
            h, centre, scale = norm_stats(held[rows, :].astype(f32))
            keep_stats(stat_one, rows, centre, scale)
            normed[rows, :] = (h * vec_out[0:1, :] + vec_out[1:2, :]).astype(bf)
            return 0
        row_loop(832, first_norm)
        keep(normed, normed_hbm)
        keep(stat_one, stat_one_hbm)

    def upstream(i):
        if i == 0:
            load.wait()
        upstream_sum(i, pair, captions, dy, dyl)
        if i == 3:
            keep(dy, dy_hbm)
            keep(dyl, dyl_hbm)

    def project(j):
        if j == 0:
            proj[832:880, :] = jnp.zeros((48, 2304), bf)
        value = dot(normed[...], unit(g2, j), 1, 0)
        for c in (0, 1):
            at = column(0, j, c)
            part = value[:, c * 384 : (c + 1) * 384]
            if at < 768:
                part = part + vec_out[2:3, at : at + 384]
            elif at >= 1536:
                part = part + vec_out[3:4, at - 1536 : at - 1152]
            proj[0:832, at : at + 384] = part.astype(bf)
        if j == 2:
            keep(proj, proj_hbm)

    def attention(i):
        attend(208 * i, proj, prob, mixed)

    def attended():
        keep(prob, prob_hbm)
        keep(mixed, mixed_hbm)
        wide[...] = dot(mixed[...], unit(g2, 3), 1, 0)

        def second_norm(rows, _):
            value = wide[rows, :] + held[rows, :].astype(f32) + vec_out[4:5, :]
            middle[rows, :] = value
            h, centre, scale = norm_stats(value)
            keep_stats(stat_two, rows, centre, scale)
            two[rows, :] = (h * vec_out[5:6, :] + vec_out[6:7, :]).astype(bf)
            return 0
        row_loop(832, second_norm)
        keep(middle, middle_hbm)
        keep(two, two_hbm)
        keep(stat_two, stat_two_hbm)

    def up(j):
        wide[...] = dot(two[...], unit(g1, j), 1, 0)

        def bend(rows, _):
            for c in (0, 1):
                at = c * 1536 + j * 384
                u = wide[rows, c * 384 : (c + 1) * 384] + vec_out[8 + at // 768 : 9 + at // 768, at % 768 : at % 768 + 384]
                u2 = u * u
                s = 0.5 + 0.5 * jnp.tanh(u * (0.7978845608028654 + 0.035677408136300125 * u2))
                bent = u * s
                active[rows, at : at + 384] = bent.astype(bf)
                slope[rows, at : at + 384] = (s + (1.5957691216057308 + 0.21406444881780074 * u2) * bent * (1.0 - s)).astype(bf)
            return 0
        row_loop(832, bend)
        if j == 3:
            keep(active, active_hbm)
            keep(slope, slope_hbm)

    def raw_down(start, stop):
        def body(z, _):
            grad[z] = dot(active[:, lanes(768 * z, 768)], dyl[...], 0, 0).astype(bf).reshape(2, 2, 4, 48, 768)
            return 0
        lax.fori_loop(start, stop, body, 0)
        if stop == 4:
            keep(grad, grad_hbm)

    def down():
        for n in range(3):
            wide[:, n * 256 : (n + 1) * 256] = dot(
                active[...], g0[:, :, :, :, :, n * 256 : (n + 1) * 256].reshape(3072, 256), 1, 0
            )
        for i in range(4):
            rows = slice(208 * i, 208 * i + 196)
            result[i] = wide[rows, :] + middle[rows, :] + vec_out[7:8, :]
        for i in range(4):
            keep(result.at[i], out_hbm.at[:, i, :])

    def end():
        sends.drain()
        for copy in local:
            copy.wait()

    def finish(n):
        ags[n].finish()
        if n in (1, 3, 5):
            keep((g2, g1, g0)[n // 2], (w2_hbm, w1_hbm, w0_hbm)[n // 2])

    begin()
    stage()
    upstream(0)
    own(0)
    own(1)
    own(2)
    own(3)
    pad()
    upstream(1)
    own(4)
    own(5)
    arrive(0)
    av.rest()
    vectors()
    first()
    forward(0)
    upstream(2)
    arrive(1)
    arrive(2)
    ags[0].share()
    upstream(3)
    forward(1)
    finish(0)
    project(0)
    project(1)
    arrive(3)
    project(2)
    attention(0)
    attention(1)
    forward(2)
    arrive(4)
    attention(2)
    ags[1].share()
    attention(3)
    ags[2].share()
    finish(1)
    forward(3)
    arrive(5)
    attended()
    finish(2)
    up(0)
    forward(4)
    ags[3].share()
    up(1)
    finish(3)
    forward(5)
    up(2)
    ags[4].share()
    up(3)
    ags[5].share()
    raw_down(0, 4)
    finish(4)
    finish(5)
    down()
    end()


def forward(images, pair, captions, weights, vectors):
    dma = pltpu.SemaphoreType.DMA
    vm = pl.BlockSpec(memory_space=VMEM)
    anyspace = pl.BlockSpec(memory_space=pl.ANY)
    S = jax.ShapeDtypeStruct
    kept = [
        S((832, 768), f32), S((832, 768), bf), S((832, 768), bf), S((880, 2304), bf), S((832, 3072), bf), S((832, 768), bf),
        S((832, 768), f32), S((832, 768), bf), S((832, 3072), bf), S((832, 3072), bf), S((832, 768), bf), S((832, 256), f32), S((832, 256), f32), S(UNIT, bf),
    ]
    return pl.pallas_call(
        forward_kernel,
        out_shape=[S(UNIT, bf)] * 3 + kept + [S(images.shape, f32), S((16, 768), f32)],
        in_specs=[anyspace, pl.BlockSpec(memory_space=pltpu.SMEM), anyspace] + [vm] * 5,
        out_specs=[anyspace] * 18 + [vm],
        scratch_shapes=[VMEM(UNIT, bf)] * 3
        + [VMEM((4, 2, 2, 2, 16, 128), f32)]
        + [VMEM((w.shape[0], w.shape[1] // 2), f32) for w in weights]
        + [VMEM(captions.shape, bf), VMEM(images.shape, bf)]
        + [VMEM(s.shape, s.dtype) for s in kept]
        + [VMEM((832, 768), f32), VMEM((4, 196, 768), f32)]
        + [dma((176,)), dma((4, 4)), dma((6, 16)), dma((6, 4)), dma((16,)), dma((4,)), dma((32,))],
        compiler_params=pltpu.CompilerParams(collective_id=0, has_side_effects=True, vmem_limit_bytes=63 << 20),
        name="forward",
    )(images, pair, captions, *weights, vectors)


def backward_kernel(
    vec, w0_hbm, w1_hbm, w2_hbm, dy_hbm, dyl_hbm, normed_hbm, proj_hbm, prob_hbm, mixed_hbm, middle_hbm, two_hbm,
    slope_hbm, held_hbm, stat_one_hbm, stat_two_hbm, grad_hbm,
    r_qkv, r_out, r_up, r_down, r_vec, r_norm, ig_hbm,
    x0, x1, x2, gd, b1, b2, dy, dyl, two, middle, mixed, wide, stats, result, *scratch,
):
    bufs, scratch = [scratch[6 * n : 6 * n + 6] for n in range(7)], scratch[42:]
    vval, vbuf, vz, nbuf, nz, send_sem, red_sem, vsem, nsem, local_sem = scratch
    place = Place()
    place.greet()
    sends = Sends(send_sem)
    count = [0]

    def fetch(hbm, ref):
        copy = pltpu.make_async_copy(hbm, ref, local_sem.at[count[0]])
        count[0] += 1
        copy.start()
        return copy
    got = {}
    puts = []
    reds = [
        Reduce(place, n, group, first, units, bufs[n], sends, red_sem.at[n])
        for n, (group, first, units) in enumerate(
            ((gd, 0, 4), (x0, 0, 2), (x0, 2, 2), (x1, 3, 1), (x1, 0, 1), (x1, 1, 1), (x1, 2, 1))
        )
    ]
    ones = jnp.ones((16, 832), bf)

    def total(ref, at):
        return dot(ones, ref[0:832, lanes(at, 768)], 1, 0)[0:1, :]

    def columns(weight, j):
        low, high = column(weight, j, 0), column(weight, j, 1)
        return jnp.concatenate([b2[0:832, lanes(low, 384)], b2[0:832, lanes(high, 384)]], axis=1)

    def begin():
        vval[12:16, :] = jnp.zeros((4, 768), f32)
        for name, hbm, ref in (
            ("grad", grad_hbm, gd), ("dyl", dyl_hbm, dyl), ("w0", w0_hbm, x0), ("slope", slope_hbm, b2.at[0:832]),
            ("two", two_hbm, two), ("w1", w1_hbm, x1), ("dy", dy_hbm, dy), ("middle", middle_hbm, middle), ("stats", stat_two_hbm, stats),
            ("mixed", mixed_hbm, mixed), ("w2", w2_hbm, x2), ("prob", prob_hbm, b1),
        ):
            got[name] = fetch(hbm, ref)

    def dy_sums():
        vval[7:8, :] = total(dyl, 0)

    def active_grad(start, stop):
        if start == 0:
            got["dyl"].wait()
            got["w0"].wait()
            got["slope"].wait()

        def body(z, _):
            at = lanes(768 * z, 768)
            low = (dot(dyl[...], x0[z].reshape(768, 768), 1, 1) * b2[0:832, at].astype(f32)).astype(bf)
            b2[0:832, at] = low
            vval[pl.ds(8 + z, 1), :] = jnp.sum(low.astype(f32), axis=0, keepdims=True)
            return 0
        lax.fori_loop(start, stop, body, 0)

    def raw_up(start, stop):
        if start == 0:
            got["two"].wait()

        def body(j, _):
            x0[:, :, :, j] = dot(two[...], columns(2, j), 0, 0).astype(bf).reshape(4, 2, 2, 48, 768)
            return 0
        lax.fori_loop(start, stop, body, 0)

    def two_grad(start, stop):
        if start == 0:
            got["w1"].wait()
            wide[...] = dot(columns(2, 0), unit(x1, 0), 1, 1)

        def body(j, _):
            wide[...] += dot(columns(2, j), unit(x1, j), 1, 1)
            return 0
        lax.fori_loop(max(start, 1), stop, body, 0)
        if stop == 4:
            got["proj"] = fetch(proj_hbm, b2.at[:, 0:2304])
            got["normed"] = fetch(normed_hbm, b2.at[0:832, 2304:3072])
    zero = jnp.zeros((8, 768), f32)

    def fold(value):
        return jnp.sum(value.reshape(CHUNK // 8, 8, 768), axis=0)

    def second():
        got["dy"].wait()
        got["middle"].wait()
        got["stats"].wait()

        def second_norm(rows, carry):
            grad = wide[rows, :]
            h, scale = normalized(middle[rows, :], stats, rows)
            e = grad * vec[5:6, :]
            mean = jnp.sum(e, axis=-1, keepdims=True) * (1.0 / 768)
            along = jnp.sum(e * h, axis=-1, keepdims=True) * (1.0 / 768)
            value = dy[rows, :] + scale * (e - mean - h * along)
            dy[rows, :] = value
            low = value.astype(bf)
            two[rows, :] = low
            return carry[0] + fold(grad * h), carry[1] + fold(grad), carry[2] + fold(low.astype(f32))
        sums = row_loop(832, second_norm, (zero, zero, zero))
        for row, part in zip((5, 6, 4), sums):
            vval[row : row + 1, :] = jnp.sum(part, axis=0, keepdims=True)

    def raw_out():
        got["mixed"].wait()
        x1[:, :, :, 3] = dot(mixed[...], two[...], 0, 0).astype(bf).reshape(4, 2, 2, 48, 768)
        got["held"] = fetch(held_hbm, mixed)
        got["stats"] = fetch(stat_one_hbm, stats)

    def mixed_grad():
        got["w2"].wait()
        dyl[...] = dot(two[...], unit(x2, 3), 1, 1).astype(bf)
        got["prob"].wait()
        got["proj"].wait()

    def attention(half, start, stop):
        first = lax.broadcasted_iota(jnp.int32, (208, 128), 1) < 64

        def heads(pair, base):
            rows, deep = pl.ds(base, 208), pl.ds(base, 256)
            at_q, at_k, at_v = lanes(pair * 128, 128), lanes(768 + pair * 128, 128), lanes(1536 + pair * 128, 128)
            q, k, v = b2[rows, at_q], both_heads(b2[deep, at_k], score_scale), both_heads(b2[deep, at_v])
            d = dyl[rows, at_q]
            low = b1[rows, lanes(pair * 512, 512)]
            p = low.astype(f32)
            weighted = p * dot(d, v, 1, 1)
            parts = []
            for h in (0, 1):
                part = slice(h * 256, h * 256 + 256)
                parts.append((weighted[:, part] - p[:, part] * jnp.sum(weighted[:, part], axis=-1, keepdims=True)).astype(bf))
            s = jnp.concatenate(parts, axis=1)
            dk, dv = dot(s, q, 0, 0), dot(low, d, 0, 0)
            b2[rows, at_q] = dot(s, k, 1, 0).astype(bf)
            b2[rows, at_k] = (jnp.where(first, dk[0:208], dk[256:464]) * score_scale).astype(bf)
            b2[rows, at_v] = jnp.where(first, dv[0:208], dv[256:464]).astype(bf)

        def body(i, _):
            for pair in range(3 * half, 3 * half + 3):
                heads(pair, pl.multiple_of(208 * i, 16))
            return 0
        lax.fori_loop(start, stop, body, 0)

    def raw_qkv(j):
        if j == 0:
            got["normed"].wait()
        x1[:, :, :, j] = dot(b2[0:832, 2304:3072], columns(0, j), 0, 0).astype(bf).reshape(4, 2, 2, 48, 768)

    def qkv_sums():
        vval[2:3, :] = total(b2, 0)
        vval[3:4, :] = total(b2, 1536)

    def normed_grad():
        wide[...] = dot(columns(0, 0), unit(x2, 0), 1, 1)
        wide[...] += dot(columns(0, 1), unit(x2, 1), 1, 1)
        wide[...] += dot(columns(0, 2), unit(x2, 2), 1, 1)

    def first():
        got["held"].wait()
        got["stats"].wait()

        def first_norm(rows, carry):
            grad = wide[rows, :]
            h, scale = normalized(mixed[rows, :].astype(f32), stats, rows)
            e = grad * vec[0:1, :]
            mean = jnp.sum(e, axis=-1, keepdims=True) * (1.0 / 768)
            along = jnp.sum(e * h, axis=-1, keepdims=True) * (1.0 / 768)
            dy[rows, :] = dy[rows, :] + scale * (e - mean - h * along)
            return carry[0] + fold(grad * h), carry[1] + fold(grad)
        sums = row_loop(832, first_norm, (zero, zero))
        for row, part in zip((0, 1), sums):
            vval[row : row + 1, :] = jnp.sum(part, axis=0, keepdims=True)
        for i in range(4):
            result[i] = dy[208 * i : 208 * i + 196, :]
            put = pltpu.make_async_copy(result.at[i], ig_hbm.at[:, i, :], local_sem.at[24 + i])
            put.start()
            puts.append(put)

    vsum = SumAll(place, vval, vbuf, vz, sends, vsem)
    nsum = SumFew(place, nbuf, nz, sends, nsem)

    def line(n):
        got["squares"] = got.get("squares", 0.0) + reds[n].line_add(n > 0)

    def vectors():
        got["vsum"] = vsum.total()
        r_vec[...] = got["vsum"]

    def norm():
        nsum.start(got["squares"])

    def emit(n):
        red = reds[n]
        weight, unit0, out = ((3, 0, r_down), (2, 0, r_up), (2, 2, r_up), (1, 0, r_out), (0, 0, r_qkv), (0, 1, r_qkv), (0, 2, r_qkv))[n]
        red.wait(red.swap, 15)
        for j in range(red.swap.shape[0]):
            if weight == 3:
                out[48 * j : 48 * (j + 1), place.col(place.c)] = red.final[place.c * 2 + j]
                out[48 * j : 48 * (j + 1), place.col(1 - place.c)] = red.swap[j]
            else:
                mine = pl.ds(pl.multiple_of(place.c * 24, 8), 24)
                out[:, lanes(column(weight, unit0 + j, place.c), 384)] = red.final[j, mine, :]
                out[:, lanes(column(weight, unit0 + j, 1 - place.c), 384)] = red.swap[j]

    def finish():
        whole = nsum.total()
        r_norm[...] = jnp.zeros((8, 128), f32) + (jnp.sum(whole) + jnp.sum(got["vsum"] * got["vsum"]))

    def end():
        sends.drain()
        for put in puts:
            put.wait()
    begin()
    place.meet()
    got["grad"].wait()
    active_grad(0, 1)
    active_grad(1, 2)
    reds[0].core_go()
    active_grad(2, 4)
    dy_sums()
    reds[0].first_go(2, 1)
    raw_up(0, 2)
    reds[1].core_go()
    raw_up(2, 4)
    reds[0].first_go(3, 0)
    two_grad(0, 1)
    reds[1].first_go()
    reds[2].core_go()
    two_grad(1, 3)
    two_grad(3, 4)
    reds[0].second_go()
    reds[2].first_go()
    second()
    raw_out()
    mixed_grad()
    attention(0, 0, 2)
    reds[3].core_go()
    reds[0].line_go()
    reds[1].second_go()
    attention(0, 2, 4)
    reds[3].first_go()
    raw_qkv(0)
    reds[4].core_go()
    attention(1, 0, 2)
    reds[2].second_go()
    reds[1].line_go()
    reds[4].first_go()
    attention(1, 2, 4)
    raw_qkv(1)
    reds[5].core_go()
    reds[3].second_go()
    reds[2].line_go()
    reds[5].first_go()
    reds[4].second_go()
    raw_qkv(2)
    reds[6].core_go()
    qkv_sums()
    normed_grad()
    reds[5].second_go()
    reds[3].line_go()
    reds[6].first_go()
    reds[4].line_go()
    first()
    reds[5].line_go()
    vsum.step(0)
    reds[6].second_go()
    vsum.step(1)
    line(1)
    reds[6].line_go()
    line(4)
    line(2)
    vsum.step(2)
    line(0)
    line(5)
    line(3)
    vsum.step(3)
    line(6)
    norm()
    nsum.turn()
    emit(5)
    emit(2)
    emit(3)
    emit(4)
    emit(0)
    vectors()
    emit(1)
    emit(6)
    finish()
    end()


def backward(shape, vec, groups, kept, shards):
    dma = pltpu.SemaphoreType.DMA
    vm = pl.BlockSpec(memory_space=VMEM)
    anyspace = pl.BlockSpec(memory_space=pl.ANY)
    S = jax.ShapeDtypeStruct
    bufs = []
    for units, apart in ((4, False), (2, True), (2, True), (1, True), (1, True), (1, True), (1, True)):
        block = (units, 48, 384)
        swap = (units, 24, 384) if apart else (units // 2, 48, 384)
        bufs += [
            VMEM((4, 2, 2) + block, bf), VMEM((4, 2) + block, bf), VMEM((4,) + block, bf), VMEM((3,) + block, bf),
            VMEM(block, f32), VMEM(swap, f32),
        ]
    return pl.pallas_call(
        backward_kernel,
        out_shape=[S(s, f32) for s in shards] + [S((16, 768), f32), S((8, 128), f32), S(shape, f32)],
        in_specs=[vm] + [anyspace] * 16,
        out_specs=[vm] * 6 + [anyspace],
        scratch_shapes=[VMEM(UNIT, bf)] * 4
        + [
            VMEM((832, 3072), bf), VMEM((880, 3072), bf), VMEM((832, 768), f32), VMEM((832, 768), bf), VMEM((832, 768), bf),
            VMEM((832, 768), f32), VMEM((832, 768), bf), VMEM((832, 768), f32), VMEM((832, 256), f32), VMEM((4, 196, 768), f32),
        ]
        + bufs
        + [VMEM((16, 768), f32), VMEM((3, 16, 768), f32), VMEM((4, 16, 768), f32)]
        + [VMEM((8, 8, 128), f32), VMEM((4, 8, 128), f32)]
        + [dma((168,)), dma((7, 16)), dma((7,)), dma((12,)), dma((28,))],
        compiler_params=pltpu.CompilerParams(collective_id=1, has_side_effects=True, vmem_limit_bytes=62 << 20),
        name="backward",
    )(vec, *groups, *kept)


def update_kernel(squares, vsum, *refs):
    loads, stores, norm_out = refs[0:21], refs[21:43], refs[43]
    held, made, wide, sems = refs[44:65], refs[65:85], refs[85], refs[86]
    moves = [pltpu.make_async_copy(s, t, sems.at[n]) for n, (s, t) in enumerate(zip(loads, held))]
    for move in moves:
        move.start()
    norm = jnp.sqrt(squares[0:1, 0:1])
    norm_out[...] = norm
    factor = clip_limit / jnp.maximum(norm, clip_limit)
    start = 24 * lax.axis_index("dev")
    wide[:, 0:768] = vsum[...]
    wide[:, 768:896] = jnp.zeros((16, 128), f32)
    window = wide[:, lanes((start // 128) * 128, 256)]
    shard = pltpu.roll(window, 256 - start % 128, 1)[0:12, 0:24]
    puts = []

    def put(ref, n):
        move = pltpu.make_async_copy(ref, stores[n], sems.at[21 + n])
        move.start()
        puts.append(move)
    for n in range(2):
        moves[n].wait()
        put(held[n], n)
    for n in range(5):
        rates = (rate_matrix, decay_matrix) if n < 4 else (rate_vector, 0.0)
        own = range(2 + 4 * n, 6 + 4 * n if n < 4 else 21)
        for m in own:
            moves[m].wait()
        values = [held[m][...] for m in own]
        master, first, second = values[:3]
        parts = adam_update(master, values[3] if n < 4 else shard, first, second, factor, *rates)
        for k in range(4):
            made[4 * n + k][...] = parts[k]
            put(made[4 * n + k], 2 + 4 * n + k)
    for move in puts:
        move.wait()


def update(squares, vsum, grads, masters, first, second, kept):
    vm = pl.BlockSpec(memory_space=VMEM)
    anyspace = pl.BlockSpec(memory_space=pl.ANY)
    S = jax.ShapeDtypeStruct
    loads = list(kept)
    for n in range(5):
        loads += [masters[n], first[n], second[n]] + ([grads[n]] if n < 4 else [])
    made = [m.shape for m in masters for _ in range(4)]
    return pl.pallas_call(
        update_kernel,
        out_shape=[S(a.shape, f32) for a in kept] + [S(m, f32) for m in made] + [S((1, 1), f32)],
        in_specs=[vm] * 2 + [anyspace] * 21,
        out_specs=[anyspace] * 22 + [vm],
        scratch_shapes=[VMEM(a.shape, f32) for a in loads] + [VMEM(m, f32) for m in made]
        + [VMEM((16, 896), f32), pltpu.SemaphoreType.DMA((43,))],
        compiler_params=pltpu.CompilerParams(vmem_limit_bytes=62 << 20),
        name="update",
    )(squares, vsum, *loads)


def local_wide(
    images,
    pair_matrix,
    caption_grads,
    qkv_weight,
    out_weight,
    up_weight,
    down_weight,
    vector_rows,
    first_qkv,
    first_out,
    first_up,
    first_down,
    first_vectors,
    second_qkv,
    second_out,
    second_up,
    second_down,
    second_vectors,
):
    image_count, patches, model_width = images.shape
    row_count = image_count * patches
    head_count = model_width // HD
    qkv_low = qkv_weight.astype(jnp.bfloat16)
    out_low = out_weight.astype(jnp.bfloat16)
    up_low = up_weight.astype(jnp.bfloat16)
    down_low = down_weight.astype(jnp.bfloat16)
    vector_low = vector_rows.astype(jnp.bfloat16)
    gathered = (
        lax.all_gather(qkv_low, "dev", axis=0, tiled=True),
        lax.all_gather(out_low, "dev", axis=0, tiled=True),
        lax.all_gather(up_low, "dev", axis=0, tiled=True),
        lax.all_gather(down_low, "dev", axis=0, tiled=True),
        lax.all_gather(vector_low, "dev", axis=1, tiled=True),
    )
    result, unused_values = forward_pass(gathered, images)
    output = result.reshape(image_count, patches, model_width)
    gathered_again = (
        lax.all_gather(qkv_low, "dev", axis=0, tiled=True),
        lax.all_gather(out_low, "dev", axis=0, tiled=True),
        lax.all_gather(up_low, "dev", axis=0, tiled=True),
        lax.all_gather(down_low, "dev", axis=0, tiled=True),
        lax.all_gather(vector_low, "dev", axis=1, tiled=True),
    )
    qkv_full, out_full, up_full, down_full, vector_again = gathered_again
    vector_full = vector_again.astype(jnp.float32)
    recomputed, kept_values = forward_pass(gathered_again, images)
    (
        flat_inputs,
        normed_low,
        queries,
        keys_all,
        values_all,
        probabilities,
        prob_low,
        mixed_low,
        middle,
        normed_two_low,
        upward,
        active_low,
    ) = kept_values
    caption_flat = caption_grads.reshape(caption_grads.shape[0], patches * model_width)
    upstream = jnp.dot(
        pair_matrix.astype(jnp.bfloat16), caption_flat, preferred_element_type=jnp.float32
    ).reshape(row_count, model_width)
    down_grad_low = upstream.astype(jnp.bfloat16)
    raw_down = contract_first(active_low, down_grad_low)
    bias_down_grad = jnp.sum(down_grad_low.astype(jnp.float32), axis=0)
    active_grad = contract_last(down_grad_low, down_full)
    gelu_value, gelu_pull = jax.vjp(gelu_tanh, upward)
    upward_grad_low = gelu_pull(active_grad)[0].astype(jnp.bfloat16)
    raw_up = contract_first(normed_two_low, upward_grad_low)
    bias_up_grad = jnp.sum(upward_grad_low.astype(jnp.float32), axis=0)
    normed_two_grad = contract_last(upward_grad_low, up_full)
    second_norm_value, second_norm_pull = jax.vjp(
        layer_norm, middle, vector_full[5], vector_full[6]
    )
    middle_norm_grad, gain_two_grad, shift_two_grad = second_norm_pull(normed_two_grad)
    middle_grad = upstream + middle_norm_grad
    attended_low = middle_grad.astype(jnp.bfloat16)
    raw_out = contract_first(mixed_low, attended_low)
    bias_out_grad = jnp.sum(attended_low.astype(jnp.float32), axis=0)
    mixed_grad_low = (
        contract_last(attended_low, out_full)
        .astype(jnp.bfloat16)
        .reshape(image_count, patches, head_count, HD)
    )
    prob_grad = jnp.einsum(
        "bqhd,bkhd->bhqk", mixed_grad_low, values_all, preferred_element_type=jnp.float32
    )
    value_grad = jnp.einsum(
        "bhqk,bqhd->bkhd", prob_low, mixed_grad_low, preferred_element_type=jnp.float32
    )
    score_grad = probabilities * (
        prob_grad - jnp.sum(probabilities * prob_grad, axis=-1, keepdims=True)
    )
    score_grad_low = score_grad.astype(jnp.bfloat16)
    query_grad = (
        jnp.einsum("bhqk,bkhd->bqhd", score_grad_low, keys_all, preferred_element_type=jnp.float32)
        * score_scale
    )
    key_grad = (
        jnp.einsum("bhqk,bqhd->bkhd", score_grad_low, queries, preferred_element_type=jnp.float32)
        * score_scale
    )
    projected_grad_low = (
        jnp.stack([query_grad, key_grad, value_grad], axis=2)
        .astype(jnp.bfloat16)
        .reshape(row_count, 3 * model_width)
    )
    raw_qkv = contract_first(normed_low, projected_grad_low)
    bias_qkv_grad = jnp.sum(projected_grad_low.astype(jnp.float32), axis=0)
    normed_grad = contract_last(projected_grad_low, qkv_full)
    first_norm_value, first_norm_pull = jax.vjp(
        layer_norm, flat_inputs, vector_full[0], vector_full[1]
    )
    inputs_norm_grad, gain_one_grad, shift_one_grad = first_norm_pull(normed_grad)
    input_grads = (middle_grad + inputs_norm_grad).reshape(image_count, patches, model_width)
    small_rows = jnp.stack(
        [
            gain_one_grad,
            shift_one_grad,
            bias_qkv_grad[:model_width],
            bias_qkv_grad[2 * model_width :],
            bias_out_grad,
            gain_two_grad,
            shift_two_grad,
            bias_down_grad,
        ]
    )
    raw_vectors = jnp.concatenate([small_rows, bias_up_grad.reshape(-1, model_width)], axis=0)
    qkv_shard, out_shard, up_shard, down_shard, vector_shard = (
        lax.psum_scatter(raw_qkv, "dev", scatter_dimension=0, tiled=True),
        lax.psum_scatter(raw_out, "dev", scatter_dimension=0, tiled=True),
        lax.psum_scatter(raw_up, "dev", scatter_dimension=0, tiled=True),
        lax.psum_scatter(raw_down, "dev", scatter_dimension=0, tiled=True),
        lax.psum_scatter(raw_vectors, "dev", scatter_dimension=1, tiled=True),
    )
    local_squares = (
        jnp.sum(qkv_shard * qkv_shard)
        + jnp.sum(out_shard * out_shard)
        + jnp.sum(up_shard * up_shard)
        + jnp.sum(down_shard * down_shard)
        + jnp.sum(vector_shard * vector_shard)
    )
    grad_norm = jnp.sqrt(lax.psum(local_squares, "dev"))
    factor = clip_limit / jnp.maximum(grad_norm, clip_limit)
    qkv_parts = adam_update(
        qkv_weight, qkv_shard, first_qkv, second_qkv, factor, rate_matrix, decay_matrix
    )
    out_parts = adam_update(
        out_weight, out_shard, first_out, second_out, factor, rate_matrix, decay_matrix
    )
    up_parts = adam_update(
        up_weight, up_shard, first_up, second_up, factor, rate_matrix, decay_matrix
    )
    down_parts = adam_update(
        down_weight, down_shard, first_down, second_down, factor, rate_matrix, decay_matrix
    )
    vector_parts = adam_update(
        vector_rows, vector_shard, first_vectors, second_vectors, factor, rate_vector, 0.0
    )
    return (
        output,
        input_grads,
        grad_norm,
        qkv_parts[0],
        qkv_parts[1],
        qkv_parts[2],
        qkv_parts[3],
        out_parts[0],
        out_parts[1],
        out_parts[2],
        out_parts[3],
        up_parts[0],
        up_parts[1],
        up_parts[2],
        up_parts[3],
        down_parts[0],
        down_parts[1],
        down_parts[2],
        down_parts[3],
        vector_parts[0],
        vector_parts[1],
        vector_parts[2],
        vector_parts[3],
    )


def local_slice(
    images,
    pair_matrix,
    caption_grads,
    qkv_weight,
    out_weight,
    up_weight,
    down_weight,
    vector_rows,
    first_qkv,
    first_out,
    first_up,
    first_down,
    first_vectors,
    second_qkv,
    second_out,
    second_up,
    second_down,
    second_vectors,
):
    weights = (qkv_weight, out_weight, up_weight, down_weight)
    results = forward(images.transpose(1, 0, 2), pair_matrix, caption_grads, weights, vector_rows)
    groups, kept, output, vector_full = results[0:3], results[3:17], results[17], results[18]
    shapes = [w.shape for w in weights]
    qkv_shard, out_shard, up_shard, down_shard, vector_sum, squares, input_grads = backward(
        output.shape, vector_full, groups, (*kept[:8], *kept[9:]), shapes
    )
    masters = (*weights, vector_rows)
    first = (first_qkv, first_out, first_up, first_down, first_vectors)
    second = (second_qkv, second_out, second_up, second_down, second_vectors)
    shards = (qkv_shard, out_shard, up_shard, down_shard)
    output, input_grads, *parts, norm = update(squares, vector_sum, shards, masters, first, second, (output, input_grads))
    return (output.transpose(1, 0, 2), input_grads.transpose(1, 0, 2), norm[0, 0], *parts)


def solution(mesh):
    fits = mesh.shape["dev"] == 32
    return jax.shard_map(
        local_slice if fits else local_wide,
        mesh=mesh,
        in_specs=(
            P("dev", None, None),
            P("dev", None),
            P("dev", None, None),
            P("dev", None),
            P("dev", None),
            P("dev", None),
            P("dev", None),
            P(None, "dev"),
            P("dev", None),
            P("dev", None),
            P("dev", None),
            P("dev", None),
            P(None, "dev"),
            P("dev", None),
            P("dev", None),
            P("dev", None),
            P("dev", None),
            P(None, "dev"),
        ),
        out_specs=(
            P("dev", None, None),
            P("dev", None, None),
            P(),
            P("dev", None),
            P("dev", None),
            P("dev", None),
            P("dev", None),
            P("dev", None),
            P("dev", None),
            P("dev", None),
            P("dev", None),
            P("dev", None),
            P("dev", None),
            P("dev", None),
            P("dev", None),
            P("dev", None),
            P("dev", None),
            P("dev", None),
            P("dev", None),
            P(None, "dev"),
            P(None, "dev"),
            P(None, "dev"),
            P(None, "dev"),
        ),
        check_vma=False,
    )
```

```python
import functools

import jax
import jax.numpy as jnp
from jax import lax
from jax.experimental import pallas as pl
from jax.experimental.pallas import tpu as pltpu
from jax.sharding import PartitionSpec as P

HD = 64
STEP = 10


norm_eps = 1e-06
clip_limit = 1.0
beta_one = 0.9
beta_two = 0.999
adam_eps = 1e-08
rate_matrix = 0.08
rate_vector = 0.5
decay_matrix = 0.1
score_scale = 0.125


def layer_norm(values, gain_row, shift_row):
    centre = jnp.mean(values, axis=-1, keepdims=True)
    offset = values - centre
    spread = jnp.mean(offset * offset, axis=-1, keepdims=True)
    return offset * lax.rsqrt(spread + norm_eps) * gain_row + shift_row


def softmax_rows(scores):
    shifted = scores - jnp.max(scores, axis=-1, keepdims=True)
    weights = jnp.exp(shifted)
    return weights / jnp.sum(weights, axis=-1, keepdims=True)


def gelu_tanh(values):
    return jax.nn.gelu(values, approximate=True)


def contract_last(left_side, right_side):
    return lax.dot_general(
        left_side, right_side, (((1,), (1,)), ((), ())), preferred_element_type=jnp.float32
    )


def contract_first(left_side, right_side):
    return lax.dot_general(
        left_side, right_side, (((0,), (0,)), ((), ())), preferred_element_type=jnp.float32
    )


def forward_pass(gathered, inputs):
    qkv_full, out_full, up_full, down_full, vector_low = gathered
    vector_full = vector_low.astype(jnp.float32)
    image_count, patches, model_width = inputs.shape
    row_count = image_count * patches
    head_count = model_width // HD
    flat_inputs = inputs.astype(jnp.float32).reshape(row_count, model_width)
    normed_low = layer_norm(flat_inputs, vector_full[0], vector_full[1]).astype(jnp.bfloat16)
    bias_qkv = jnp.concatenate([vector_full[2], jnp.zeros_like(vector_full[2]), vector_full[3]])
    projected = jnp.dot(normed_low, qkv_full, preferred_element_type=jnp.float32) + bias_qkv
    projected_low = projected.astype(jnp.bfloat16).reshape(image_count, patches, 3, head_count, HD)
    queries = projected_low[:, :, 0]
    keys_all = projected_low[:, :, 1]
    values_all = projected_low[:, :, 2]
    scores = (
        jnp.einsum("bqhd,bkhd->bhqk", queries, keys_all, preferred_element_type=jnp.float32)
        * score_scale
    )
    probabilities = softmax_rows(scores)
    prob_low = probabilities.astype(jnp.bfloat16)
    mixed_heads = jnp.einsum(
        "bhqk,bkhd->bqhd", prob_low, values_all, preferred_element_type=jnp.float32
    )
    mixed_low = mixed_heads.reshape(row_count, model_width).astype(jnp.bfloat16)
    attended = jnp.dot(mixed_low, out_full, preferred_element_type=jnp.float32) + vector_full[4]
    middle = flat_inputs + attended
    normed_two_low = layer_norm(middle, vector_full[5], vector_full[6]).astype(jnp.bfloat16)
    upward = jnp.dot(normed_two_low, up_full, preferred_element_type=jnp.float32) + vector_full[
        8:
    ].reshape(-1)
    active_low = gelu_tanh(upward).astype(jnp.bfloat16)
    downward = jnp.dot(active_low, down_full, preferred_element_type=jnp.float32) + vector_full[7]
    result = middle + downward
    kept_values = (
        flat_inputs,
        normed_low,
        queries,
        keys_all,
        values_all,
        probabilities,
        prob_low,
        mixed_low,
        middle,
        normed_two_low,
        upward,
        active_low,
    )
    return (result, kept_values)


def adam_update(master, raw_grad, moment_one, moment_two, factor, step_rate, decay_rate):
    clipped = raw_grad * factor
    moment_one_new = beta_one * moment_one + (1.0 - beta_one) * clipped
    moment_two_new = beta_two * moment_two + (1.0 - beta_two) * clipped * clipped
    first_hat = moment_one_new / (1.0 - beta_one**STEP)
    second_hat = moment_two_new / (1.0 - beta_two**STEP)
    master_new = master - step_rate * (
        first_hat / (jnp.sqrt(second_hat) + adam_eps) + decay_rate * master
    )
    return (clipped, master_new, moment_one_new, moment_two_new)


MESH = pl.DeviceIdType.MESH
bf = jnp.bfloat16
f32 = jnp.float32
VMEM = pltpu.VMEM
ROWS = 208
UNIT = (4, 2, 2, 4, 48, 768)
CHUNKS = ((2, 0, 3, 0), (2, 3, 1, 1), (1, 0, 2, 2), (1, 2, 2, 2), (0, 0, 2, 3), (0, 2, 2, 3))


QKV_AT = ((0, 768), (1536, 384), (1152, 1920))


def column(weight, unit, c):
    if weight == 0:
        low, high = QKV_AT[unit]
        return low + c * (high - low)
    return c * (1536 if weight == 2 else 384) + (384 * unit if weight == 2 else 0)


class Place:
    def __init__(self):
        me = lax.axis_index("dev")
        self.me = me
        self.c = me % 2
        self.x = (me // 2) % 2
        self.y = (me // 4) % 2
        self.z = me // 8
        self.q = me // 2
        self.sib = me + 1 - 2 * self.c
        self.xn = me + 2 - 4 * self.x
        self.yn = me + 4 - 8 * self.y
        self.xo = 1 - self.x
        self.yo = 1 - self.y

    def zz(self, k):
        return (self.z + k) % 4

    def zp(self, k):
        return self.zz(k) * 8 + self.me % 8

    def col(self, c):
        return pl.ds(pl.multiple_of(c * 384, 128), 384)

    def greet(self):
        bar = pltpu.get_barrier_semaphore()
        for dev in [self.near(n) for n in range(1, 8)] + [self.zp(1), self.zp(2), self.zp(3)]:
            pl.semaphore_signal(bar, inc=1, device_id=(dev,), device_id_type=MESH)

    def near(self, n):
        return self.z * 8 + (self.me + n) % 8

    def meet(self):
        pl.semaphore_wait(pltpu.get_barrier_semaphore(), 10)


class Sends:
    def __init__(self, sems):
        self.sems = sems
        self.used = 0
        self.open = []

    def go(self, src, dst, recv, dev):
        copy = pltpu.make_async_remote_copy(
            src_ref=src, dst_ref=dst, send_sem=self.sems.at[self.used], recv_sem=recv,
            device_id=(dev,), device_id_type=MESH,
        )
        self.used += 1
        copy.start()
        self.open.append(copy)

    def drain(self):
        for copy in self.open:
            copy.wait_send()
        self.open = []


def await_recv(place, ref, recv, spare):
    pltpu.make_async_remote_copy(
        src_ref=ref, dst_ref=ref, send_sem=spare, recv_sem=recv,
        device_id=(place.sib,), device_id_type=MESH,
    ).wait_recv()


class Gather:
    def __init__(self, place, chunk, group, sends, rail_sem, sib_sem):
        self.p, self.group, self.sends = place, group, sends
        self.number = chunk
        _, self.first, self.count, _ = CHUNKS[chunk]
        self.rail_sem, self.sib_sem = rail_sem.at[chunk], sib_sem.at[chunk]

    def at(self, k, y, x):
        return self.group.at[self.p.zz(k), y, x, pl.ds(self.first, self.count), :, self.p.col(self.p.c)]

    def sem(self, k, y, x):
        return self.rail_sem.at[self.p.zz(k) * 4 + y * 2 + x]

    def go(self, k, y, x, dev):
        ref = self.at(k, y, x)
        self.sends.go(ref, ref, self.sem(k, y, x), dev)

    def wait(self, k, y, x):
        await_recv(self.p, self.at(k, y, x), self.sem(k, y, x), self.sends.sems.at[0])

    def own(self):
        p = self.p
        for k in (2, 1, 3):
            self.go(0, p.y, p.x, p.zp(k))
        self.plane(0)

    def turn(self, k):
        return (k + self.number) % 2 == 0

    def plane(self, k):
        p = self.p
        for dev in (p.xn, p.yn) if self.turn(k) else (p.yn, p.xn):
            self.go(k, p.y, p.x, dev)

    def arrive(self, k):
        self.wait(k, self.p.y, self.p.x)
        self.plane(k)

    def forward(self, k):
        p = self.p
        if self.turn(k):
            self.wait(k, p.y, p.xo)
            self.go(k, p.y, p.xo, p.yn)
        else:
            self.wait(k, p.yo, p.x)
            self.go(k, p.yo, p.x, p.xn)


    def level(self, k, c):
        return self.group.at[self.p.zz(k), :, :, pl.ds(self.first, self.count), :, self.p.col(c)]

    def share(self):
        p = self.p
        for k in (0, 1, 3, 2):
            if self.turn(k):
                self.wait(k, p.yo, p.x)
            else:
                self.wait(k, p.y, p.xo)
            self.wait(k, p.yo, p.xo)
            ref = self.level(k, p.c)
            self.sends.go(ref, ref, self.sib_sem.at[p.zz(k)], p.sib)

    def finish(self):
        p = self.p
        for k in (0, 1, 3, 2):
            await_recv(p, self.level(k, 1 - p.c), self.sib_sem.at[p.zz(k)], self.sends.sems.at[0])


class GatherVectors:
    def __init__(self, place, slots, sends, rail_sem, sib_sem):
        self.p, self.slots, self.sends, self.rail_sem, self.sib_sem = place, slots, sends, rail_sem, sib_sem

    def at(self, k, y, x, c):
        return self.slots.at[self.p.zz(k), y, x, c]

    def sem(self, k, y, x):
        return self.rail_sem.at[self.p.zz(k) * 4 + y * 2 + x]

    def go(self, k, y, x, dev):
        ref = self.at(k, y, x, self.p.c)
        self.sends.go(ref, ref, self.sem(k, y, x), dev)

    def wait(self, k, y, x):
        await_recv(self.p, self.at(k, y, x, self.p.c), self.sem(k, y, x), self.sends.sems.at[0])

    def own(self):
        p = self.p
        for k in (1, 2, 3):
            self.go(0, p.y, p.x, p.zp(k))
        self.go(0, p.y, p.x, p.xn)
        self.go(0, p.y, p.x, p.yn)

    def rest(self):
        p = self.p
        for k in range(4):
            if k:
                self.wait(k, p.y, p.x)
                self.go(k, p.y, p.x, p.xn)
                self.go(k, p.y, p.x, p.yn)
        for k in range(4):
            self.wait(k, p.y, p.xo)
            self.go(k, p.y, p.xo, p.yn)
        for k in range(4):
            self.wait(k, p.yo, p.x)
            self.wait(k, p.yo, p.xo)
            ref = self.slots.at[p.zz(k), :, :, p.c]
            self.sends.go(ref, ref, self.sib_sem.at[p.zz(k)], p.sib)
        for k in range(4):
            await_recv(p, self.slots.at[p.zz(k), :, :, 1 - p.c], self.sib_sem.at[p.zz(k)], self.sends.sems.at[0])


def join_vectors(slots):
    lane = lax.broadcasted_iota(jnp.int32, (16, 128), 1)
    tiles = [jnp.zeros((16, 128), f32) for _ in range(7)]
    for d in range(32):
        tile, off = (24 * d) // 128, (24 * d) % 128
        held = slots[d // 8, (d // 4) % 2, (d // 2) % 2, d % 2]
        turned = pltpu.roll(held, off, 1) if off else held
        tiles[tile] = jnp.where((lane >= off) & (lane < off + 24), turned, tiles[tile])
        if off + 24 > 128:
            tiles[tile + 1] = jnp.where(lane < off - 104, turned, tiles[tile + 1])
    return jnp.concatenate(tiles[:6], axis=1).astype(bf).astype(f32)


ORDER = (2, 1, 3, 0)


class Reduce:
    def __init__(self, place, turn, grad, first, count, bufs, sends, sems):
        self.p, self.parity, self.grad, self.first, self.count = place, turn, grad, first, count
        self.cb, self.pb, self.qb, self.zb, self.final, self.swap = bufs
        self.sends, self.sems = sends, sems

    def at(self, z, y, x, c):
        return (z, y, x, pl.ds(self.first, self.count), slice(None), self.p.col(c))

    def turn(self, k):
        return (k + self.parity) % 2 == 0

    def wait(self, ref, n):
        await_recv(self.p, ref, self.sems.at[n], self.sends.sems.at[0])

    def go(self, index, dst, n, dev):
        self.sends.go(self.grad.at[index], dst, self.sems.at[n], dev)

    def add(self, index, buf, at):
        self.grad[index] = self.grad[index] + buf[at]

    def core_go(self, *ks):
        every = slice(None)
        for k in ks or ORDER:
            self.go(self.at(self.p.zz(k), every, every, 1 - self.p.c), self.cb.at[k], k, self.p.sib)

    def first_go(self, *ks):
        p, every = self.p, slice(None)
        for k in ks or ORDER:
            self.wait(self.cb.at[k], k)
            z = p.zz(k)

            def body(i, _, k=k, z=z):
                self.add(self.at(z, i // 2, i % 2, p.c), self.cb, (k, i // 2, i % 2))
                return 0
            lax.fori_loop(0, 4, body, 0)
            if self.turn(k):
                self.go(self.at(z, p.yo, every, p.c), self.pb.at[k], 4 + k, p.yn)
            else:
                self.go(self.at(z, every, p.xo, p.c), self.pb.at[k], 4 + k, p.xn)

    def second_go(self, *ks):
        p = self.p
        for k in ks or ORDER:
            self.wait(self.pb.at[k], 4 + k)
            z = p.zz(k)
            for o in (0, 1):
                y, x = (p.y, o) if self.turn(k) else (o, p.x)
                self.add(self.at(z, y, x, p.c), self.pb, (k, o))
            if self.turn(k):
                self.go(self.at(z, p.y, p.xo, p.c), self.qb.at[k], 8 + k, p.xn)
            else:
                self.go(self.at(z, p.yo, p.x, p.c), self.qb.at[k], 8 + k, p.yn)

    def line_go(self):
        p = self.p
        for k in ORDER:
            self.wait(self.qb.at[k], 8 + k)
            self.add(self.at(p.zz(k), p.y, p.x, p.c), self.qb, (k,))
            if k:
                self.go(self.at(p.zz(k), p.y, p.x, p.c), self.zb.at[k - 1], 11 + k, p.zp(k))

    def line_add(self, rows_apart):
        p = self.p
        for k in (1, 2, 3):
            self.wait(self.zb.at[k - 1], 11 + k)
        total = self.grad[self.at(p.z, p.y, p.x, p.c)].astype(f32)
        for k in range(3):
            total = total + self.zb[k].astype(f32)
        self.final[...] = total
        if rows_apart:
            ref = self.final.at[:, pl.ds(pl.multiple_of((1 - p.c) * 24, 8), 24), :]
        else:
            ref = self.final.at[pl.ds((1 - p.c) * (self.count // 2), self.count // 2)]
        self.sends.go(ref, self.swap, self.sems.at[15], p.sib)
        square = total * total
        tile = jnp.sum(square.reshape(self.count * 6, 8, 384), axis=0)
        return tile[:, :128] + tile[:, 128:256] + tile[:, 256:384]


class SumAll:
    def __init__(self, place, value, buf, zbuf, sends, sems):
        self.p, self.value, self.buf, self.zbuf, self.sends, self.sems = place, value, buf, zbuf, sends, sems

    def go(self, n):
        self.sends.go(self.value, self.buf.at[n], self.sems.at[n], (self.p.sib, self.p.xn, self.p.yn)[n])
        self.copy = self.sends.open.pop()

    def add(self, n):
        await_recv(self.p, self.buf.at[n], self.sems.at[n], self.sends.sems.at[0])
        self.copy.wait_send()
        self.value[...] = self.value[...] + self.buf[n]

    def step(self, n):
        p = self.p
        if n:
            self.add(n - 1)
        if n < 3:
            self.go(n)
        else:
            self.zbuf[p.z] = self.value[...]
            for k in (2, 1, 3):
                self.sends.go(self.value, self.zbuf.at[p.z], self.sems.at[3 + p.z], p.zp(k))

    def total(self):
        p = self.p
        for k in (1, 2, 3):
            await_recv(p, self.zbuf.at[p.zz(k)], self.sems.at[3 + p.zz(k)], self.sends.sems.at[0])
        return (self.zbuf[0] + self.zbuf[1]) + (self.zbuf[2] + self.zbuf[3])


class SumFew:
    def __init__(self, place, buf, zbuf, sends, sems):
        self.p, self.buf, self.zbuf, self.sends, self.sems = place, buf, zbuf, sends, sems

    def start(self, value):
        p = self.p
        mine = p.me % 8
        self.buf[mine] = value
        for n in range(1, 8):
            self.sends.go(self.buf.at[mine], self.buf.at[mine], self.sems.at[mine], p.near(n))

    def turn(self):
        p = self.p
        for n in range(1, 8):
            slot = (p.me + n) % 8
            await_recv(p, self.buf.at[slot], self.sems.at[slot], self.sends.sems.at[0])
        self.zbuf[p.z] = jnp.sum(self.buf[...], axis=0)
        for k in (2, 1, 3):
            self.sends.go(self.zbuf.at[p.z], self.zbuf.at[p.z], self.sems.at[8 + p.z], p.zp(k))

    def total(self):
        p = self.p
        for k in (1, 2, 3):
            await_recv(p, self.zbuf.at[p.zz(k)], self.sems.at[8 + p.zz(k)], self.sends.sems.at[0])
        return (self.zbuf[0] + self.zbuf[1]) + (self.zbuf[2] + self.zbuf[3])


def dot(a, b, ca, cb):
    return lax.dot_general(a, b, (((ca,), (cb,)), ((), ())), preferred_element_type=f32)


def unit(group, j):
    return group[:, :, :, j].reshape(768, 768)


def lanes(start, size):
    return pl.ds(pl.multiple_of(start, 128), size)


CHUNK = 32


def row_loop(count, body, init=0, unroll=2):
    def step(i, carry):
        return body(pl.ds(pl.multiple_of(i * CHUNK, CHUNK), CHUNK), carry)
    return lax.fori_loop(0, count // CHUNK, step, init, unroll=unroll)


def norm_stats(rows):
    centre = jnp.sum(rows, axis=-1, keepdims=True) * (1.0 / 768)
    offset = rows - centre
    spread = jnp.sum(offset * offset, axis=-1, keepdims=True) * (1.0 / 768)
    scale = lax.rsqrt(spread + norm_eps)
    return offset * scale, centre, scale


def keep_stats(stats, rows, centre, scale):
    stats[rows, 0:128] = jnp.broadcast_to(centre, (CHUNK, 128))
    stats[rows, 128:256] = jnp.broadcast_to(scale, (CHUNK, 128))


def normalized(values, stats, rows):
    scale = stats[rows, 128:129]
    return (values - stats[rows, 0:1]) * scale, scale


def pad_images(images, held):
    for i in range(4):
        held[208 * i + 192 : 208 * i + 208, :] = jnp.zeros((16, 768), bf)
        held[208 * i : 208 * i + 196, :] = images[:, i, :]


def upstream_sum(i, pair, captions, dy, dy_low):
    dy[208 * i + 192 : 208 * i + 208, :] = jnp.zeros((16, 768), f32)
    dy_low[208 * i + 192 : 208 * i + 208, :] = jnp.zeros((16, 768), bf)
    weights = [pair[i, c].astype(f32) for c in range(14)]

    def body(j, _):
        col = lanes(j * 128, 128)
        total = weights[0] * captions[0, :, col].astype(f32)
        for c in range(1, 14):
            total = total + weights[c] * captions[c, :, col].astype(f32)
        dy[208 * i : 208 * i + 196, col] = total
        dy_low[208 * i : 208 * i + 196, col] = total.astype(bf)
        return 0
    lax.fori_loop(0, 6, body, 0)


def head_masks(value):
    lane = lax.broadcasted_iota(jnp.int32, (1, 128), 1)
    return jnp.where(lane < 64, value, 0.0).astype(bf), jnp.where(lane < 64, 0.0, value).astype(bf)


def both_heads(rows, value=1.0):
    first, second = head_masks(value)
    return jnp.concatenate([rows * first, rows * second], axis=0)


def attend(base, proj, prob, mixed):
    valid = lax.broadcasted_iota(jnp.int32, (208, 128), 1) < 68

    def body(pair, _):
        rows, wide = pl.ds(base, 208), pl.ds(base, 256)
        q = proj[rows, lanes(pair * 128, 128)]
        k = both_heads(proj[wide, lanes(768 + pair * 128, 128)], score_scale)
        v = both_heads(proj[wide, lanes(1536 + pair * 128, 128)])
        scores = dot(q, k, 1, 1)
        lows = []
        for h in (0, 1):
            near = scores[:, h * 256 : h * 256 + 128]
            far = jnp.where(valid, scores[:, h * 256 + 128 : h * 256 + 256], -1e30)
            top = jnp.max(jnp.maximum(near, far), axis=-1, keepdims=True)
            near, far = jnp.exp(near - top), jnp.exp(far - top)
            factor = 1.0 / jnp.sum(near + far, axis=-1, keepdims=True)
            lows += [(near * factor).astype(bf), (far * factor).astype(bf)]
        low = jnp.concatenate(lows, axis=1)
        prob[rows, lanes(pair * 512, 512)] = low
        mixed[rows, lanes(pair * 128, 128)] = dot(low, v, 1, 0).astype(bf)
        return 0
    lax.fori_loop(0, 6, body, 0, unroll=3)


def own_block(place, shard, stage, group, chunk):
    p = place
    _, first, count, weight = chunk
    low = p.c == 0
    for n in range(count):
        if weight == 3:
            rows = slice(48 * n, 48 * n + 48)
            block = jnp.where(p.c == first // 2, shard[rows, p.col(p.c)], stage[rows, :])
        else:
            j = first + n if weight != 1 else 0
            mine = shard[:, lanes(column(weight, j, p.c), 384)]
            other = stage[:, j * 384 : (j + 1) * 384]
            block = jnp.concatenate([jnp.where(low, mine, other), jnp.where(low, other, mine)], axis=0)
        group[p.z, p.y, p.x, first + n, :, p.col(p.c)] = block.astype(bf)


def forward_kernel(
    images_hbm, pair, captions_hbm, qkv_in, out_in, up_in, down_in, vec_in,
    w0_hbm, w1_hbm, w2_hbm, dy_hbm, dyl_hbm, normed_hbm, proj_hbm, prob_hbm, mixed_hbm, middle_hbm, two_hbm,
    active_hbm, slope_hbm, held_hbm, stat_one_hbm, stat_two_hbm, grad_hbm, out_hbm, vec_out,
    g0, g1, g2, slots, s0, s1, s2, s3, captions, images, dy, dyl, normed, proj, prob, mixed, middle, two, active, slope, held, stat_one, stat_two, grad,
    wide, result, send_sem, stage_sem, rail_sem, sib_sem, vrail_sem, vsib_sem, local_sem,
):
    place = Place()
    place.greet()
    sends = Sends(send_sem)
    groups = (g0, g1, g2)
    shards, stages = (qkv_in, out_in, up_in, down_in), (s0, s1, s2, s3)
    local = []

    def keep(ref, hbm):
        copy = pltpu.make_async_copy(ref, hbm, local_sem.at[len(local)])
        copy.start()
        local.append(copy)
    fetch = pltpu.make_async_copy(images_hbm, images, local_sem.at[30])
    load = pltpu.make_async_copy(captions_hbm, captions, local_sem.at[31])
    ags = [Gather(place, n, groups[CHUNKS[n][0]], sends, rail_sem, sib_sem) for n in range(6)]
    av = GatherVectors(place, slots, sends, vrail_sem, vsib_sem)

    def begin():
        fetch.start()
        load.start()
        slots[place.z, place.y, place.x, place.c] = jnp.zeros((16, 128), f32)
        slots[place.z, place.y, place.x, place.c, 0:12, 0:24] = vec_in[...]
        place.meet()

    def stage():
        for weight, units in enumerate((3, 1, 4, 1)):
            for j in range(units):
                sends.go(
                    shards[weight].at[:, lanes(column(weight, j, 1 - place.c), 384)],
                    stages[weight].at[:, j * 384 : (j + 1) * 384], stage_sem.at[weight, j], place.sib,
                )
        av.own()

    def own(n):
        group, first, _, weight = CHUNKS[n]
        if n in (0, 1, 2, 4):
            for j in range(stages[weight].shape[1] // 384):
                await_recv(place, stages[weight].at[:, j * 384 : (j + 1) * 384], stage_sem.at[weight, j], send_sem.at[0])
        own_block(place, shards[weight], stages[weight], groups[group], CHUNKS[n])
        ags[n].own()

    def arrive(n):
        for k in (1, 3, 2):
            ags[n].arrive(k)

    def forward(n):
        for k in (0, 1, 3, 2):
            ags[n].forward(k)

    def pad():
        fetch.wait()
        pad_images(images, held)
        keep(held, held_hbm)

    def vectors():
        vec_out[...] = join_vectors(slots)

    def first():
        def first_norm(rows, _):
            h, centre, scale = norm_stats(held[rows, :].astype(f32))
            keep_stats(stat_one, rows, centre, scale)
            normed[rows, :] = (h * vec_out[0:1, :] + vec_out[1:2, :]).astype(bf)
            return 0
        row_loop(832, first_norm)
        keep(normed, normed_hbm)
        keep(stat_one, stat_one_hbm)

    def upstream(i):
        if i == 0:
            load.wait()
        upstream_sum(i, pair, captions, dy, dyl)
        if i == 3:
            keep(dy, dy_hbm)
            keep(dyl, dyl_hbm)

    def project(j):
        if j == 0:
            proj[832:880, :] = jnp.zeros((48, 2304), bf)
        value = dot(normed[...], unit(g2, j), 1, 0)
        for c in (0, 1):
            at = column(0, j, c)
            part = value[:, c * 384 : (c + 1) * 384]
            if at < 768:
                part = part + vec_out[2:3, at : at + 384]
            elif at >= 1536:
                part = part + vec_out[3:4, at - 1536 : at - 1152]
            proj[0:832, at : at + 384] = part.astype(bf)
        if j == 2:
            keep(proj, proj_hbm)

    def attention(i):
        attend(208 * i, proj, prob, mixed)

    def attended():
        keep(prob, prob_hbm)
        keep(mixed, mixed_hbm)
        wide[...] = dot(mixed[...], unit(g2, 3), 1, 0)

        def second_norm(rows, _):
            value = wide[rows, :] + held[rows, :].astype(f32) + vec_out[4:5, :]
            middle[rows, :] = value
            h, centre, scale = norm_stats(value)
            keep_stats(stat_two, rows, centre, scale)
            two[rows, :] = (h * vec_out[5:6, :] + vec_out[6:7, :]).astype(bf)
            return 0
        row_loop(832, second_norm)
        keep(middle, middle_hbm)
        keep(two, two_hbm)
        keep(stat_two, stat_two_hbm)

    def up(j):
        wide[...] = dot(two[...], unit(g1, j), 1, 0)

        def bend(rows, _):
            for c in (0, 1):
                at = c * 1536 + j * 384
                u = wide[rows, c * 384 : (c + 1) * 384] + vec_out[8 + at // 768 : 9 + at // 768, at % 768 : at % 768 + 384]
                u2 = u * u
                s = 0.5 + 0.5 * jnp.tanh(u * (0.7978845608028654 + 0.035677408136300125 * u2))
                bent = u * s
                active[rows, at : at + 384] = bent.astype(bf)
                slope[rows, at : at + 384] = (s + (1.5957691216057308 + 0.21406444881780074 * u2) * bent * (1.0 - s)).astype(bf)
            return 0
        row_loop(832, bend)
        if j == 3:
            keep(active, active_hbm)
            keep(slope, slope_hbm)

    def raw_down(start, stop):
        def body(z, _):
            grad[z] = dot(active[:, lanes(768 * z, 768)], dyl[...], 0, 0).astype(bf).reshape(2, 2, 4, 48, 768)
            return 0
        lax.fori_loop(start, stop, body, 0)
        if stop == 4:
            keep(grad, grad_hbm)

    def down():
        for n in range(3):
            wide[:, n * 256 : (n + 1) * 256] = dot(
                active[...], g0[:, :, :, :, :, n * 256 : (n + 1) * 256].reshape(3072, 256), 1, 0
            )
        for i in range(4):
            rows = slice(208 * i, 208 * i + 196)
            result[i] = wide[rows, :] + middle[rows, :] + vec_out[7:8, :]
        for i in range(4):
            keep(result.at[i], out_hbm.at[:, i, :])

    def end():
        sends.drain()
        for copy in local:
            copy.wait()

    def finish(n):
        ags[n].finish()
        if n in (1, 3, 5):
            keep((g2, g1, g0)[n // 2], (w2_hbm, w1_hbm, w0_hbm)[n // 2])

    begin()
    stage()
    upstream(0)
    own(0)
    own(1)
    own(2)
    own(3)
    pad()
    upstream(1)
    own(4)
    own(5)
    arrive(0)
    av.rest()
    vectors()
    first()
    forward(0)
    upstream(2)
    arrive(1)
    arrive(2)
    ags[0].share()
    upstream(3)
    forward(1)
    finish(0)
    project(0)
    project(1)
    arrive(3)
    project(2)
    attention(0)
    attention(1)
    forward(2)
    arrive(4)
    attention(2)
    ags[1].share()
    attention(3)
    ags[2].share()
    finish(1)
    forward(3)
    arrive(5)
    attended()
    finish(2)
    up(0)
    forward(4)
    ags[3].share()
    up(1)
    finish(3)
    forward(5)
    up(2)
    ags[4].share()
    up(3)
    ags[5].share()
    raw_down(0, 4)
    finish(4)
    finish(5)
    down()
    end()


def forward(images, pair, captions, weights, vectors):
    dma = pltpu.SemaphoreType.DMA
    vm = pl.BlockSpec(memory_space=VMEM)
    anyspace = pl.BlockSpec(memory_space=pl.ANY)
    S = jax.ShapeDtypeStruct
    kept = [
        S((832, 768), f32), S((832, 768), bf), S((832, 768), bf), S((880, 2304), bf), S((832, 3072), bf), S((832, 768), bf),
        S((832, 768), f32), S((832, 768), bf), S((832, 3072), bf), S((832, 3072), bf), S((832, 768), bf), S((832, 256), f32), S((832, 256), f32), S(UNIT, bf),
    ]
    return pl.pallas_call(
        forward_kernel,
        out_shape=[S(UNIT, bf)] * 3 + kept + [S(images.shape, f32), S((16, 768), f32)],
        in_specs=[anyspace, pl.BlockSpec(memory_space=pltpu.SMEM), anyspace] + [vm] * 5,
        out_specs=[anyspace] * 18 + [vm],
        scratch_shapes=[VMEM(UNIT, bf)] * 3
        + [VMEM((4, 2, 2, 2, 16, 128), f32)]
        + [VMEM((w.shape[0], w.shape[1] // 2), f32) for w in weights]
        + [VMEM(captions.shape, bf), VMEM(images.shape, bf)]
        + [VMEM(s.shape, s.dtype) for s in kept]
        + [VMEM((832, 768), f32), VMEM((4, 196, 768), f32)]
        + [dma((176,)), dma((4, 4)), dma((6, 16)), dma((6, 4)), dma((16,)), dma((4,)), dma((32,))],
        compiler_params=pltpu.CompilerParams(collective_id=0, has_side_effects=True, vmem_limit_bytes=63 << 20),
        name="forward",
    )(images, pair, captions, *weights, vectors)


def backward_kernel(
    vec, w0_hbm, w1_hbm, w2_hbm, dy_hbm, dyl_hbm, normed_hbm, proj_hbm, prob_hbm, mixed_hbm, middle_hbm, two_hbm,
    slope_hbm, held_hbm, stat_one_hbm, stat_two_hbm, grad_hbm,
    r_qkv, r_out, r_up, r_down, r_vec, r_norm, ig_hbm,
    x0, x1, x2, gd, b1, b2, dy, dyl, two, middle, mixed, wide, stats, result, *scratch,
):
    bufs, scratch = [scratch[6 * n : 6 * n + 6] for n in range(7)], scratch[42:]
    vval, vbuf, vz, nbuf, nz, send_sem, red_sem, vsem, nsem, local_sem = scratch
    place = Place()
    place.greet()
    sends = Sends(send_sem)
    count = [0]

    def fetch(hbm, ref):
        copy = pltpu.make_async_copy(hbm, ref, local_sem.at[count[0]])
        count[0] += 1
        copy.start()
        return copy
    got = {}
    puts = []
    reds = [
        Reduce(place, n, group, first, units, bufs[n], sends, red_sem.at[n])
        for n, (group, first, units) in enumerate(
            ((gd, 0, 4), (x0, 0, 2), (x0, 2, 2), (x1, 3, 1), (x1, 0, 1), (x1, 1, 1), (x1, 2, 1))
        )
    ]
    ones = jnp.ones((16, 832), bf)

    def total(ref, at):
        return dot(ones, ref[0:832, lanes(at, 768)], 1, 0)[0:1, :]

    def columns(weight, j):
        low, high = column(weight, j, 0), column(weight, j, 1)
        return jnp.concatenate([b2[0:832, lanes(low, 384)], b2[0:832, lanes(high, 384)]], axis=1)

    def begin():
        vval[12:16, :] = jnp.zeros((4, 768), f32)
        for name, hbm, ref in (
            ("grad", grad_hbm, gd), ("dyl", dyl_hbm, dyl), ("w0", w0_hbm, x0), ("slope", slope_hbm, b2.at[0:832]),
            ("two", two_hbm, two), ("w1", w1_hbm, x1), ("dy", dy_hbm, dy), ("middle", middle_hbm, middle), ("stats", stat_two_hbm, stats),
            ("mixed", mixed_hbm, mixed), ("w2", w2_hbm, x2), ("prob", prob_hbm, b1),
        ):
            got[name] = fetch(hbm, ref)

    def dy_sums():
        vval[7:8, :] = total(dyl, 0)

    def active_grad(start, stop):
        if start == 0:
            got["dyl"].wait()
            got["w0"].wait()
            got["slope"].wait()

        def body(z, _):
            at = lanes(768 * z, 768)
            low = (dot(dyl[...], x0[z].reshape(768, 768), 1, 1) * b2[0:832, at].astype(f32)).astype(bf)
            b2[0:832, at] = low
            vval[pl.ds(8 + z, 1), :] = jnp.sum(low.astype(f32), axis=0, keepdims=True)
            return 0
        lax.fori_loop(start, stop, body, 0)

    def raw_up(start, stop):
        if start == 0:
            got["two"].wait()

        def body(j, _):
            x0[:, :, :, j] = dot(two[...], columns(2, j), 0, 0).astype(bf).reshape(4, 2, 2, 48, 768)
            return 0
        lax.fori_loop(start, stop, body, 0)

    def two_grad(start, stop):
        if start == 0:
            got["w1"].wait()
            wide[...] = dot(columns(2, 0), unit(x1, 0), 1, 1)

        def body(j, _):
            wide[...] += dot(columns(2, j), unit(x1, j), 1, 1)
            return 0
        lax.fori_loop(max(start, 1), stop, body, 0)
        if stop == 4:
            got["proj"] = fetch(proj_hbm, b2.at[:, 0:2304])
            got["normed"] = fetch(normed_hbm, b2.at[0:832, 2304:3072])
    zero = jnp.zeros((8, 768), f32)

    def fold(value):
        return jnp.sum(value.reshape(CHUNK // 8, 8, 768), axis=0)

    def second():
        got["dy"].wait()
        got["middle"].wait()
        got["stats"].wait()

        def second_norm(rows, carry):
            grad = wide[rows, :]
            h, scale = normalized(middle[rows, :], stats, rows)
            e = grad * vec[5:6, :]
            mean = jnp.sum(e, axis=-1, keepdims=True) * (1.0 / 768)
            along = jnp.sum(e * h, axis=-1, keepdims=True) * (1.0 / 768)
            value = dy[rows, :] + scale * (e - mean - h * along)
            dy[rows, :] = value
            low = value.astype(bf)
            two[rows, :] = low
            return carry[0] + fold(grad * h), carry[1] + fold(grad), carry[2] + fold(low.astype(f32))
        sums = row_loop(832, second_norm, (zero, zero, zero))
        for row, part in zip((5, 6, 4), sums):
            vval[row : row + 1, :] = jnp.sum(part, axis=0, keepdims=True)

    def raw_out():
        got["mixed"].wait()
        x1[:, :, :, 3] = dot(mixed[...], two[...], 0, 0).astype(bf).reshape(4, 2, 2, 48, 768)
        got["held"] = fetch(held_hbm, mixed)
        got["stats"] = fetch(stat_one_hbm, stats)

    def mixed_grad():
        got["w2"].wait()
        dyl[...] = dot(two[...], unit(x2, 3), 1, 1).astype(bf)
        got["prob"].wait()
        got["proj"].wait()

    def attention(half, start, stop):
        first = lax.broadcasted_iota(jnp.int32, (208, 128), 1) < 64

        def heads(pair, base):
            rows, deep = pl.ds(base, 208), pl.ds(base, 256)
            at_q, at_k, at_v = lanes(pair * 128, 128), lanes(768 + pair * 128, 128), lanes(1536 + pair * 128, 128)
            q, k, v = b2[rows, at_q], both_heads(b2[deep, at_k], score_scale), both_heads(b2[deep, at_v])
            d = dyl[rows, at_q]
            low = b1[rows, lanes(pair * 512, 512)]
            p = low.astype(f32)
            weighted = p * dot(d, v, 1, 1)
            parts = []
            for h in (0, 1):
                part = slice(h * 256, h * 256 + 256)
                parts.append((weighted[:, part] - p[:, part] * jnp.sum(weighted[:, part], axis=-1, keepdims=True)).astype(bf))
            s = jnp.concatenate(parts, axis=1)
            dk, dv = dot(s, q, 0, 0), dot(low, d, 0, 0)
            b2[rows, at_q] = dot(s, k, 1, 0).astype(bf)
            b2[rows, at_k] = (jnp.where(first, dk[0:208], dk[256:464]) * score_scale).astype(bf)
            b2[rows, at_v] = jnp.where(first, dv[0:208], dv[256:464]).astype(bf)

        def body(i, _):
            for pair in range(3 * half, 3 * half + 3):
                heads(pair, pl.multiple_of(208 * i, 16))
            return 0
        lax.fori_loop(start, stop, body, 0)

    def raw_qkv(j):
        if j == 0:
            got["normed"].wait()
        x1[:, :, :, j] = dot(b2[0:832, 2304:3072], columns(0, j), 0, 0).astype(bf).reshape(4, 2, 2, 48, 768)

    def qkv_sums():
        vval[2:3, :] = total(b2, 0)
        vval[3:4, :] = total(b2, 1536)

    def normed_grad():
        wide[...] = dot(columns(0, 0), unit(x2, 0), 1, 1)
        wide[...] += dot(columns(0, 1), unit(x2, 1), 1, 1)
        wide[...] += dot(columns(0, 2), unit(x2, 2), 1, 1)

    def first():
        got["held"].wait()
        got["stats"].wait()

        def first_norm(rows, carry):
            grad = wide[rows, :]
            h, scale = normalized(mixed[rows, :].astype(f32), stats, rows)
            e = grad * vec[0:1, :]
            mean = jnp.sum(e, axis=-1, keepdims=True) * (1.0 / 768)
            along = jnp.sum(e * h, axis=-1, keepdims=True) * (1.0 / 768)
            dy[rows, :] = dy[rows, :] + scale * (e - mean - h * along)
            return carry[0] + fold(grad * h), carry[1] + fold(grad)
        sums = row_loop(832, first_norm, (zero, zero))
        for row, part in zip((0, 1), sums):
            vval[row : row + 1, :] = jnp.sum(part, axis=0, keepdims=True)
        for i in range(4):
            result[i] = dy[208 * i : 208 * i + 196, :]
            put = pltpu.make_async_copy(result.at[i], ig_hbm.at[:, i, :], local_sem.at[24 + i])
            put.start()
            puts.append(put)

    vsum = SumAll(place, vval, vbuf, vz, sends, vsem)
    nsum = SumFew(place, nbuf, nz, sends, nsem)

    def line(n):
        got["squares"] = got.get("squares", 0.0) + reds[n].line_add(n > 0)

    def vectors():
        got["vsum"] = vsum.total()
        r_vec[...] = got["vsum"]

    def norm():
        nsum.start(got["squares"])

    def emit(n):
        red = reds[n]
        weight, unit0, out = ((3, 0, r_down), (2, 0, r_up), (2, 2, r_up), (1, 0, r_out), (0, 0, r_qkv), (0, 1, r_qkv), (0, 2, r_qkv))[n]
        red.wait(red.swap, 15)
        for j in range(red.swap.shape[0]):
            if weight == 3:
                out[48 * j : 48 * (j + 1), place.col(place.c)] = red.final[place.c * 2 + j]
                out[48 * j : 48 * (j + 1), place.col(1 - place.c)] = red.swap[j]
            else:
                mine = pl.ds(pl.multiple_of(place.c * 24, 8), 24)
                out[:, lanes(column(weight, unit0 + j, place.c), 384)] = red.final[j, mine, :]
                out[:, lanes(column(weight, unit0 + j, 1 - place.c), 384)] = red.swap[j]

    def finish():
        whole = nsum.total()
        r_norm[...] = jnp.zeros((8, 128), f32) + (jnp.sum(whole) + jnp.sum(got["vsum"] * got["vsum"]))

    def end():
        sends.drain()
        for put in puts:
            put.wait()
    begin()
    place.meet()
    got["grad"].wait()
    active_grad(0, 1)
    active_grad(1, 2)
    reds[0].core_go()
    active_grad(2, 4)
    dy_sums()
    reds[0].first_go(2, 1)
    raw_up(0, 2)
    reds[1].core_go()
    raw_up(2, 4)
    reds[0].first_go(3, 0)
    two_grad(0, 1)
    reds[1].first_go()
    reds[2].core_go()
    two_grad(1, 3)
    two_grad(3, 4)
    reds[0].second_go()
    reds[2].first_go()
    second()
    raw_out()
    mixed_grad()
    attention(0, 0, 2)
    reds[3].core_go()
    reds[0].line_go()
    reds[1].second_go()
    attention(0, 2, 4)
    reds[3].first_go()
    raw_qkv(0)
    reds[4].core_go()
    attention(1, 0, 2)
    reds[2].second_go()
    reds[1].line_go()
    reds[4].first_go()
    attention(1, 2, 4)
    raw_qkv(1)
    reds[5].core_go()
    reds[3].second_go()
    reds[2].line_go()
    reds[5].first_go()
    reds[4].second_go()
    raw_qkv(2)
    reds[6].core_go()
    qkv_sums()
    normed_grad()
    reds[5].second_go()
    reds[3].line_go()
    reds[6].first_go()
    reds[4].line_go()
    first()
    reds[5].line_go()
    vsum.step(0)
    reds[6].second_go()
    vsum.step(1)
    line(1)
    reds[6].line_go()
    line(4)
    line(2)
    vsum.step(2)
    line(0)
    line(5)
    line(3)
    vsum.step(3)
    line(6)
    norm()
    nsum.turn()
    emit(5)
    emit(2)
    emit(3)
    emit(4)
    emit(0)
    vectors()
    emit(1)
    emit(6)
    finish()
    end()


def backward(shape, vec, groups, kept, shards):
    dma = pltpu.SemaphoreType.DMA
    vm = pl.BlockSpec(memory_space=VMEM)
    anyspace = pl.BlockSpec(memory_space=pl.ANY)
    S = jax.ShapeDtypeStruct
    bufs = []
    for units, apart in ((4, False), (2, True), (2, True), (1, True), (1, True), (1, True), (1, True)):
        block = (units, 48, 384)
        swap = (units, 24, 384) if apart else (units // 2, 48, 384)
        bufs += [
            VMEM((4, 2, 2) + block, bf), VMEM((4, 2) + block, bf), VMEM((4,) + block, bf), VMEM((3,) + block, bf),
            VMEM(block, f32), VMEM(swap, f32),
        ]
    return pl.pallas_call(
        backward_kernel,
        out_shape=[S(s, f32) for s in shards] + [S((16, 768), f32), S((8, 128), f32), S(shape, f32)],
        in_specs=[vm] + [anyspace] * 16,
        out_specs=[vm] * 6 + [anyspace],
        scratch_shapes=[VMEM(UNIT, bf)] * 4
        + [
            VMEM((832, 3072), bf), VMEM((880, 3072), bf), VMEM((832, 768), f32), VMEM((832, 768), bf), VMEM((832, 768), bf),
            VMEM((832, 768), f32), VMEM((832, 768), bf), VMEM((832, 768), f32), VMEM((832, 256), f32), VMEM((4, 196, 768), f32),
        ]
        + bufs
        + [VMEM((16, 768), f32), VMEM((3, 16, 768), f32), VMEM((4, 16, 768), f32)]
        + [VMEM((8, 8, 128), f32), VMEM((4, 8, 128), f32)]
        + [dma((168,)), dma((7, 16)), dma((7,)), dma((12,)), dma((28,))],
        compiler_params=pltpu.CompilerParams(collective_id=1, has_side_effects=True, vmem_limit_bytes=62 << 20),
        name="backward",
    )(vec, *groups, *kept)


def update_kernel(squares, vsum, *refs):
    loads, stores, norm_out = refs[0:21], refs[21:43], refs[43]
    held, made, wide, sems = refs[44:65], refs[65:85], refs[85], refs[86]
    moves = [pltpu.make_async_copy(s, t, sems.at[n]) for n, (s, t) in enumerate(zip(loads, held))]
    for move in moves:
        move.start()
    norm = jnp.sqrt(squares[0:1, 0:1])
    norm_out[...] = norm
    factor = clip_limit / jnp.maximum(norm, clip_limit)
    start = 24 * lax.axis_index("dev")
    wide[:, 0:768] = vsum[...]
    wide[:, 768:896] = jnp.zeros((16, 128), f32)
    window = wide[:, lanes((start // 128) * 128, 256)]
    shard = pltpu.roll(window, 256 - start % 128, 1)[0:12, 0:24]
    puts = []

    def put(ref, n):
        move = pltpu.make_async_copy(ref, stores[n], sems.at[21 + n])
        move.start()
        puts.append(move)
    for n in range(2):
        moves[n].wait()
        put(held[n], n)
    for n in range(5):
        rates = (rate_matrix, decay_matrix) if n < 4 else (rate_vector, 0.0)
        own = range(2 + 4 * n, 6 + 4 * n if n < 4 else 21)
        for m in own:
            moves[m].wait()
        values = [held[m][...] for m in own]
        master, first, second = values[:3]
        parts = adam_update(master, values[3] if n < 4 else shard, first, second, factor, *rates)
        for k in range(4):
            made[4 * n + k][...] = parts[k]
            put(made[4 * n + k], 2 + 4 * n + k)
    for move in puts:
        move.wait()


def update(squares, vsum, grads, masters, first, second, kept):
    vm = pl.BlockSpec(memory_space=VMEM)
    anyspace = pl.BlockSpec(memory_space=pl.ANY)
    S = jax.ShapeDtypeStruct
    loads = list(kept)
    for n in range(5):
        loads += [masters[n], first[n], second[n]] + ([grads[n]] if n < 4 else [])
    made = [m.shape for m in masters for _ in range(4)]
    return pl.pallas_call(
        update_kernel,
        out_shape=[S(a.shape, f32) for a in kept] + [S(m, f32) for m in made] + [S((1, 1), f32)],
        in_specs=[vm] * 2 + [anyspace] * 21,
        out_specs=[anyspace] * 22 + [vm],
        scratch_shapes=[VMEM(a.shape, f32) for a in loads] + [VMEM(m, f32) for m in made]
        + [VMEM((16, 896), f32), pltpu.SemaphoreType.DMA((43,))],
        compiler_params=pltpu.CompilerParams(vmem_limit_bytes=62 << 20),
        name="update",
    )(squares, vsum, *loads)


def local_wide(
    images,
    pair_matrix,
    caption_grads,
    qkv_weight,
    out_weight,
    up_weight,
    down_weight,
    vector_rows,
    first_qkv,
    first_out,
    first_up,
    first_down,
    first_vectors,
    second_qkv,
    second_out,
    second_up,
    second_down,
    second_vectors,
):
    image_count, patches, model_width = images.shape
    row_count = image_count * patches
    head_count = model_width // HD
    qkv_low = qkv_weight.astype(jnp.bfloat16)
    out_low = out_weight.astype(jnp.bfloat16)
    up_low = up_weight.astype(jnp.bfloat16)
    down_low = down_weight.astype(jnp.bfloat16)
    vector_low = vector_rows.astype(jnp.bfloat16)
    gathered = (
        lax.all_gather(qkv_low, "dev", axis=0, tiled=True),
        lax.all_gather(out_low, "dev", axis=0, tiled=True),
        lax.all_gather(up_low, "dev", axis=0, tiled=True),
        lax.all_gather(down_low, "dev", axis=0, tiled=True),
        lax.all_gather(vector_low, "dev", axis=1, tiled=True),
    )
    result, unused_values = forward_pass(gathered, images)
    output = result.reshape(image_count, patches, model_width)
    gathered_again = (
        lax.all_gather(qkv_low, "dev", axis=0, tiled=True),
        lax.all_gather(out_low, "dev", axis=0, tiled=True),
        lax.all_gather(up_low, "dev", axis=0, tiled=True),
        lax.all_gather(down_low, "dev", axis=0, tiled=True),
        lax.all_gather(vector_low, "dev", axis=1, tiled=True),
    )
    qkv_full, out_full, up_full, down_full, vector_again = gathered_again
    vector_full = vector_again.astype(jnp.float32)
    recomputed, kept_values = forward_pass(gathered_again, images)
    (
        flat_inputs,
        normed_low,
        queries,
        keys_all,
        values_all,
        probabilities,
        prob_low,
        mixed_low,
        middle,
        normed_two_low,
        upward,
        active_low,
    ) = kept_values
    caption_flat = caption_grads.reshape(caption_grads.shape[0], patches * model_width)
    upstream = jnp.dot(
        pair_matrix.astype(jnp.bfloat16), caption_flat, preferred_element_type=jnp.float32
    ).reshape(row_count, model_width)
    down_grad_low = upstream.astype(jnp.bfloat16)
    raw_down = contract_first(active_low, down_grad_low)
    bias_down_grad = jnp.sum(down_grad_low.astype(jnp.float32), axis=0)
    active_grad = contract_last(down_grad_low, down_full)
    gelu_value, gelu_pull = jax.vjp(gelu_tanh, upward)
    upward_grad_low = gelu_pull(active_grad)[0].astype(jnp.bfloat16)
    raw_up = contract_first(normed_two_low, upward_grad_low)
    bias_up_grad = jnp.sum(upward_grad_low.astype(jnp.float32), axis=0)
    normed_two_grad = contract_last(upward_grad_low, up_full)
    second_norm_value, second_norm_pull = jax.vjp(
        layer_norm, middle, vector_full[5], vector_full[6]
    )
    middle_norm_grad, gain_two_grad, shift_two_grad = second_norm_pull(normed_two_grad)
    middle_grad = upstream + middle_norm_grad
    attended_low = middle_grad.astype(jnp.bfloat16)
    raw_out = contract_first(mixed_low, attended_low)
    bias_out_grad = jnp.sum(attended_low.astype(jnp.float32), axis=0)
    mixed_grad_low = (
        contract_last(attended_low, out_full)
        .astype(jnp.bfloat16)
        .reshape(image_count, patches, head_count, HD)
    )
    prob_grad = jnp.einsum(
        "bqhd,bkhd->bhqk", mixed_grad_low, values_all, preferred_element_type=jnp.float32
    )
    value_grad = jnp.einsum(
        "bhqk,bqhd->bkhd", prob_low, mixed_grad_low, preferred_element_type=jnp.float32
    )
    score_grad = probabilities * (
        prob_grad - jnp.sum(probabilities * prob_grad, axis=-1, keepdims=True)
    )
    score_grad_low = score_grad.astype(jnp.bfloat16)
    query_grad = (
        jnp.einsum("bhqk,bkhd->bqhd", score_grad_low, keys_all, preferred_element_type=jnp.float32)
        * score_scale
    )
    key_grad = (
        jnp.einsum("bhqk,bqhd->bkhd", score_grad_low, queries, preferred_element_type=jnp.float32)
        * score_scale
    )
    projected_grad_low = (
        jnp.stack([query_grad, key_grad, value_grad], axis=2)
        .astype(jnp.bfloat16)
        .reshape(row_count, 3 * model_width)
    )
    raw_qkv = contract_first(normed_low, projected_grad_low)
    bias_qkv_grad = jnp.sum(projected_grad_low.astype(jnp.float32), axis=0)
    normed_grad = contract_last(projected_grad_low, qkv_full)
    first_norm_value, first_norm_pull = jax.vjp(
        layer_norm, flat_inputs, vector_full[0], vector_full[1]
    )
    inputs_norm_grad, gain_one_grad, shift_one_grad = first_norm_pull(normed_grad)
    input_grads = (middle_grad + inputs_norm_grad).reshape(image_count, patches, model_width)
    small_rows = jnp.stack(
        [
            gain_one_grad,
            shift_one_grad,
            bias_qkv_grad[:model_width],
            bias_qkv_grad[2 * model_width :],
            bias_out_grad,
            gain_two_grad,
            shift_two_grad,
            bias_down_grad,
        ]
    )
    raw_vectors = jnp.concatenate([small_rows, bias_up_grad.reshape(-1, model_width)], axis=0)
    qkv_shard, out_shard, up_shard, down_shard, vector_shard = (
        lax.psum_scatter(raw_qkv, "dev", scatter_dimension=0, tiled=True),
        lax.psum_scatter(raw_out, "dev", scatter_dimension=0, tiled=True),
        lax.psum_scatter(raw_up, "dev", scatter_dimension=0, tiled=True),
        lax.psum_scatter(raw_down, "dev", scatter_dimension=0, tiled=True),
        lax.psum_scatter(raw_vectors, "dev", scatter_dimension=1, tiled=True),
    )
    local_squares = (
        jnp.sum(qkv_shard * qkv_shard)
        + jnp.sum(out_shard * out_shard)
        + jnp.sum(up_shard * up_shard)
        + jnp.sum(down_shard * down_shard)
        + jnp.sum(vector_shard * vector_shard)
    )
    grad_norm = jnp.sqrt(lax.psum(local_squares, "dev"))
    factor = clip_limit / jnp.maximum(grad_norm, clip_limit)
    qkv_parts = adam_update(
        qkv_weight, qkv_shard, first_qkv, second_qkv, factor, rate_matrix, decay_matrix
    )
    out_parts = adam_update(
        out_weight, out_shard, first_out, second_out, factor, rate_matrix, decay_matrix
    )
    up_parts = adam_update(
        up_weight, up_shard, first_up, second_up, factor, rate_matrix, decay_matrix
    )
    down_parts = adam_update(
        down_weight, down_shard, first_down, second_down, factor, rate_matrix, decay_matrix
    )
    vector_parts = adam_update(
        vector_rows, vector_shard, first_vectors, second_vectors, factor, rate_vector, 0.0
    )
    return (
        output,
        input_grads,
        grad_norm,
        qkv_parts[0],
        qkv_parts[1],
        qkv_parts[2],
        qkv_parts[3],
        out_parts[0],
        out_parts[1],
        out_parts[2],
        out_parts[3],
        up_parts[0],
        up_parts[1],
        up_parts[2],
        up_parts[3],
        down_parts[0],
        down_parts[1],
        down_parts[2],
        down_parts[3],
        vector_parts[0],
        vector_parts[1],
        vector_parts[2],
        vector_parts[3],
    )


def local_slice(
    images,
    pair_matrix,
    caption_grads,
    qkv_weight,
    out_weight,
    up_weight,
    down_weight,
    vector_rows,
    first_qkv,
    first_out,
    first_up,
    first_down,
    first_vectors,
    second_qkv,
    second_out,
    second_up,
    second_down,
    second_vectors,
):
    weights = (qkv_weight, out_weight, up_weight, down_weight)
    results = forward(images.transpose(1, 0, 2), pair_matrix, caption_grads, weights, vector_rows)
    groups, kept, output, vector_full = results[0:3], results[3:17], results[17], results[18]
    shapes = [w.shape for w in weights]
    qkv_shard, out_shard, up_shard, down_shard, vector_sum, squares, input_grads = backward(
        output.shape, vector_full, groups, (*kept[:8], *kept[9:]), shapes
    )
    masters = (*weights, vector_rows)
    first = (first_qkv, first_out, first_up, first_down, first_vectors)
    second = (second_qkv, second_out, second_up, second_down, second_vectors)
    shards = (qkv_shard, out_shard, up_shard, down_shard)
    output, input_grads, *parts, norm = update(squares, vector_sum, shards, masters, first, second, (output, input_grads))
    return (output.transpose(1, 0, 2), input_grads.transpose(1, 0, 2), norm[0, 0], *parts)


def solution(mesh):
    fits = mesh.shape["dev"] == 32
    return jax.shard_map(
        local_slice if fits else local_wide,
        mesh=mesh,
        in_specs=(
            P("dev", None, None),
            P("dev", None),
            P("dev", None, None),
            P("dev", None),
            P("dev", None),
            P("dev", None),
            P("dev", None),
            P(None, "dev"),
            P("dev", None),
            P("dev", None),
            P("dev", None),
            P("dev", None),
            P(None, "dev"),
            P("dev", None),
            P("dev", None),
            P("dev", None),
            P("dev", None),
            P(None, "dev"),
        ),
        out_specs=(
            P("dev", None, None),
            P("dev", None, None),
            P(),
            P("dev", None),
            P("dev", None),
            P("dev", None),
            P("dev", None),
            P("dev", None),
            P("dev", None),
            P("dev", None),
            P("dev", None),
            P("dev", None),
            P("dev", None),
            P("dev", None),
            P("dev", None),
            P("dev", None),
            P("dev", None),
            P("dev", None),
            P("dev", None),
            P(None, "dev"),
            P(None, "dev"),
            P(None, "dev"),
            P(None, "dev"),
        ),
        check_vma=False,
    )
```
